32 devices in a mesh: dp: 16 (over z, y, x), mp: 2 (over core).
Axes of the slice: x: 2, y: 2, z: 4, core: 2. Of those that a mesh axis runs over, the one named last changes fastest.
Arguments:
- tokens: bfloat16 [32768, 768], P('dp'), may hold values from -6 to 6
- segments: int32 [32768], P('dp'), may hold values from 0 to 31, as said below
- lengths: int32 [32, 32], P('dp'), may hold values from 0 to 1024, as said below
- ln1_gain: bfloat16 [768], replicated, may hold values from 0.25 to 1.75
- ln1_bias: bfloat16 [768], replicated, may hold values from -4 to 4
- w_qkv: bfloat16 [768, 3, 768], P(None, None, 'mp'), may hold values from -0.21875 to 0.21875
- b_qv: bfloat16 [2, 768], P(None, 'mp'), may hold values from -4 to 4
- w_out: bfloat16 [768, 768], P('mp'), may hold values from -0.625 to 0.625
- out_bias: bfloat16 [768], replicated, may hold values from -4 to 4
- ln2_gain: bfloat16 [768], replicated, may hold values from 0.25 to 1.75
- ln2_bias: bfloat16 [768], replicated, may hold values from -4 to 4
- w_fc: bfloat16 [768, 3072], P(None, 'mp'), may hold values from -0.21875 to 0.21875
- b_fc: bfloat16 [3072], P('mp'), may hold values from -4 to 4
- w_proj: bfloat16 [3072, 768], P('mp'), may hold values from -0.109375 to 0.109375
- proj_bias: bfloat16 [768], replicated, may hold values from -4 to 4
- cotangent: bfloat16 [32768, 768], P('dp'), may hold values from -17 to 17
Outputs:
- block_out: bfloat16 [32768, 768], P('dp')
- input_grad: float32 [32768, 768], P('dp')
- grad_ln1_gain: float32 [768], replicated
- grad_ln1_bias: float32 [768], replicated
- grad_w_qkv: float32 [768, 3, 768], P(None, None, 'mp')
- grad_b_qv: float32 [2, 768], P(None, 'mp')
- grad_w_out: float32 [768, 768], P('mp')
- grad_out_bias: float32 [768], replicated
- grad_ln2_gain: float32 [768], replicated
- grad_ln2_bias: float32 [768], replicated
- grad_w_fc: float32 [768, 3072], P(None, 'mp')
- grad_b_fc: float32 [3072], P('mp')
- grad_w_proj: float32 [3072, 768], P('mp')
- grad_proj_bias: float32 [768], replicated
The draws below stay inside these ranges and needn't reach their ends.
Inputs may be any that keep to these rules, and one draw needn't show every extreme that they name: `segments`: within each bin of 1024 rows the document numbers start at 0, never fall and rise by one at each new document; a bin holds 1 to 32 documents; some bin holds 32. lengths[b, s] is the number of rows of bin b whose document number is s, 0 for numbers that the bin does not use; some bin is one document of 1024 rows.
All inputs are finite; a program needn't handle non-finite values.
Results may differ from the reference program's by a relative error of at most 0.009.
Values sent between devices are 32-bit elements; how exact they have to be, the bound alone decides.
A program may use at most 192 MiB of HBM per device.

```python
import jax
import jax.numpy as jnp
from jax import lax

D = 768
HEADS = 12
HEAD_DIM = 64
FF = 3072
BIN = 1024
SEGS = 32
BINS = 32
TOKENS = 32768


def bin_layout(key):
    base_key = jax.random.fold_in(key, 7)
    count_key, score_key, choose_key, order_key = jax.random.split(base_key, 4)
    few_docs = jax.random.randint(count_key, (BINS,), 1, 3)
    many_docs = jax.random.randint(jax.random.fold_in(count_key, 1), (BINS,), max(SEGS // 2, 1), SEGS + 1)
    chooser = jax.random.randint(choose_key, (BINS,), 0, 10)
    doc_counts = jnp.where(chooser < 3, few_docs, many_docs)
    ranking = jax.random.permutation(order_key, BINS)
    doc_counts = jnp.where(ranking == 0, 1, doc_counts)
    doc_counts = jnp.where(ranking == 1, SEGS, doc_counts)
    cut_scores = jax.random.randint(score_key, (BINS, BIN - 1), 0, 1 << 20) * BIN + jnp.arange(BIN - 1, dtype=jnp.int32)[None, :]
    ranked = -jnp.sort(-cut_scores, axis=1)
    cut_index = jnp.clip(doc_counts - 2, 0, BIN - 2)
    threshold = jnp.take_along_axis(ranked, cut_index[:, None], axis=1)
    cuts = (cut_scores >= threshold) & (doc_counts[:, None] >= 2)
    seg_table = jnp.concatenate([jnp.zeros((BINS, 1), jnp.int32), jnp.cumsum(cuts.astype(jnp.int32), axis=1)], axis=1)
    labels = jnp.arange(SEGS, dtype=jnp.int32)
    length_table = jnp.sum((seg_table[:, :, None] == labels[None, None, :]).astype(jnp.int32), axis=1)
    return (seg_table.reshape(BINS * BIN).astype(jnp.int32), length_table.astype(jnp.int32))


def draw_segments(key, part):
    seg_rows, length_table = bin_layout(key)
    return seg_rows


def draw_lengths(key, part):
    seg_rows, length_table = bin_layout(key)
    return length_table


def draw_cotangent(key, part):
    noise_key, row_key = jax.random.split(jax.random.fold_in(key, 11), 2)
    noise = jnp.clip(jax.random.normal(noise_key, (TOKENS, D), jnp.float32), -4.0, 4.0)
    rough = jax.random.uniform(row_key, (TOKENS, 1), jnp.float32, 0.6, 1.4)
    bin_number = (jnp.arange(TOKENS, dtype=jnp.int32) // BIN).astype(jnp.float32)[:, None]
    rising = jnp.exp(jnp.log(3.0) * bin_number / (BINS - 1))
    return (noise * rough * rising).astype(jnp.bfloat16)


def levels(stream_key, shape, pieces, smallest, high):
    level, own = 1.0, jax.random.fold_in(stream_key, 6)
    for position, parts in pieces:
        heights = jnp.exp(jax.random.uniform(jax.random.fold_in(own, position), (parts,), jnp.float32, smallest / len(pieces), high / len(pieces)))
        level = level * jnp.repeat(heights, shape[position] // parts).reshape([-1 if axis == position else 1 for axis in range(len(shape))])
    return level


def centred(key, dims, scale, reach, cuts=(), kind=jnp.bfloat16):
    result = jax.random.normal(key, dims, jnp.float32) * scale
    if len(cuts) > 0:
        result = levels(key, dims, cuts, -0.22, 0.18) * result
    return jnp.clip(result, min=-reach, max=reach).astype(kind)


def setup_inputs(seed: int = 0) -> dict:
    arg_keys = jax.random.split(jax.random.key(seed), 17)
    return {
        "tokens": centred(arg_keys[0], (TOKENS, D), 1.0, 6.0, ((0, 16),)),
        "segments": draw_segments(jax.random.fold_in(arg_keys[16], 71), 0),
        "lengths": draw_lengths(jax.random.fold_in(arg_keys[16], 71), 0),
        "ln1_gain": jnp.clip(1.0 + 0.15 * jax.random.normal(arg_keys[3], (D,), jnp.float32), 0.25, 1.75).astype(jnp.bfloat16),
        "ln1_bias": centred(arg_keys[4], (D,), 0.3, 4.0),
        "w_qkv": centred(arg_keys[5], (D, 3, D), D ** -0.5, 0.21875, ((2, 2),)),
        "b_qv": centred(arg_keys[6], (2, D), 0.3, 4.0, ((1, 2),)),
        "w_out": centred(arg_keys[7], (D, D), (D // 8) ** -0.5, 0.625, ((0, 2),)),
        "out_bias": centred(arg_keys[8], (D,), 0.3, 4.0),
        "ln2_gain": jnp.clip(1.0 + 0.15 * jax.random.normal(arg_keys[9], (D,), jnp.float32), 0.25, 1.75).astype(jnp.bfloat16),
        "ln2_bias": centred(arg_keys[10], (D,), 0.3, 4.0),
        "w_fc": centred(arg_keys[11], (D, FF), D ** -0.5, 0.21875, ((1, 2),)),
        "b_fc": centred(arg_keys[12], (FF,), 0.3, 4.0, ((0, 2),)),
        "w_proj": centred(arg_keys[13], (FF, D), FF ** -0.5, 0.109375, ((0, 2),)),
        "proj_bias": centred(arg_keys[14], (D,), 0.3, 4.0),
        "cotangent": draw_cotangent(jax.random.fold_in(arg_keys[16], 71), 0),
    }


@jax.custom_vjp
def low(v):
    return lax.optimization_barrier(v.astype(jnp.bfloat16)).astype(jnp.float32)

@jax.custom_vjp
def low_back(v):
    return v

def low_keep(v):
    return (low(v), None)

def low_pass(kept, grad):
    return (grad,)

def back_keep(v):
    return (v, None)

def back_low(kept, grad):
    return (low(grad),)
low.defvjp(low_keep, low_pass)
low_back.defvjp(back_keep, back_low)
epsilon = 1e-05
gelu_scale = 0.7978845608028654
gelu_cubic = 0.044715
score_scale = 0.125
masked_score = -1e+30

def product(left, right):
    return jnp.dot(left, right, precision=lax.Precision.HIGHEST, preferred_element_type=jnp.float32)

def layer_norm(values, gain, bias_vec):
    center = values - lax.optimization_barrier(jnp.mean(values, axis=-1, keepdims=True))
    spread = lax.optimization_barrier(jnp.mean(center * center, axis=-1, keepdims=True))
    return center * lax.rsqrt(spread + epsilon) * gain + bias_vec

def gelu_tanh(values):
    return 0.5 * values * (1.0 + jnp.tanh(gelu_scale * (values + gelu_cubic * values * values * values)))

def row_starts(segments, lengths):
    offsets = jnp.cumsum(lengths, axis=1) - lengths
    labels = jnp.arange(SEGS, dtype=jnp.int32)
    chosen = segments.reshape(BINS, BIN)[:, :, None] == labels[None, None, :]
    return lax.optimization_barrier(jnp.sum(jnp.where(chosen, offsets[:, None, :], 0), axis=2)).astype(jnp.int32)

def visible_pairs(seg_bin, start_bin):
    places = jnp.arange(BIN, dtype=jnp.int32)
    causal = places[None, :] <= places[:, None]
    same_doc = seg_bin[None, :] == seg_bin[:, None]
    after_start = places[None, :] >= start_bin[:, None]
    return causal & same_doc & after_start

def attend_bin(operands):
    qkv_bin, seg_bin, start_bin = operands
    queries = qkv_bin[:, 0]
    key_rows = qkv_bin[:, 1]
    value_rows = qkv_bin[:, 2]
    scores = jnp.einsum('qhd,khd->hqk', queries, key_rows, precision=lax.Precision.HIGHEST) * score_scale
    scores = low_back(scores)
    scores = jnp.where(visible_pairs(seg_bin, start_bin)[None], scores, masked_score)
    attn_probs = low(jax.nn.softmax(scores, axis=-1))
    mixed_rows = jnp.einsum('hqk,khd->qhd', attn_probs, value_rows, precision=lax.Precision.HIGHEST)
    return mixed_rows.reshape(BIN, D)

def block_forward(tokens_f, start_rows, seg_rows, params):
    gain_one, bias_one, qkv_weight, qv_bias, out_weight, out_shift, gain_two, bias_two, fc_weight, fc_shift, proj_weight, proj_shift = params
    normed_one = low(layer_norm(tokens_f, gain_one, bias_one))
    joined_qkv = product(normed_one, qkv_weight.reshape(D, 3 * D)).reshape(TOKENS, 3, D)
    bias_rows = jnp.stack([qv_bias[0], jnp.zeros_like(qv_bias[0]), qv_bias[1]])
    joined_qkv = low_back(low(joined_qkv + bias_rows[None]))
    heads_view = joined_qkv.reshape(BINS, BIN, 3, HEADS, HEAD_DIM)
    mixed_rows = lax.map(jax.checkpoint(attend_bin), (heads_view, seg_rows, start_rows))
    mixed_rows = low_back(low(mixed_rows.reshape(TOKENS, D)))
    branch = low_back(product(mixed_rows, out_weight) + out_shift)
    first_sum = tokens_f + branch
    normed_two = low(layer_norm(first_sum, gain_two, bias_two))
    hidden_pre = low_back(product(normed_two, fc_weight) + fc_shift)
    hidden = low(gelu_tanh(hidden_pre))
    return first_sum + product(hidden, proj_weight) + proj_shift

def reference(tokens, segments, lengths, ln1_gain, ln1_bias, w_qkv, b_qv, w_out, out_bias, ln2_gain, ln2_bias, w_fc, b_fc, w_proj, proj_bias, cotangent):
    tables = (ln1_gain, ln1_bias, w_qkv, b_qv, w_out, out_bias, ln2_gain, ln2_bias, w_fc, b_fc, w_proj, proj_bias)
    params = tuple((table.astype(jnp.float32) for table in tables))
    start_rows = row_starts(segments, lengths)
    seg_rows = segments.reshape(BINS, BIN)

    def forward_fn(tokens_f, *weights):
        return block_forward(tokens_f, start_rows, seg_rows, weights)
    output, pullback = jax.vjp(forward_fn, tokens.astype(jnp.float32), *params)
    gradients = pullback(cotangent.astype(jnp.float32))
    return (output.astype(jnp.bfloat16), gradients[0], gradients[1], gradients[2], gradients[3], gradients[4], gradients[5], gradients[6], gradients[7], gradients[8], gradients[9], gradients[10], gradients[11], gradients[12])
```

```python
import functools

import jax
import jax.numpy as jnp
from jax import lax
from jax.experimental import pallas as pl
from jax.experimental.pallas import tpu as pltpu
from jax.sharding import PartitionSpec as P

HEAD_DIM = 64
BIN = 1024
PAIR = 2 * HEAD_DIM
BLOCK = 256
CHUNK = 256
SLOTS = 6
AHEAD = 2
DELAY = 2

epsilon = 1e-05
gelu_scale = 0.7978845608028654
gelu_cubic = 0.044715
score_scale = 0.125
masked_score = -1e30

MESH = pl.DeviceIdType.MESH
F32 = jnp.float32
BF16 = jnp.bfloat16
VMEM_LIMIT = 64_000_000


def dot_nn(left, right):
    return lax.dot_general(left, right, (((1,), (0,)), ((), ())), preferred_element_type=F32)


def dot_nt(left, right):
    return lax.dot_general(left, right, (((1,), (1,)), ((), ())), preferred_element_type=F32)


def dot_tn(left, right):
    return lax.dot_general(left, right, (((0,), (0,)), ((), ())), preferred_element_type=F32)


def norm_parts(values):
    center = values - jnp.mean(values, axis=-1, keepdims=True)
    inverse = lax.rsqrt(jnp.mean(center * center, axis=-1, keepdims=True) + epsilon)
    return center * inverse, inverse


def norm_back(upstream, normal, inverse, gain):
    scaled = upstream * gain
    centered = scaled - jnp.mean(scaled, axis=-1, keepdims=True)
    return inverse * (centered - normal * jnp.mean(scaled * normal, axis=-1, keepdims=True))


def gelu_pair(values):
    square = values * values
    tangent = jnp.tanh(gelu_scale * (values + gelu_cubic * square * values))
    half = 0.5 * (1.0 + tangent)
    slope = half + 0.5 * values * (1.0 - tangent * tangent) * (
        gelu_scale + 3.0 * gelu_cubic * gelu_scale * square
    )
    return values * half, slope


def column_to_row(column):
    rows = column.shape[0]
    return jnp.broadcast_to(column, (rows, 128)).T[0:1]


def head_mask(head, scale):
    lane = lax.broadcasted_iota(jnp.int32, (1, PAIR), 1)
    return jnp.where(lane // HEAD_DIM == head, scale, 0.0).astype(BF16)


def attend_pair(qkv_ref, start_ref, attn_ref, lse_ref):
    lane = lax.broadcasted_iota(jnp.int32, (1, PAIR), 1)
    for block in range(BIN // BLOCK):
        rows = slice(block * BLOCK, (block + 1) * BLOCK)
        seen = (block + 1) * BLOCK
        queries = qkv_ref[0, 0, rows]
        key_rows = qkv_ref[0, 1, 0:seen]
        value_rows = qkv_ref[0, 2, 0:seen]
        j = lax.broadcasted_iota(jnp.int32, (BLOCK, seen), 1)
        i = lax.broadcasted_iota(jnp.int32, (BLOCK, seen), 0) + block * BLOCK
        visible = (j >= start_ref[rows]) & (j <= i)
        mixed = []
        for head in range(2):
            scores = dot_nt(queries * head_mask(head, score_scale), key_rows)
            scores = jnp.where(visible, scores, masked_score)
            highest = jnp.max(scores, axis=-1, keepdims=True)
            weights = jnp.exp(scores - highest)
            totals = jnp.sum(weights, axis=-1, keepdims=True)
            mixed.append(dot_nn(weights.astype(BF16), value_rows) / totals)
            lse_ref[0, head : head + 1, rows] = column_to_row(highest + jnp.log(totals))
        attn_ref[0, rows] = jnp.where(lane < HEAD_DIM, mixed[0], mixed[1]).astype(BF16)


def project_and_attend(h1, w_ref, bias_ref, start_ref, qkv_ref, attn_ref, lse_ref):
    for c in range(3):
        out = dot_nn(h1, w_ref[c].astype(BF16)) + bias_ref[c : c + 1]
        qkv_ref[0, c] = out.astype(BF16)
    attend_pair(qkv_ref, start_ref, attn_ref, lse_ref)


def own_front_kernel(
    mp_ref, x_ref, seg_ref, len_ref, gain_ref, shift_ref, w_ref, bias_ref,
    qkv_ref, attn_ref, lse_ref, h1_ref, start_ref, row_ref,
):
    @pl.when(pl.program_id(0) == 0)
    def _():
        gain = gain_ref[...].astype(F32)
        shift = shift_ref[...].astype(F32)
        for block in range(BIN // BLOCK):
            rows = slice(block * BLOCK, (block + 1) * BLOCK)
            normal, _ = norm_parts(x_ref[rows].astype(F32))
            h1_ref[rows] = (normal * gain + shift).astype(BF16)
        mine = mp_ref[0]
        count = len_ref.shape[1]
        seg = seg_ref[pl.ds(mine, 1), :].astype(F32)
        seg = jnp.broadcast_to(seg, (128, BIN)).T
        seg = seg[:, :count]
        label = lax.broadcasted_iota(jnp.int32, (BIN, count), 1).astype(F32)
        sizes = len_ref[pl.ds(mine, 1), :].astype(F32)
        start = jnp.sum(jnp.where(label < seg, sizes, 0.0), axis=1, keepdims=True)
        rows_of = jnp.sum(jnp.where(label == seg, 1.0, 0.0), axis=0, keepdims=True)
        first = jnp.sum(jnp.where(label < seg, rows_of, 0.0), axis=1, keepdims=True)
        start = jnp.maximum(start, first)
        start_ref[...] = start.astype(jnp.int32)
        row_ref[...] = column_to_row(start).astype(jnp.int32)

    project_and_attend(h1_ref[...], w_ref, bias_ref, start_ref, qkv_ref, attn_ref, lse_ref)


def other_front_kernel(h1_ref, start_ref, w_ref, bias_ref, qkv_ref, attn_ref, lse_ref):
    project_and_attend(h1_ref[...], w_ref, bias_ref, start_ref, qkv_ref, attn_ref, lse_ref)


def fixed(shape):
    return pl.BlockSpec(shape, lambda *_: (0,) * len(shape), pipeline_mode=pl.Buffered(1))


def front(mine, x, seg, lens, gain, shift, w_own, bias_own, width):
    model = x.shape[1]
    pairs = width // PAIR
    per_pair = [
        pl.BlockSpec((3, model, PAIR), lambda p, *_: (0, 0, p)),
        pl.BlockSpec((3, PAIR), lambda p, *_: (0, p)),
    ]
    outs = [
        pl.BlockSpec((1, 3, BIN, PAIR), lambda p, *_: (p, 0, 0, 0)),
        pl.BlockSpec((1, BIN, PAIR), lambda p, *_: (p, 0, 0)),
        pl.BlockSpec((1, 8, BIN), lambda p, *_: (p, 0, 0)),
    ]
    out_shapes = [
        jax.ShapeDtypeStruct((pairs, 3, BIN, PAIR), BF16),
        jax.ShapeDtypeStruct((pairs, BIN, PAIR), BF16),
        jax.ShapeDtypeStruct((pairs, 8, BIN), F32),
    ]
    cost = pl.CostEstimate(flops=6_000_000_000, bytes_accessed=10_000_000, transcendentals=0)
    params = pltpu.CompilerParams(vmem_limit_bytes=VMEM_LIMIT)
    own = pl.pallas_call(
        own_front_kernel,
        out_shape=out_shapes
        + [
            jax.ShapeDtypeStruct((BIN, model), BF16),
            jax.ShapeDtypeStruct((BIN, 1), jnp.int32),
            jax.ShapeDtypeStruct((1, BIN), jnp.int32),
        ],
        grid_spec=pltpu.PrefetchScalarGridSpec(
            num_scalar_prefetch=1,
            grid=(pairs,),
            in_specs=[
                pl.BlockSpec((BIN, model), lambda p, m: (m[0], 0)),
                fixed(seg.shape), fixed(lens.shape), fixed((1, model)), fixed((1, model)),
            ]
            + per_pair,
            out_specs=outs
            + [
                pl.BlockSpec((BIN, model), lambda p, *_: (0, 0)),
                pl.BlockSpec((BIN, 1), lambda p, *_: (0, 0)),
                pl.BlockSpec((1, BIN), lambda p, *_: (0, 0)),
            ],
        ),
        compiler_params=params,
        cost_estimate=cost,
        name="own_front",
    )

    def other(h1, start, w_other, bias_other):
        return pl.pallas_call(
            other_front_kernel,
            out_shape=out_shapes,
            grid=(pairs,),
            in_specs=[fixed((BIN, model)), fixed((BIN, 1))] + per_pair,
            out_specs=outs,
            compiler_params=params,
            cost_estimate=cost,
            name="other_front",
        )(h1, start, w_other, bias_other)

    return own(mine, x, seg, lens, gain, shift, w_own, bias_own), other


def middle_kernel(
    mp_ref, x_ref, cot_ref, attn_own_ref, attn_other_ref, vec_in_ref, bfc_ref,
    wo_own_ref, wo_f_ref, wf_own_ref, wf_f_ref, wp_own_ref, wp_f_ref,
    g_ref, df_ref, h2_ref, da_ref, dattn_ref, dr1_ref, sum_ref, vec_ref,
    wo_other_ref, wf_other_ref, wp_other_ref,
):
    @pl.when(pl.program_id(0) == 0)
    def _():
        wo_other_ref[...] = wo_f_ref[...].astype(BF16)
        wf_other_ref[...] = wf_f_ref[...].astype(BF16)
        wp_other_ref[...] = wp_f_ref[...].astype(BF16)
        vec_ref[...] = jnp.zeros_like(vec_ref)

    pairs = attn_own_ref.shape[0]
    model = x_ref.shape[1]
    hidden = wf_own_ref.shape[1]
    out_bias = vec_in_ref[0:1]
    gain = vec_in_ref[1:2]
    shift = vec_in_ref[2:3]
    x = x_ref[...].astype(F32)
    cot = cot_ref[...]
    upstream = cot.astype(F32)
    mixed_own = jnp.concatenate([attn_own_ref[p] for p in range(pairs)], axis=1)
    mixed_other = jnp.concatenate([attn_other_ref[p] for p in range(pairs)], axis=1)
    branch = dot_nn(mixed_own, wo_own_ref[...]) + dot_nn(mixed_other, wo_other_ref[...])
    first = x + (branch + out_bias)
    normal, inverse = norm_parts(first)
    h2 = (normal * gain + shift).astype(BF16)
    h2_ref[...] = h2
    total = first
    dh2 = jnp.zeros_like(first)
    for half in range(2):
        wf = (wf_own_ref, wf_other_ref)[half]
        wp = (wp_own_ref, wp_other_ref)[half]
        pre = dot_nn(h2, wf[...]) + bfc_ref[half : half + 1]
        act, slope = gelu_pair(pre)
        act = act.astype(BF16)
        g_ref[half] = act
        total = total + dot_nn(act, wp[...])
        df = (dot_nt(cot, wp[...]) * slope).astype(BF16)
        df_ref[half] = df
        dh2 = dh2 + dot_nt(df, wf[...])
        df_sum = jnp.sum(df.astype(F32), axis=0, keepdims=True)
        for piece in range(hidden // model):
            cols = slice(piece * model, (piece + 1) * model)
            row = slice(6 + piece, 7 + piece)
            vec_ref[half, row] = vec_ref[half, row] + df_sum[:, cols]
    sum_ref[...] = total
    dr1 = upstream + norm_back(dh2, normal, inverse, gain)
    dr1_ref[...] = dr1
    da = dr1.astype(BF16)
    da_ref[...] = da
    for half in range(2):
        wo = (wo_own_ref, wo_other_ref)[half]
        dattn = dot_nt(da, wo[...]).astype(BF16)
        for p in range(pairs):
            dattn_ref[half * pairs + p] = dattn[:, p * PAIR : (p + 1) * PAIR]
    sums = [
        jnp.sum(da.astype(F32), axis=0, keepdims=True),
        jnp.sum(dh2 * normal, axis=0, keepdims=True),
        jnp.sum(dh2, axis=0, keepdims=True),
        jnp.sum(upstream, axis=0, keepdims=True),
    ]
    for half in range(2):
        for n, item in enumerate(sums):
            row = slice(2 + n, 3 + n)
            vec_ref[half, row] = vec_ref[half, row] + item


def middle(mine, x, cot, attn_own, attn_other, vec_in, bfc, weights):
    model = x.shape[1]
    pairs = attn_own.shape[0]
    hidden = bfc.shape[1]
    steps = BIN // BLOCK
    rows = lambda i, m: (i, 0)
    mine_rows = lambda i, m: (m[0] * steps + i, 0)
    return pl.pallas_call(
        middle_kernel,
        out_shape=[
            jax.ShapeDtypeStruct((2, BIN, hidden), BF16),
            jax.ShapeDtypeStruct((2, BIN, hidden), BF16),
            jax.ShapeDtypeStruct((BIN, model), BF16),
            jax.ShapeDtypeStruct((BIN, model), BF16),
            jax.ShapeDtypeStruct((2 * pairs, BIN, PAIR), BF16),
            jax.ShapeDtypeStruct((BIN, model), F32),
            jax.ShapeDtypeStruct((BIN, model), F32),
            jax.ShapeDtypeStruct((2, 16, model), F32),
        ],
        grid_spec=pltpu.PrefetchScalarGridSpec(
            num_scalar_prefetch=1,
            grid=(steps,),
            in_specs=[
                pl.BlockSpec((BLOCK, model), mine_rows),
                pl.BlockSpec((BLOCK, model), mine_rows),
                pl.BlockSpec((pairs, BLOCK, PAIR), lambda i, m: (0, i, 0)),
                pl.BlockSpec((pairs, BLOCK, PAIR), lambda i, m: (0, i, 0)),
                fixed(vec_in.shape), fixed(bfc.shape),
            ]
            + [fixed(w.shape) for w in weights],
            out_specs=[
                pl.BlockSpec((2, BLOCK, hidden), lambda i, m: (0, i, 0)),
                pl.BlockSpec((2, BLOCK, hidden), lambda i, m: (0, i, 0)),
                pl.BlockSpec((BLOCK, model), rows),
                pl.BlockSpec((BLOCK, model), rows),
                pl.BlockSpec((2 * pairs, BLOCK, PAIR), lambda i, m: (0, i, 0)),
                pl.BlockSpec((BLOCK, model), rows),
                pl.BlockSpec((BLOCK, model), rows),
                pl.BlockSpec((2, 16, model), lambda i, m: (0, 0, 0)),
            ],
            scratch_shapes=[pltpu.VMEM(w.shape, BF16) for w in weights[1::2]],
        ),
        compiler_params=pltpu.CompilerParams(vmem_limit_bytes=VMEM_LIMIT),
        cost_estimate=pl.CostEstimate(
            flops=22_000_000_000, bytes_accessed=40_000_000, transcendentals=0
        ),
        name="middle",
    )(mine, x, cot, attn_own, attn_other, vec_in, bfc, *weights)


def proj_grad_kernel(mp_ref, left_ref, right_ref, out_ref):
    out_ref[0] = dot_tn(left_ref[0], right_ref[...])


def proj_grad(mine, g, cot):
    hidden = g.shape[2]
    model = cot.shape[1]
    width = 512
    return pl.pallas_call(
        proj_grad_kernel,
        out_shape=jax.ShapeDtypeStruct((2, hidden, model), F32),
        grid_spec=pltpu.PrefetchScalarGridSpec(
            num_scalar_prefetch=1,
            grid=(2, hidden // width),
            in_specs=[
                pl.BlockSpec((1, BIN, width), lambda h, n, m: (h, 0, n)),
                pl.BlockSpec((BIN, model), lambda h, n, m: (m[0], 0)),
            ],
            out_specs=pl.BlockSpec((1, width, model), lambda h, n, m: (h, n, 0)),
        ),
        compiler_params=pltpu.CompilerParams(vmem_limit_bytes=VMEM_LIMIT),
        name="proj_grad",
    )(mine, g, cot)


def fc_grad_kernel(left_ref, right_ref, out_ref):
    out_ref[0] = dot_tn(left_ref[...], right_ref[0])


def fc_grad(h2, df):
    hidden = df.shape[2]
    model = h2.shape[1]
    return pl.pallas_call(
        fc_grad_kernel,
        out_shape=jax.ShapeDtypeStruct((2, hidden, model), F32),
        grid=(2, hidden // model),
        in_specs=[
            fixed((BIN, model)),
            pl.BlockSpec((1, BIN, model), lambda h, n: (h, 0, n)),
        ],
        out_specs=pl.BlockSpec((1, model, model), lambda h, n: (h, n, 0)),
        compiler_params=pltpu.CompilerParams(vmem_limit_bytes=VMEM_LIMIT),
        name="fc_grad",
    )(h2, df)


def halving_plan(order, rows):
    first, back = [], []
    size = rows
    for n, bit in enumerate(order):
        if n < len(order) - 1 and size % 16 == 0:
            size //= 2
            first.append((bit, size, 0))
            back.append((bit, size, 2))
        else:
            first.append((bit, size, 1))
    return first + back[::-1]


def color_plans(bits):
    orders = [list(range(bits)), list(range(bits))]
    if bits > 1:
        orders[1][:2] = [1, 0]
    return [halving_plan(order, CHUNK // 2) for order in orders]


def attend_back_pair(pair, qkv, dattn, lse_ref, row_ref, dk, dv, vec, pairs):
    dk[...] = jnp.zeros_like(dk)
    dv[...] = jnp.zeros_like(dv)
    half = pair // pairs
    place = pair - half * pairs
    dq_sum = jnp.zeros((1, PAIR), F32)
    for block in range(BIN // BLOCK):
        rows = slice(block * BLOCK, (block + 1) * BLOCK)
        seen = (block + 1) * BLOCK
        queries = qkv[pair, 0, rows]
        upstream = dattn[pair, rows]
        key_rows = qkv[pair, 1, 0:seen]
        value_rows = qkv[pair, 2, 0:seen]
        j = lax.broadcasted_iota(jnp.int32, (seen, BLOCK), 0)
        i = lax.broadcasted_iota(jnp.int32, (seen, BLOCK), 1) + block * BLOCK
        visible = (j >= row_ref[0:1, rows]) & (j <= i)
        dq = jnp.zeros((BLOCK, PAIR), F32)
        for head in range(2):
            masked_q = queries * head_mask(head, score_scale)
            masked_up = upstream * head_mask(head, 1.0)
            scores = dot_nt(key_rows, masked_q)
            probs = jnp.exp(scores - lse_ref[pair, head : head + 1, rows])
            probs = jnp.where(visible, probs, 0.0)
            dprobs = dot_nt(value_rows, masked_up)
            inner = jnp.sum(probs * dprobs, axis=0, keepdims=True)
            dscores = (probs * (dprobs - inner)).astype(BF16)
            dv[0:seen] = dv[0:seen] + dot_nn(probs.astype(BF16), masked_up)
            dk[0:seen] = dk[0:seen] + dot_nn(dscores, masked_q)
            dq = dq + dot_tn(dscores, key_rows * head_mask(head, 1.0))
        dq = (dq * score_scale).astype(BF16)
        qkv[pair, 0, rows] = dq
        dq_sum = dq_sum + jnp.sum(dq.astype(F32), axis=0, keepdims=True)
    dv_low = dv[...].astype(BF16)
    qkv[pair, 1] = dk[...].astype(BF16)
    qkv[pair, 2] = dv_low
    dv_sum = jnp.sum(dv_low.astype(F32), axis=0, keepdims=True)
    width = pairs * PAIR
    vec[half, 8:9, pl.ds(pl.multiple_of(place * PAIR, PAIR), PAIR)] = dq_sum
    vec[half, 8:9, pl.ds(pl.multiple_of(width + place * PAIR, PAIR), PAIR)] = dv_sum


def back_kernel(
    bits, groups,
    gp_ref, gf_ref, qkv_own_ref, qkv_other_ref, dattn_ref, attn_own_ref, attn_other_ref,
    da_ref, h1_ref, w_own_ref, w_other_ref, x_ref, dr1_ref, lse_own_ref, lse_other_ref,
    row_ref, gain_ref, vec_in_ref,
    op_ref, of_ref, oa_ref, ig_ref, vo_ref,
    acc, other, mpbuf, rbufs, qkv, dattn, attn, da, h1, w, x, dh1, ig, lse, dk, dv, vec, vrecv,
    ssem, rsem, mps, mpr, osem, wsem, lsem, igsem, vsem,
):
    dp = lax.axis_index("dp")
    mp = lax.axis_index("mp")
    chunks = 3 * groups
    half_rows = CHUNK // 2
    own_bits = [(dp // (1 << b)) % 2 for b in range(bits)]
    partner = [dp + (1 - 2 * own_bits[b]) * (1 << b) for b in range(bits)]
    plans = color_plans(bits)
    stages = len(plans[0])
    pairs = qkv_own_ref.shape[0]
    model = x_ref.shape[1]
    width = pairs * PAIR

    barrier = pltpu.get_barrier_semaphore()
    for b in range(bits):
        pl.semaphore_signal(barrier, inc=1, device_id=(partner[b], mp), device_id_type=MESH)
    pl.semaphore_signal(barrier, inc=1, device_id=(dp, 1 - mp), device_id_type=MESH)
    pl.semaphore_wait(barrier, bits + 1)

    my_rows = pl.ds(pl.multiple_of(mp * BIN, BIN), BIN)
    loads = []

    def load(src, dst):
        loads.append(pltpu.make_async_copy(src, dst, lsem.at[len(loads)]))

    load(qkv_own_ref, qkv.at[0:pairs])
    load(qkv_other_ref, qkv.at[pairs : 2 * pairs])
    load(dattn_ref, dattn)
    load(lse_own_ref, lse.at[0:pairs])
    load(lse_other_ref, lse.at[pairs : 2 * pairs])
    load(vec_in_ref, vec)
    early = len(loads)
    load(attn_own_ref, attn.at[0:pairs])
    load(attn_other_ref, attn.at[pairs : 2 * pairs])
    load(da_ref, da)
    load(h1_ref, h1)
    load(w_own_ref, w.at[0])
    load(w_other_ref, w.at[1])
    load(x_ref.at[my_rows], x)
    load(dr1_ref, ig)

    starts = []
    for color in range(2):
        base = color * half_rows
        found = []
        for bit, size, kind in plans[color]:
            found.append(base)
            if kind == 0:
                base = base + own_bits[bit] * size
            if kind == 2:
                base = base - own_bits[bit] * size
        starts.append(found)

    def copy(c, color, s):
        bit, size, kind = plans[color][s]
        slot = c % SLOTS
        base = starts[color][s]
        if kind == 0:
            base = base + (1 - own_bits[bit]) * size
        src = acc.at[c, pl.ds(pl.multiple_of(base, 8), size)]
        dst = src if kind == 2 else rbufs[color][s].at[slot]
        return pltpu.make_async_remote_copy(
            src, dst, ssem.at[slot, color, s], rsem.at[slot, color, s],
            device_id=(partner[bit], mp), device_id_type=MESH,
        )

    def finish(c, color, s):
        bit, size, kind = plans[color][s]
        copy(c, color, s).wait()
        base = starts[color][s]
        if kind == 2:
            return
        if kind == 0:
            base = base + own_bits[bit] * size
        rows = pl.ds(pl.multiple_of(base, 8), size)
        acc[c, rows] = acc[c, rows] + rbufs[color][s][c % SLOTS]

    def mp_copy(src, c):
        slot = c % SLOTS
        return pltpu.make_async_remote_copy(
            src, mpbuf.at[slot], mps.at[slot], mpr.at[slot],
            device_id=(dp, 1 - mp), device_id_type=MESH,
        )

    def own_copy(src, c):
        return pltpu.make_async_copy(src, acc.at[c], osem.at[c % SLOTS])

    def chunk_rows(c):
        return pl.ds(pl.multiple_of(c * CHUNK, CHUNK), CHUNK)

    def begin(c):
        @pl.when(c < groups)
        def _():
            mp_copy(gp_ref.at[1, chunk_rows(c)], c).start()
            own_copy(gp_ref.at[0, chunk_rows(c)], c).start()

        @pl.when((c >= groups) & (c < 2 * groups))
        def _():
            mp_copy(gf_ref.at[1, chunk_rows(c - groups)], c).start()
            own_copy(gf_ref.at[0, chunk_rows(c - groups)], c).start()

        @pl.when((c >= 2 * groups) & (c < chunks))
        def _():
            mp_copy(other.at[c - 2 * groups], c).start()

    def out_copy(dst, c):
        return pltpu.make_async_copy(acc.at[c], dst, wsem.at[c % SLOTS])

    def write(c):
        @pl.when(c < groups)
        def _():
            out_copy(op_ref.at[chunk_rows(c)], c).start()

        @pl.when((c >= groups) & (c < 2 * groups))
        def _():
            n = c - groups
            per = model // CHUNK
            cols = pl.ds(pl.multiple_of((n // per) * model, 128), model)
            out_copy(of_ref.at[chunk_rows(n % per), cols], c).start()

        @pl.when(c >= 2 * groups)
        def _():
            out_copy(oa_ref.at[chunk_rows(c - 2 * groups)], c).start()

    def ring_tick(t):
        @pl.when(t < chunks)
        def _():
            mp_copy(other.at[0], t).wait()

            @pl.when(t < 2 * groups)
            def _():
                own_copy(gp_ref.at[0, chunk_rows(0)], t).wait()

            acc[t] = acc[t] + mpbuf[t % SLOTS]

        for s in range(stages):
            c = t - (DELAY + s)

            @pl.when((c >= 0) & (c < chunks))
            def _():
                for color in range(2):
                    finish(c, color, s)

        for s in range(stages)[::-1]:
            c = t - (DELAY + s)

            @pl.when((c >= 0) & (c < chunks))
            def _():
                if s + 1 == stages:
                    write(c)
                else:
                    for color in range(2):
                        copy(c, color, s + 1).start()

        @pl.when(t < chunks)
        def _():
            for color in range(2):
                copy(t, color, 0).start()

        @pl.when(t + AHEAD < chunks)
        def _():
            begin(t + AHEAD)

        c = t - (DELAY + stages)

        @pl.when(c >= 0)
        def _():
            out_copy(op_ref.at[chunk_rows(0)], c).wait()

    def put_grad(half, row, value):
        rows = value.shape[0]
        for piece in range(rows // 128):
            at = row + piece * 128
            block = value[piece * 128 : (piece + 1) * 128]
            dst = (at // CHUNK, slice(at % CHUNK, at % CHUNK + 128))
            if half == 0:
                acc[2 * groups + dst[0], dst[1]] = block
            else:
                other[dst[0], dst[1]] = block

    def side(half, c):
        return jnp.concatenate([qkv[half * pairs + p, c] for p in range(pairs)], axis=1)

    def out_grad(half):
        mixed = jnp.concatenate([attn[half * pairs + p] for p in range(pairs)], axis=1)
        put_grad(half, 0, dot_tn(mixed, da[...]))

    def qkv_grad(half, c):
        low = side(half, c)
        grad = dot_tn(h1[...], low)
        split = model // 2
        put_grad(half, width * (c + 1), jnp.concatenate([grad[:split], grad[split:]], axis=1))
        part = dot_nt(low, w[half, c].astype(BF16))
        if half == 0 and c == 0:
            dh1[...] = part
        else:
            dh1[...] = dh1[...] + part

    def input_grad():
        gain = gain_ref[...].astype(F32)
        gain_sum = jnp.zeros((1, model), F32)
        shift_sum = jnp.zeros((1, model), F32)
        for block in range(BIN // BLOCK):
            rows = slice(block * BLOCK, (block + 1) * BLOCK)
            normal, inverse = norm_parts(x[rows].astype(F32))
            up = dh1[rows]
            gain_sum = gain_sum + jnp.sum(up * normal, axis=0, keepdims=True)
            shift_sum = shift_sum + jnp.sum(up, axis=0, keepdims=True)
            ig[rows] = ig[rows] + norm_back(up, normal, inverse, gain)
        for half in range(2):
            vec[half, 0:1] = gain_sum
            vec[half, 1:2] = shift_sum

    def ig_copies():
        local = pltpu.make_async_copy(ig, ig_ref.at[my_rows], igsem.at[0])
        remote = pltpu.make_async_remote_copy(
            ig, ig_ref.at[my_rows], igsem.at[1], igsem.at[2],
            device_id=(dp, 1 - mp), device_id_type=MESH,
        )
        return local, remote

    def vec_copy(n):
        if n == 0:
            src, device = vec.at[1], (dp, 1 - mp)
        else:
            src, device = vec.at[0], (partner[n - 1], mp)
        return pltpu.make_async_remote_copy(
            src, vrecv.at[n], vsem.at[0, n], vsem.at[1, n], device_id=device, device_id_type=MESH
        )

    for item in loads:
        item.start()
    for c in range(AHEAD):
        begin(c)
    for item in loads[:early]:
        item.wait()

    attend_ticks = 2 * pairs
    grad_tick = attend_ticks
    input_tick = grad_tick + 3
    ticks = chunks + DELAY + stages

    def tick(t, carry):
        ring_tick(t)

        @pl.when(t < attend_ticks)
        def _():
            attend_back_pair(t, qkv, dattn, lse, row_ref, dk, dv, vec, pairs)

        for c in range(3):
            @pl.when(t == grad_tick + c)
            def _():
                if c == 0:
                    for item in loads[early:]:
                        item.wait()
                    out_grad(0)
                    out_grad(1)
                qkv_grad(0, c)
                qkv_grad(1, c)

        @pl.when(t == input_tick)
        def _():
            input_grad()
            for item in ig_copies():
                item.start()
            vec_copy(0).start()

        for n in range(bits + 1):
            @pl.when(t == input_tick + 1 + n)
            def _():
                vec_copy(n).wait()
                vec[0] = vec[0] + vrecv[n]
                if n < bits:
                    vec_copy(n + 1).start()

        return carry

    lax.fori_loop(0, ticks, tick, 0)
    for item in ig_copies():
        item.wait()
    vo_ref[...] = vec[0]


def back(bits, proj, fc, arrays, row, gain, vec, sizes):
    pairs, hidden, model = sizes
    width = pairs * PAIR
    groups = hidden // CHUNK
    chunks = 3 * groups
    plans = color_plans(bits)
    stages = len(plans[0])
    recv = [
        [pltpu.VMEM((SLOTS, size, model), F32) for _, size, kind in plan if kind < 2]
        for plan in plans
    ]
    here = pl.BlockSpec(memory_space=pl.ANY)
    vmem = pl.BlockSpec(memory_space=pltpu.VMEM)
    dma = pltpu.SemaphoreType.DMA
    return pl.pallas_call(
        functools.partial(back_kernel, bits, groups),
        out_shape=[
            jax.ShapeDtypeStruct((hidden, model), F32),
            jax.ShapeDtypeStruct((model, hidden), F32),
            jax.ShapeDtypeStruct((4 * width, model), F32),
            jax.ShapeDtypeStruct((2 * BIN, model), F32),
            jax.ShapeDtypeStruct((16, model), F32),
        ],
        in_specs=[here] * (2 + len(arrays)) + [vmem, vmem, here],
        out_specs=[here] * 4 + [vmem],
        scratch_shapes=[
            pltpu.VMEM((chunks, CHUNK, model), F32),
            pltpu.VMEM((groups, CHUNK, model), F32),
            pltpu.VMEM((SLOTS, CHUNK, model), F32),
            recv,
            pltpu.VMEM((2 * pairs, 3, BIN, PAIR), BF16),
            pltpu.VMEM((2 * pairs, BIN, PAIR), BF16),
            pltpu.VMEM((2 * pairs, BIN, PAIR), BF16),
            pltpu.VMEM((BIN, model), BF16),
            pltpu.VMEM((BIN, model), BF16),
            pltpu.VMEM((2, 3, model, width), F32),
            pltpu.VMEM((BIN, model), BF16),
            pltpu.VMEM((BIN, model), F32),
            pltpu.VMEM((BIN, model), F32),
            pltpu.VMEM((2 * pairs, 8, BIN), F32),
            pltpu.VMEM((BIN, PAIR), F32),
            pltpu.VMEM((BIN, PAIR), F32),
            pltpu.VMEM((2, 16, model), F32),
            pltpu.VMEM((bits + 1, 16, model), F32),
            dma((SLOTS, 2, stages)),
            dma((SLOTS, 2, stages)),
            dma((SLOTS,)),
            dma((SLOTS,)),
            dma((SLOTS,)),
            dma((SLOTS,)),
            dma((14,)),
            dma((3,)),
            dma((2, bits + 1)),
        ],
        compiler_params=pltpu.CompilerParams(
            collective_id=0, has_side_effects=True, vmem_limit_bytes=67_000_000
        ),
        name="back",
    )(proj, fc, *arrays, row, gain, vec)


def on_device(
    tokens, segments, lengths, ln1_gain, ln1_bias, w_qkv, b_qv, w_out, out_bias,
    ln2_gain, ln2_bias, w_fc, b_fc, w_proj, proj_bias, cotangent,
):
    model = tokens.shape[1]
    width = w_qkv.shape[2]
    hidden = w_fc.shape[1]
    pairs = width // PAIR
    groups = lax.axis_size("dp")
    bits = groups.bit_length() - 1
    if lax.axis_size("mp") != 2 or groups != 1 << bits or tokens.shape[0] != 2 * BIN:
        raise ValueError("unsupported mesh")
    side = lax.axis_index("mp")
    mine = side.astype(jnp.int32).reshape(1)
    swap = [(0, 1), (1, 0)]

    def cross(value):
        return lax.ppermute(value, "mp", swap)

    w3 = jnp.transpose(w_qkv, (1, 0, 2)).astype(F32)
    small = jnp.concatenate([b_qv.reshape(-1), b_fc]).astype(F32)
    small_other = cross(small)
    w3_other = cross(w3)
    wo_other = cross(w_out.astype(F32))
    wf_other = cross(w_fc.astype(F32))
    wp_other = cross(w_proj.astype(F32))

    def qkv_bias(flat):
        return jnp.stack([flat[:width], jnp.zeros((width,), F32), flat[width : 2 * width]])

    own, other_front = front(
        mine, tokens, segments.reshape(2, BIN), lengths,
        ln1_gain.reshape(1, -1), ln1_bias.reshape(1, -1), w3, qkv_bias(small), width,
    )
    qkv_own, attn_own, lse_own, h1, start, row = own
    qkv_other, attn_other, lse_other = other_front(h1, start, w3_other, qkv_bias(small_other))
    vec_in = jnp.stack([out_bias, ln2_gain, ln2_bias, proj_bias]).astype(F32)
    bfc = jnp.stack([small[2 * width :], small_other[2 * width :]])
    g, df, h2, da, dattn, dr1, block_sum, vec = middle(
        mine, tokens, cotangent, attn_own, attn_other, vec_in, bfc,
        (w_out, wo_other, w_fc, wf_other, w_proj, wp_other),
    )
    sum_other = cross(block_sum)
    proj = proj_grad(mine, g, cotangent)
    fc = fc_grad(h2, df)
    arrays = (
        qkv_own, qkv_other, dattn, attn_own, attn_other, da, h1, w3, w3_other, tokens, dr1,
        lse_own, lse_other,
    )
    grad_proj, grad_fc, grad_attn, input_grad, rows = back(
        bits, proj, fc, arrays, row, ln1_gain.reshape(1, -1), vec, (pairs, hidden, model)
    )
    first = jnp.where(side == 0, block_sum, sum_other)
    second = jnp.where(side == 0, sum_other, block_sum)
    block_out = (jnp.concatenate([first, second]) + vec_in[3]).astype(BF16)
    grad_out = grad_attn[:width]
    grad_qkv = grad_attn[width:].reshape(3, width, 2, width)
    grad_qkv = jnp.transpose(grad_qkv, (2, 1, 0, 3)).reshape(model, 3, width)
    return (
        block_out,
        input_grad,
        rows[0],
        rows[1],
        grad_qkv,
        rows[8].reshape(2, width),
        grad_out,
        rows[2],
        rows[3],
        rows[4],
        grad_fc,
        rows[6:8].reshape(-1),
        grad_proj,
        rows[5],
    )


def solution(mesh):
    rows = P("dp", None)
    placed = (
        rows, P("dp"), rows, P(), P(), P(None, None, "mp"), P(None, "mp"), P("mp", None), P(),
        P(), P(), P(None, "mp"), P("mp"), P("mp", None), P(), rows,
    )
    results = (
        rows, rows, P(), P(), P(None, None, "mp"), P(None, "mp"), P("mp", None), P(), P(), P(),
        P(None, "mp"), P("mp"), P("mp", None), P(),
    )
    return jax.shard_map(
        on_device, mesh=mesh, in_specs=placed, out_specs=results, check_vma=False
    )
```

```python
import functools

import jax
import jax.numpy as jnp
from jax import lax
from jax.experimental import pallas as pl
from jax.experimental.pallas import tpu as pltpu
from jax.sharding import PartitionSpec as P

HEAD_DIM = 64
BIN = 1024
PAIR = 2 * HEAD_DIM
BLOCK = 256
CHUNK = 256
SLOTS = 4
SENDS = 4
LANDS = 5
DELAY = 2

epsilon = 1e-05
gelu_scale = 0.7978845608028654
gelu_cubic = 0.044715
score_scale = 0.125
masked_score = -1e30

MESH = pl.DeviceIdType.MESH
F32 = jnp.float32
BF16 = jnp.bfloat16
VMEM_LIMIT = 64_000_000


def dot_nn(left, right):
    return lax.dot_general(left, right, (((1,), (0,)), ((), ())), preferred_element_type=F32)


def dot_nt(left, right):
    return lax.dot_general(left, right, (((1,), (1,)), ((), ())), preferred_element_type=F32)


def dot_tn(left, right):
    return lax.dot_general(left, right, (((0,), (0,)), ((), ())), preferred_element_type=F32)


def norm_parts(values):
    center = values - jnp.mean(values, axis=-1, keepdims=True)
    inverse = lax.rsqrt(jnp.mean(center * center, axis=-1, keepdims=True) + epsilon)
    return center * inverse, inverse


def norm_back(upstream, normal, inverse, gain):
    scaled = upstream * gain
    centered = scaled - jnp.mean(scaled, axis=-1, keepdims=True)
    return inverse * (centered - normal * jnp.mean(scaled * normal, axis=-1, keepdims=True))


def gelu_pair(values):
    square = values * values
    tangent = jnp.tanh(gelu_scale * (values + gelu_cubic * square * values))
    half = 0.5 * (1.0 + tangent)
    slope = half + 0.5 * values * (1.0 - tangent * tangent) * (
        gelu_scale + 3.0 * gelu_cubic * gelu_scale * square
    )
    return values * half, slope


def column_to_row(column):
    rows = column.shape[0]
    return jnp.broadcast_to(column, (rows, 128)).T[0:1]


def head_mask(head, scale):
    lane = lax.broadcasted_iota(jnp.int32, (1, PAIR), 1)
    return jnp.where(lane // HEAD_DIM == head, scale, 0.0).astype(BF16)


def attend_pair(qkv_ref, start_ref, attn_ref, lse_ref):
    lane = lax.broadcasted_iota(jnp.int32, (1, PAIR), 1)
    for block in range(BIN // BLOCK):
        rows = slice(block * BLOCK, (block + 1) * BLOCK)
        seen = (block + 1) * BLOCK
        queries = qkv_ref[0, 0, rows]
        key_rows = qkv_ref[0, 1, 0:seen]
        value_rows = qkv_ref[0, 2, 0:seen]
        j = lax.broadcasted_iota(jnp.int32, (BLOCK, seen), 1)
        i = lax.broadcasted_iota(jnp.int32, (BLOCK, seen), 0) + block * BLOCK
        visible = (j >= start_ref[rows]) & (j <= i)
        mixed = []
        for head in range(2):
            scores = dot_nt(queries * head_mask(head, score_scale), key_rows)
            scores = jnp.where(visible, scores, masked_score)
            highest = jnp.max(scores, axis=-1, keepdims=True)
            weights = jnp.exp(scores - highest)
            totals = jnp.sum(weights, axis=-1, keepdims=True)
            mixed.append(dot_nn(weights.astype(BF16), value_rows) / totals)
            lse_ref[0, head : head + 1, rows] = column_to_row(highest + jnp.log(totals))
        attn_ref[0, rows] = jnp.where(lane < HEAD_DIM, mixed[0], mixed[1]).astype(BF16)


def project_and_attend(h1, w_ref, bias_ref, start_ref, qkv_ref, attn_ref, lse_ref):
    for c in range(3):
        out = dot_nn(h1, w_ref[c].astype(BF16)) + bias_ref[c : c + 1]
        qkv_ref[0, c] = out.astype(BF16)
    attend_pair(qkv_ref, start_ref, attn_ref, lse_ref)


def own_front_kernel(
    mp_ref, x_ref, seg_ref, len_ref, gain_ref, shift_ref, w_ref, bias_ref,
    qkv_ref, attn_ref, lse_ref, h1_ref, start_ref, row_ref,
):
    @pl.when(pl.program_id(0) == 0)
    def _():
        gain = gain_ref[...].astype(F32)
        shift = shift_ref[...].astype(F32)
        for block in range(BIN // BLOCK):
            rows = slice(block * BLOCK, (block + 1) * BLOCK)
            normal, _ = norm_parts(x_ref[rows].astype(F32))
            h1_ref[rows] = (normal * gain + shift).astype(BF16)
        mine = mp_ref[0]
        count = len_ref.shape[1]
        seg = seg_ref[pl.ds(mine, 1), :].astype(F32)
        seg = jnp.broadcast_to(seg, (128, BIN)).T
        seg = seg[:, :count]
        label = lax.broadcasted_iota(jnp.int32, (BIN, count), 1).astype(F32)
        sizes = len_ref[pl.ds(mine, 1), :].astype(F32)
        start = jnp.sum(jnp.where(label < seg, sizes, 0.0), axis=1, keepdims=True)
        rows_of = jnp.sum(jnp.where(label == seg, 1.0, 0.0), axis=0, keepdims=True)
        first = jnp.sum(jnp.where(label < seg, rows_of, 0.0), axis=1, keepdims=True)
        start = jnp.maximum(start, first)
        start_ref[...] = start.astype(jnp.int32)
        row_ref[...] = column_to_row(start).astype(jnp.int32)

    project_and_attend(h1_ref[...], w_ref, bias_ref, start_ref, qkv_ref, attn_ref, lse_ref)


def other_front_kernel(h1_ref, start_ref, w_ref, bias_ref, qkv_ref, attn_ref, lse_ref):
    project_and_attend(h1_ref[...], w_ref, bias_ref, start_ref, qkv_ref, attn_ref, lse_ref)


def fixed(shape):
    return pl.BlockSpec(shape, lambda *_: (0,) * len(shape), pipeline_mode=pl.Buffered(1))


def front(mine, x, seg, lens, gain, shift, w_own, bias_own, width):
    model = x.shape[1]
    pairs = width // PAIR
    per_pair = [
        pl.BlockSpec((3, model, PAIR), lambda p, *_: (0, 0, p)),
        pl.BlockSpec((3, PAIR), lambda p, *_: (0, p)),
    ]
    outs = [
        pl.BlockSpec((1, 3, BIN, PAIR), lambda p, *_: (p, 0, 0, 0)),
        pl.BlockSpec((1, BIN, PAIR), lambda p, *_: (p, 0, 0)),
        pl.BlockSpec((1, 8, BIN), lambda p, *_: (p, 0, 0)),
    ]
    out_shapes = [
        jax.ShapeDtypeStruct((pairs, 3, BIN, PAIR), BF16),
        jax.ShapeDtypeStruct((pairs, BIN, PAIR), BF16),
        jax.ShapeDtypeStruct((pairs, 8, BIN), F32),
    ]
    cost = pl.CostEstimate(flops=6_000_000_000, bytes_accessed=10_000_000, transcendentals=0)
    params = pltpu.CompilerParams(vmem_limit_bytes=VMEM_LIMIT)
    own = pl.pallas_call(
        own_front_kernel,
        out_shape=out_shapes
        + [
            jax.ShapeDtypeStruct((BIN, model), BF16),
            jax.ShapeDtypeStruct((BIN, 1), jnp.int32),
            jax.ShapeDtypeStruct((1, BIN), jnp.int32),
        ],
        grid_spec=pltpu.PrefetchScalarGridSpec(
            num_scalar_prefetch=1,
            grid=(pairs,),
            in_specs=[
                pl.BlockSpec((BIN, model), lambda p, m: (m[0], 0)),
                fixed(seg.shape), fixed(lens.shape), fixed((1, model)), fixed((1, model)),
            ]
            + per_pair,
            out_specs=outs
            + [
                pl.BlockSpec((BIN, model), lambda p, *_: (0, 0)),
                pl.BlockSpec((BIN, 1), lambda p, *_: (0, 0)),
                pl.BlockSpec((1, BIN), lambda p, *_: (0, 0)),
            ],
        ),
        compiler_params=params,
        cost_estimate=cost,
        name="own_front",
    )

    def other(h1, start, w_other, bias_other):
        return pl.pallas_call(
            other_front_kernel,
            out_shape=out_shapes,
            grid=(pairs,),
            in_specs=[fixed((BIN, model)), fixed((BIN, 1))] + per_pair,
            out_specs=outs,
            compiler_params=params,
            cost_estimate=cost,
            name="other_front",
        )(h1, start, w_other, bias_other)

    return own(mine, x, seg, lens, gain, shift, w_own, bias_own), other


def halving_plan(order, rows):
    first, back = [], []
    size = rows
    for n, bit in enumerate(order):
        if n < len(order) - 1 and size % 16 == 0:
            size //= 2
            first.append((bit, size, 0))
            back.append((bit, size, 2))
        else:
            first.append((bit, size, 1))
    return first + back[::-1]


def color_plans(bits):
    orders = [list(range(bits)), list(range(bits))]
    if bits > 1:
        orders[1][:2] = [1, 0]
    return [halving_plan(order, CHUNK // 2) for order in orders]


def attend_back_pair(pair, qkv, dattn, lse_ref, row_ref, dk, dv, vec, pairs):
    dk[...] = jnp.zeros_like(dk)
    dv[...] = jnp.zeros_like(dv)
    half = pair // pairs
    place = pair - half * pairs
    dq_sum = jnp.zeros((1, PAIR), F32)
    for block in range(BIN // BLOCK):
        rows = slice(block * BLOCK, (block + 1) * BLOCK)
        seen = (block + 1) * BLOCK
        queries = qkv[pair, 0, rows]
        upstream = dattn[pair, rows]
        key_rows = qkv[pair, 1, 0:seen]
        value_rows = qkv[pair, 2, 0:seen]
        j = lax.broadcasted_iota(jnp.int32, (seen, BLOCK), 0)
        i = lax.broadcasted_iota(jnp.int32, (seen, BLOCK), 1) + block * BLOCK
        visible = (j >= row_ref[0:1, rows]) & (j <= i)
        dq = jnp.zeros((BLOCK, PAIR), F32)
        for head in range(2):
            masked_q = queries * head_mask(head, score_scale)
            masked_up = upstream * head_mask(head, 1.0)
            scores = dot_nt(key_rows, masked_q)
            probs = jnp.exp(scores - lse_ref[pair, head : head + 1, rows])
            probs = jnp.where(visible, probs, 0.0)
            dprobs = dot_nt(value_rows, masked_up)
            inner = jnp.sum(probs * dprobs, axis=0, keepdims=True)
            dscores = (probs * (dprobs - inner)).astype(BF16)
            dv[0:seen] = dv[0:seen] + dot_nn(probs.astype(BF16), masked_up)
            dk[0:seen] = dk[0:seen] + dot_nn(dscores, masked_q)
            dq = dq + dot_tn(dscores, key_rows * head_mask(head, 1.0))
        dq = (dq * score_scale).astype(BF16)
        qkv[pair, 0, rows] = dq
        dq_sum = dq_sum + jnp.sum(dq.astype(F32), axis=0, keepdims=True)
    dv_low = dv[...].astype(BF16)
    qkv[pair, 1] = dk[...].astype(BF16)
    qkv[pair, 2] = dv_low
    dv_sum = jnp.sum(dv_low.astype(F32), axis=0, keepdims=True)
    width = pairs * PAIR
    vec[half, 8:9, pl.ds(pl.multiple_of(place * PAIR, PAIR), PAIR)] = dq_sum
    vec[half, 8:9, pl.ds(pl.multiple_of(width + place * PAIR, PAIR), PAIR)] = dv_sum


def back_kernel(
    bits, groups,
    qkv_own_ref, qkv_other_ref, attn_own_ref, attn_other_ref, h1_ref, w3_own_ref, w3_other_ref,
    x_ref, cot_ref, wo_own_ref, wo_other_ref, wf_own_ref, wf_other_ref, wp_own_ref, wp_other_ref,
    lse_own_ref, lse_other_ref, row_ref, gain_ref, vec_in_ref, bfc_ref,
    op_ref, of_ref, oa_ref, ig_ref, sum_ref, vo_ref,
    acc, other, mpbuf, rbufs, qkv, dattn, attn, cot, x, tall, flip, total, dwide, first,
    wf_own, wf_other, wp_own, wp_other, wo_own, wo_other, w3, act, slope, lse, dk, dv, vec, vrecv,
    ssem, rsem, mps, mpr, wsem, lsem, bsem, hsem, igsem, vsem,
):
    dp = lax.axis_index("dp")
    mp = lax.axis_index("mp")
    chunks = 3 * groups
    half_rows = CHUNK // 2
    own_bits = [(dp // (1 << b)) % 2 for b in range(bits)]
    partner = [dp + (1 - 2 * own_bits[b]) * (1 << b) for b in range(bits)]
    plans = color_plans(bits)
    stages = len(plans[0])
    pairs = qkv_own_ref.shape[0]
    model = x_ref.shape[1]
    width = pairs * PAIR
    pieces = model // CHUNK

    my_rows = pl.ds(pl.multiple_of(mp * BIN, BIN), BIN)
    loads = []

    def load(src, dst):
        loads.append(pltpu.make_async_copy(src, dst, lsem.at[len(loads)]))

    load(attn_own_ref, attn.at[0:pairs])
    load(attn_other_ref, attn.at[pairs : 2 * pairs])
    load(wo_own_ref, wo_own)
    load(wo_other_ref, wo_other)
    load(x_ref.at[my_rows], x)
    load(cot_ref.at[my_rows], cot)
    early = len(loads)
    load(qkv_own_ref, qkv.at[0:pairs])
    load(qkv_other_ref, qkv.at[pairs : 2 * pairs])
    load(lse_own_ref, lse.at[0:pairs])
    load(lse_other_ref, lse.at[pairs : 2 * pairs])

    def block_loads(b):
        slot = b % 2
        at = pl.ds(pl.multiple_of(b * CHUNK, CHUNK), CHUNK)
        return [
            pltpu.make_async_copy(wf_own_ref.at[:, at], wf_own.at[slot], bsem.at[slot, 0]),
            pltpu.make_async_copy(wf_other_ref.at[:, at], wf_other.at[slot], bsem.at[slot, 1]),
            pltpu.make_async_copy(wp_own_ref.at[at], wp_own.at[slot], bsem.at[slot, 2]),
            pltpu.make_async_copy(wp_other_ref.at[at], wp_other.at[slot], bsem.at[slot, 3]),
        ]

    def w3_loads(c):
        return [
            pltpu.make_async_copy(w3_own_ref.at[c], w3.at[0], hsem.at[0]),
            pltpu.make_async_copy(w3_other_ref.at[c], w3.at[1], hsem.at[1]),
        ]

    def h1_load():
        return pltpu.make_async_copy(h1_ref, tall, hsem.at[2])

    for item in loads:
        item.start()
    for item in block_loads(0):
        item.start()

    barrier = pltpu.get_barrier_semaphore()
    for b in range(bits):
        pl.semaphore_signal(barrier, inc=1, device_id=(partner[b], mp), device_id_type=MESH)
    pl.semaphore_signal(barrier, inc=1, device_id=(dp, 1 - mp), device_id_type=MESH)
    pl.semaphore_wait(barrier, bits + 1)

    starts = []
    for color in range(2):
        base = color * half_rows
        found = []
        for bit, size, kind in plans[color]:
            found.append(base)
            if kind == 0:
                base = base + own_bits[bit] * size
            if kind == 2:
                base = base - own_bits[bit] * size
        starts.append(found)

    def copy(c, color, s):
        bit, size, kind = plans[color][s]
        slot = c % SLOTS
        base = starts[color][s]
        if kind == 0:
            base = base + (1 - own_bits[bit]) * size
        src = acc.at[c, pl.ds(pl.multiple_of(base, 8), size)]
        dst = src if kind == 2 else rbufs[color][s].at[slot]
        return pltpu.make_async_remote_copy(
            src, dst, ssem.at[slot, color, s], rsem.at[slot, color, s],
            device_id=(partner[bit], mp), device_id_type=MESH,
        )

    def finish(c, color, s):
        bit, size, kind = plans[color][s]
        copy(c, color, s).wait()
        base = starts[color][s]
        if kind == 2:
            return
        if kind == 0:
            base = base + own_bits[bit] * size
        rows = pl.ds(pl.multiple_of(base, 8), size)
        acc[c, rows] = acc[c, rows] + rbufs[color][s][c % SLOTS]

    def mp_copy(c):
        slot, place = c % SENDS, c % LANDS
        return pltpu.make_async_remote_copy(
            other.at[slot], mpbuf.at[place], mps.at[place], mpr.at[place],
            device_id=(dp, 1 - mp), device_id_type=MESH,
        )

    def mp_finish(c):
        mp_copy(c).wait()
        acc[c] = acc[c] + mpbuf[c % LANDS]

    def chunk_rows(n):
        return pl.ds(pl.multiple_of(n * CHUNK, CHUNK), CHUNK)

    def whole_copy(dst, c):
        return pltpu.make_async_copy(acc.at[c], dst, wsem.at[c % SLOTS, 0])

    def piece_copies(c):
        at = chunk_rows(c // 2)
        return [
            pltpu.make_async_copy(
                acc.at[c, :, n * CHUNK : (n + 1) * CHUNK],
                of_ref.at[n * CHUNK : (n + 1) * CHUNK, at],
                wsem.at[c % SLOTS, n],
            )
            for n in range(pieces)
        ]

    def write(c, begin):
        @pl.when((c < 2 * groups) & (c % 2 == 0))
        def _():
            item = whole_copy(op_ref.at[chunk_rows(c // 2)], c)
            item.start() if begin else item.wait()

        @pl.when((c < 2 * groups) & (c % 2 == 1))
        def _():
            for item in piece_copies(c):
                item.start() if begin else item.wait()

        @pl.when(c >= 2 * groups)
        def _():
            item = whole_copy(oa_ref.at[chunk_rows(c - 2 * groups)], c)
            item.start() if begin else item.wait()

    out_tick = groups
    attend_tick = out_tick + 1
    grad_tick = attend_tick + 2 * pairs
    input_tick = grad_tick + 2
    ticks = chunks + 1 + DELAY + stages

    def ring_tick(t):
        @pl.when((t >= 1) & (t <= groups))
        def _():
            mp_finish(2 * t - 2)
            mp_finish(2 * t - 1)

        for at, made in ((out_tick, [0]), (grad_tick, [1, 2, 3]), (grad_tick + 1, [4, 5])):
            @pl.when(t == at + 1)
            def _():
                for n in made:
                    mp_finish(2 * groups + n)

        for s in range(stages):
            c = t - (1 + DELAY + s)

            @pl.when((c >= 0) & (c < chunks))
            def _():
                for color in range(2):
                    finish(c, color, s)

        for s in range(stages)[::-1]:
            c = t - (1 + DELAY + s)

            @pl.when((c >= 0) & (c < chunks))
            def _():
                if s + 1 == stages:
                    write(c, True)
                else:
                    for color in range(2):
                        copy(c, color, s + 1).start()

        c = t - 1

        @pl.when((c >= 0) & (c < chunks))
        def _():
            for color in range(2):
                copy(c, color, 0).start()

    def begin_layer():
        for item in loads[:early]:
            item.wait()
        out_bias = vec_in_ref[0:1]
        gain = vec_in_ref[1:2]
        shift = vec_in_ref[2:3]
        wo = [wo_own[...], wo_other[...].astype(BF16)]
        vec[...] = jnp.zeros_like(vec)
        for block in range(BIN // BLOCK):
            rows = slice(block * BLOCK, (block + 1) * BLOCK)
            branch = out_bias
            for half in range(2):
                mixed = [attn[half * pairs + p, rows] for p in range(pairs)]
                branch = branch + dot_nn(jnp.concatenate(mixed, axis=1), wo[half])
            r1 = x[rows].astype(F32) + branch
            first[rows] = r1
            total[rows] = r1
            normal, _ = norm_parts(r1)
            h2 = (normal * gain + shift).astype(BF16)
            tall[rows] = h2
            flip[:, rows] = h2.T

    def hidden_block(b):
        slot = b % 2
        for item in block_loads(b):
            item.wait()

        @pl.when(b + 1 < groups)
        def _():
            for item in block_loads(b + 1):
                item.start()

        span = 2 * BLOCK
        for half in range(2):
            wf = wf_own[slot] if half == 0 else wf_other[slot].astype(BF16)
            wp = wp_own[slot] if half == 0 else wp_other[slot].astype(BF16)
            bias = bfc_ref[pl.ds(half * groups + b, 1), :]
            df_sum = jnp.zeros((1, CHUNK), F32)
            for block in range(BIN // span):
                rows = slice(block * span, (block + 1) * span)
                pre = dot_nn(tall[rows], wf) + bias
                hidden, rise = gelu_pair(pre)
                hidden = hidden.astype(BF16)
                act[rows] = hidden
                total[rows] = total[rows] + dot_nn(hidden, wp)
                df = (dot_nt(cot[rows], wp) * rise).astype(BF16)
                slope[rows] = df
                df_sum = df_sum + jnp.sum(df.astype(F32), axis=0, keepdims=True)
                up = dot_nt(df, wf)

                @pl.when(b == 0)
                def _():
                    if half == 0:
                        dwide[rows] = up
                    else:
                        dwide[rows] = dwide[rows] + up

                @pl.when(b > 0)
                def _():
                    dwide[rows] = dwide[rows] + up

            vec[half, pl.ds(6 + b // pieces, 1), pl.ds(pl.multiple_of((b % pieces) * CHUNK, CHUNK), CHUNK)] = df_sum
            proj = dot_tn(act[...], cot[...])
            fc = dot_nn(flip[...], slope[...])
            if half == 0:
                acc[2 * b] = proj
                for n in range(pieces):
                    acc[2 * b + 1, :, n * CHUNK : (n + 1) * CHUNK] = fc[n * CHUNK : (n + 1) * CHUNK]
            else:
                other[(2 * b) % SENDS] = proj
                at = (2 * b + 1) % SENDS
                for n in range(pieces):
                    other[at, :, n * CHUNK : (n + 1) * CHUNK] = fc[n * CHUNK : (n + 1) * CHUNK]
        mp_copy(2 * b).start()
        mp_copy(2 * b + 1).start()

    def put_grad(half, row, value):
        rows = value.shape[0]
        for piece in range(rows // 128):
            at = row + piece * 128
            block = value[piece * 128 : (piece + 1) * 128]
            chunk, place = at // CHUNK, slice(at % CHUNK, at % CHUNK + 128)
            if half == 0:
                acc[2 * groups + chunk, place] = block
            else:
                other[(2 * groups + chunk) % SENDS, place] = block

    def sum_copies():
        local = pltpu.make_async_copy(total, sum_ref.at[my_rows], igsem.at[3])
        remote = pltpu.make_async_remote_copy(
            total, sum_ref.at[my_rows], igsem.at[4], igsem.at[5],
            device_id=(dp, 1 - mp), device_id_type=MESH,
        )
        return local, remote

    def middle_back():
        for item in sum_copies():
            item.start()
        gain = vec_in_ref[1:2]
        sums = [jnp.zeros((1, model), F32) for _ in range(4)]
        wo = [wo_own[...], wo_other[...].astype(BF16)]
        for block in range(BIN // BLOCK):
            rows = slice(block * BLOCK, (block + 1) * BLOCK)
            normal, inverse = norm_parts(first[rows])
            up = dwide[rows]
            upstream = cot[rows].astype(F32)
            dr1 = upstream + norm_back(up, normal, inverse, gain)
            first[rows] = dr1
            da = dr1.astype(BF16)
            tall[rows] = da
            for n, item in enumerate((da.astype(F32), up * normal, up, upstream)):
                sums[n] = sums[n] + jnp.sum(item, axis=0, keepdims=True)
            for half in range(2):
                back = dot_nt(da, wo[half]).astype(BF16)
                for p in range(pairs):
                    dattn[half * pairs + p, rows] = back[:, p * PAIR : (p + 1) * PAIR]
        for half in range(2):
            for n in range(4):
                vec[half, 2 + n : 3 + n] = sums[n]
            mixed = jnp.concatenate([attn[half * pairs + p] for p in range(pairs)], axis=1)
            put_grad(half, 0, dot_tn(mixed, tall[...]))
        mp_copy(2 * groups).start()
        h1_load().start()
        for item in w3_loads(0):
            item.start()
        for item in loads[early:]:
            item.wait()

    def qkv_grad(c):
        if c == 0:
            h1_load().wait()
            flip[...] = tall[...].T
        for item in w3_loads(c):
            item.wait()
        for half in range(2):
            low = jnp.concatenate([qkv[half * pairs + p, c] for p in range(pairs)], axis=1)
            grad = dot_nn(flip[...], low)
            split = model // 2
            put_grad(half, width * (c + 1), jnp.concatenate([grad[:split], grad[split:]], axis=1))
            part = dot_nt(low, w3[half].astype(BF16))
            if half == 0 and c == 0:
                dwide[...] = part
            else:
                dwide[...] = dwide[...] + part
        if c < 2:
            for item in w3_loads(c + 1):
                item.start()

    def input_grad():
        gain = gain_ref[...].astype(F32)
        gain_sum = jnp.zeros((1, model), F32)
        shift_sum = jnp.zeros((1, model), F32)
        for block in range(BIN // BLOCK):
            rows = slice(block * BLOCK, (block + 1) * BLOCK)
            normal, inverse = norm_parts(x[rows].astype(F32))
            up = dwide[rows]
            gain_sum = gain_sum + jnp.sum(up * normal, axis=0, keepdims=True)
            shift_sum = shift_sum + jnp.sum(up, axis=0, keepdims=True)
            first[rows] = first[rows] + norm_back(up, normal, inverse, gain)
        for half in range(2):
            vec[half, 0:1] = gain_sum
            vec[half, 1:2] = shift_sum

    def ig_copies():
        local = pltpu.make_async_copy(first, ig_ref.at[my_rows], igsem.at[0])
        remote = pltpu.make_async_remote_copy(
            first, ig_ref.at[my_rows], igsem.at[1], igsem.at[2],
            device_id=(dp, 1 - mp), device_id_type=MESH,
        )
        return local, remote

    def vec_copy(n):
        if n == 0:
            src, device = vec.at[1], (dp, 1 - mp)
        else:
            src, device = vec.at[0], (partner[n - 1], mp)
        return pltpu.make_async_remote_copy(
            src, vrecv.at[n], vsem.at[0, n], vsem.at[1, n], device_id=device, device_id_type=MESH
        )

    begin_layer()

    def tick(t, carry):
        ring_tick(t)

        @pl.when(t < groups)
        def _():
            hidden_block(t)

        @pl.when(t == out_tick)
        def _():
            middle_back()

        @pl.when((t >= attend_tick) & (t < grad_tick))
        def _():
            attend_back_pair(t - attend_tick, qkv, dattn, lse, row_ref, dk, dv, vec, pairs)

        @pl.when(t == grad_tick)
        def _():
            qkv_grad(0)
            qkv_grad(1)
            for n in (1, 2, 3):
                mp_copy(2 * groups + n).start()

        @pl.when(t == grad_tick + 1)
        def _():
            qkv_grad(2)
            for n in (4, 5):
                mp_copy(2 * groups + n).start()

        @pl.when(t == input_tick)
        def _():
            input_grad()
            for item in ig_copies():
                item.start()
            vec_copy(0).start()

        for n in range(bits + 1):
            @pl.when(t == input_tick + 1 + n)
            def _():
                vec_copy(n).wait()
                vec[0] = vec[0] + vrecv[n]
                if n < bits:
                    vec_copy(n + 1).start()

        c = t - (1 + DELAY + stages)

        @pl.when(c >= 0)
        def _():
            write(c, False)

        return carry

    lax.fori_loop(0, ticks, tick, 0)
    for item in ig_copies() + sum_copies():
        item.wait()
    vo_ref[...] = vec[0]


def back(bits, arrays, row, gain, vec_in, bfc, sizes):
    pairs, hidden, model = sizes
    width = pairs * PAIR
    groups = hidden // CHUNK
    chunks = 3 * groups
    plans = color_plans(bits)
    stages = len(plans[0])
    recv = [
        [pltpu.VMEM((SLOTS, size, model), F32) for _, size, kind in plan if kind < 2]
        for plan in plans
    ]
    here = pl.BlockSpec(memory_space=pl.ANY)
    vmem = pl.BlockSpec(memory_space=pltpu.VMEM)
    dma = pltpu.SemaphoreType.DMA
    return pl.pallas_call(
        functools.partial(back_kernel, bits, groups),
        out_shape=[
            jax.ShapeDtypeStruct((hidden, model), F32),
            jax.ShapeDtypeStruct((model, hidden), F32),
            jax.ShapeDtypeStruct((4 * width, model), F32),
            jax.ShapeDtypeStruct((2 * BIN, model), F32),
            jax.ShapeDtypeStruct((2 * BIN, model), F32),
            jax.ShapeDtypeStruct((16, model), F32),
        ],
        in_specs=[here] * len(arrays) + [vmem] * 4,
        out_specs=[here] * 5 + [vmem],
        scratch_shapes=[
            pltpu.VMEM((chunks, CHUNK, model), F32),
            pltpu.VMEM((SENDS, CHUNK, model), F32),
            pltpu.VMEM((LANDS, CHUNK, model), F32),
            recv,
            pltpu.VMEM((2 * pairs, 3, BIN, PAIR), BF16),
            pltpu.VMEM((2 * pairs, BIN, PAIR), BF16),
            pltpu.VMEM((2 * pairs, BIN, PAIR), BF16),
            pltpu.VMEM((BIN, model), BF16),
            pltpu.VMEM((BIN, model), BF16),
            pltpu.VMEM((BIN, model), BF16),
            pltpu.VMEM((model, BIN), BF16),
            pltpu.VMEM((BIN, model), F32),
            pltpu.VMEM((BIN, model), F32),
            pltpu.VMEM((BIN, model), F32),
            pltpu.VMEM((2, model, CHUNK), BF16),
            pltpu.VMEM((2, model, CHUNK), F32),
            pltpu.VMEM((2, CHUNK, model), BF16),
            pltpu.VMEM((2, CHUNK, model), F32),
            pltpu.VMEM((width, model), BF16),
            pltpu.VMEM((width, model), F32),
            pltpu.VMEM((2, model, width), F32),
            pltpu.VMEM((BIN, CHUNK), BF16),
            pltpu.VMEM((BIN, CHUNK), BF16),
            pltpu.VMEM((2 * pairs, 8, BIN), F32),
            pltpu.VMEM((BIN, PAIR), F32),
            pltpu.VMEM((BIN, PAIR), F32),
            pltpu.VMEM((2, 16, model), F32),
            pltpu.VMEM((bits + 1, 16, model), F32),
            dma((SLOTS, 2, stages)),
            dma((SLOTS, 2, stages)),
            dma((LANDS,)),
            dma((LANDS,)),
            dma((SLOTS, model // CHUNK)),
            dma((10,)),
            dma((2, 4)),
            dma((3,)),
            dma((6,)),
            dma((2, bits + 1)),
        ],
        compiler_params=pltpu.CompilerParams(
            collective_id=0, has_side_effects=True, vmem_limit_bytes=67_043_328
        ),
        name="back",
    )(*arrays, row, gain, vec_in, bfc)


def on_device(
    tokens, segments, lengths, ln1_gain, ln1_bias, w_qkv, b_qv, w_out, out_bias,
    ln2_gain, ln2_bias, w_fc, b_fc, w_proj, proj_bias, cotangent,
):
    model = tokens.shape[1]
    width = w_qkv.shape[2]
    hidden = w_fc.shape[1]
    pairs = width // PAIR
    groups = lax.axis_size("dp")
    bits = groups.bit_length() - 1
    if lax.axis_size("mp") != 2 or groups != 1 << bits or tokens.shape[0] != 2 * BIN:
        raise ValueError("unsupported mesh")
    side = lax.axis_index("mp")
    mine = side.astype(jnp.int32).reshape(1)
    swap = [(0, 1), (1, 0)]

    def cross(value):
        return lax.ppermute(value, "mp", swap)

    w3 = jnp.transpose(w_qkv, (1, 0, 2)).astype(F32)
    small = jnp.concatenate([b_qv.reshape(-1), b_fc]).astype(F32)
    small_other = cross(small)
    w3_other = cross(w3)
    wo_other = cross(w_out.astype(F32))
    wf_other = cross(w_fc.astype(F32))
    wp_other = cross(w_proj.astype(F32))

    def qkv_bias(flat):
        return jnp.stack([flat[:width], jnp.zeros((width,), F32), flat[width : 2 * width]])

    own, other_front = front(
        mine, tokens, segments.reshape(2, BIN), lengths,
        ln1_gain.reshape(1, -1), ln1_bias.reshape(1, -1), w3, qkv_bias(small), width,
    )
    qkv_own, attn_own, lse_own, h1, start, row = own
    small_other, w3_other, h1 = lax.optimization_barrier((small_other, w3_other, h1))
    qkv_other, attn_other, lse_other = other_front(h1, start, w3_other, qkv_bias(small_other))
    vec_in = jnp.stack([out_bias, ln2_gain, ln2_bias, proj_bias]).astype(F32)
    bfc = jnp.concatenate([small[2 * width :], small_other[2 * width :]]).reshape(-1, CHUNK)
    arrays = (
        qkv_own, qkv_other, attn_own, attn_other, h1, w3, w3_other, tokens, cotangent,
        w_out, wo_other, w_fc, wf_other, w_proj, wp_other, lse_own, lse_other,
    )
    grad_proj, grad_fc, grad_attn, input_grad, block_sum, rows = back(
        bits, arrays, row, ln1_gain.reshape(1, -1), vec_in, bfc, (pairs, hidden, model)
    )
    block_out = (block_sum + vec_in[3]).astype(BF16)
    grad_out = grad_attn[:width]
    grad_qkv = grad_attn[width:].reshape(3, width, 2, width)
    grad_qkv = jnp.transpose(grad_qkv, (2, 1, 0, 3)).reshape(model, 3, width)
    return (
        block_out,
        input_grad,
        rows[0],
        rows[1],
        grad_qkv,
        rows[8].reshape(2, width),
        grad_out,
        rows[2],
        rows[3],
        rows[4],
        grad_fc,
        rows[6:8].reshape(-1),
        grad_proj,
        rows[5],
    )


def solution(mesh):
    rows = P("dp", None)
    placed = (
        rows, P("dp"), rows, P(), P(), P(None, None, "mp"), P(None, "mp"), P("mp", None), P(),
        P(), P(), P(None, "mp"), P("mp"), P("mp", None), P(), rows,
    )
    results = (
        rows, rows, P(), P(), P(None, None, "mp"), P(None, "mp"), P("mp", None), P(), P(), P(),
        P(None, "mp"), P("mp"), P("mp", None), P(),
    )
    return jax.shard_map(
        on_device, mesh=mesh, in_specs=placed, out_specs=results, check_vma=False
    )
```

```python
import functools

import jax
import jax.numpy as jnp
from jax import lax
from jax.experimental import pallas as pl
from jax.experimental.pallas import tpu as pltpu
from jax.sharding import PartitionSpec as P

HEAD_DIM = 64
BIN = 1024
PAIR = 2 * HEAD_DIM
BLOCK = 256
CHUNK = 256
SLOTS = 4
SENDS = 4
LANDS = 5

epsilon = 1e-05
gelu_scale = 0.7978845608028654
gelu_cubic = 0.044715
score_scale = 0.125
masked_score = -1e30

MESH = pl.DeviceIdType.MESH
F32 = jnp.float32
BF16 = jnp.bfloat16
VMEM_LIMIT = 64_000_000


def dot_nn(left, right):
    return lax.dot_general(left, right, (((1,), (0,)), ((), ())), preferred_element_type=F32)


def dot_nt(left, right):
    return lax.dot_general(left, right, (((1,), (1,)), ((), ())), preferred_element_type=F32)


def dot_tn(left, right):
    return lax.dot_general(left, right, (((0,), (0,)), ((), ())), preferred_element_type=F32)


def norm_parts(values):
    center = values - jnp.mean(values, axis=-1, keepdims=True)
    inverse = lax.rsqrt(jnp.mean(center * center, axis=-1, keepdims=True) + epsilon)
    return center * inverse, inverse


def norm_back(upstream, normal, inverse, gain):
    scaled = upstream * gain
    centered = scaled - jnp.mean(scaled, axis=-1, keepdims=True)
    return inverse * (centered - normal * jnp.mean(scaled * normal, axis=-1, keepdims=True))


def gelu_pair(values):
    square = values * values
    tangent = jnp.tanh(gelu_scale * (values + gelu_cubic * square * values))
    half = 0.5 * (1.0 + tangent)
    slope = half + 0.5 * values * (1.0 - tangent * tangent) * (
        gelu_scale + 3.0 * gelu_cubic * gelu_scale * square
    )
    return values * half, slope


def column_to_row(column):
    rows = column.shape[0]
    return jnp.broadcast_to(column, (rows, 128)).T[0:1]


def head_mask(head, scale):
    lane = lax.broadcasted_iota(jnp.int32, (1, PAIR), 1)
    return jnp.where(lane // HEAD_DIM == head, scale, 0.0).astype(BF16)


def attend_pair(qkv_ref, start_ref, attn_ref, lse_ref):
    lane = lax.broadcasted_iota(jnp.int32, (1, PAIR), 1)
    for block in range(BIN // BLOCK):
        rows = slice(block * BLOCK, (block + 1) * BLOCK)
        seen = (block + 1) * BLOCK
        queries = qkv_ref[0, 0, rows]
        key_rows = qkv_ref[0, 1, 0:seen]
        value_rows = qkv_ref[0, 2, 0:seen]
        j = lax.broadcasted_iota(jnp.int32, (BLOCK, seen), 1)
        i = lax.broadcasted_iota(jnp.int32, (BLOCK, seen), 0) + block * BLOCK
        visible = (j >= start_ref[rows]) & (j <= i)
        mixed = []
        for head in range(2):
            scores = dot_nt(queries * head_mask(head, score_scale), key_rows)
            scores = jnp.where(visible, scores, masked_score)
            highest = jnp.max(scores, axis=-1, keepdims=True)
            weights = jnp.exp(scores - highest)
            totals = jnp.sum(weights, axis=-1, keepdims=True)
            mixed.append(dot_nn(weights.astype(BF16), value_rows) / totals)
            lse_ref[0, head : head + 1, rows] = column_to_row(highest + jnp.log(totals))
        attn_ref[0, rows] = jnp.where(lane < HEAD_DIM, mixed[0], mixed[1]).astype(BF16)


def project_and_attend(h1, w_ref, bias_ref, start_ref, qkv_ref, attn_ref, lse_ref):
    for c in range(3):
        out = dot_nn(h1, w_ref[c].astype(BF16)) + bias_ref[c : c + 1]
        qkv_ref[0, c] = out.astype(BF16)
    attend_pair(qkv_ref, start_ref, attn_ref, lse_ref)


def own_front_kernel(
    mp_ref, x_ref, seg_ref, len_ref, gain_ref, shift_ref, w_ref, bias_ref,
    qkv_ref, attn_ref, lse_ref, h1_ref, start_ref, row_ref,
):
    @pl.when(pl.program_id(0) == 0)
    def _():
        gain = gain_ref[...].astype(F32)
        shift = shift_ref[...].astype(F32)
        for block in range(BIN // BLOCK):
            rows = slice(block * BLOCK, (block + 1) * BLOCK)
            normal, _ = norm_parts(x_ref[rows].astype(F32))
            h1_ref[rows] = (normal * gain + shift).astype(BF16)
        mine = mp_ref[0]
        count = len_ref.shape[1]
        seg = seg_ref[pl.ds(mine, 1), :].astype(F32)
        seg = jnp.broadcast_to(seg, (128, BIN)).T
        seg = seg[:, :count]
        label = lax.broadcasted_iota(jnp.int32, (BIN, count), 1).astype(F32)
        sizes = len_ref[pl.ds(mine, 1), :].astype(F32)
        start = jnp.sum(jnp.where(label < seg, sizes, 0.0), axis=1, keepdims=True)
        rows_of = jnp.sum(jnp.where(label == seg, 1.0, 0.0), axis=0, keepdims=True)
        first = jnp.sum(jnp.where(label < seg, rows_of, 0.0), axis=1, keepdims=True)
        start = jnp.maximum(start, first)
        start_ref[...] = start.astype(jnp.int32)
        row_ref[...] = column_to_row(start).astype(jnp.int32)

    project_and_attend(h1_ref[...], w_ref, bias_ref, start_ref, qkv_ref, attn_ref, lse_ref)


def other_front_kernel(h1_ref, start_ref, w_ref, bias_ref, qkv_ref, attn_ref, lse_ref):
    project_and_attend(h1_ref[...], w_ref, bias_ref, start_ref, qkv_ref, attn_ref, lse_ref)


def fixed(shape):
    return pl.BlockSpec(shape, lambda *_: (0,) * len(shape), pipeline_mode=pl.Buffered(1))


def front(mine, x, seg, lens, gain, shift, w_own, bias_own, width):
    model = x.shape[1]
    pairs = width // PAIR
    per_pair = [
        pl.BlockSpec((3, model, PAIR), lambda p, *_: (0, 0, p)),
        pl.BlockSpec((3, PAIR), lambda p, *_: (0, p)),
    ]
    outs = [
        pl.BlockSpec((1, 3, BIN, PAIR), lambda p, *_: (p, 0, 0, 0)),
        pl.BlockSpec((1, BIN, PAIR), lambda p, *_: (p, 0, 0)),
        pl.BlockSpec((1, 8, BIN), lambda p, *_: (p, 0, 0)),
    ]
    out_shapes = [
        jax.ShapeDtypeStruct((pairs, 3, BIN, PAIR), BF16),
        jax.ShapeDtypeStruct((pairs, BIN, PAIR), BF16),
        jax.ShapeDtypeStruct((pairs, 8, BIN), F32),
    ]
    cost = pl.CostEstimate(flops=6_000_000_000, bytes_accessed=10_000_000, transcendentals=0)
    params = pltpu.CompilerParams(vmem_limit_bytes=VMEM_LIMIT)
    own = pl.pallas_call(
        own_front_kernel,
        out_shape=out_shapes
        + [
            jax.ShapeDtypeStruct((BIN, model), BF16),
            jax.ShapeDtypeStruct((BIN, 1), jnp.int32),
            jax.ShapeDtypeStruct((1, BIN), jnp.int32),
        ],
        grid_spec=pltpu.PrefetchScalarGridSpec(
            num_scalar_prefetch=1,
            grid=(pairs,),
            in_specs=[
                pl.BlockSpec((BIN, model), lambda p, m: (m[0], 0)),
                fixed(seg.shape), fixed(lens.shape), fixed((1, model)), fixed((1, model)),
            ]
            + per_pair,
            out_specs=outs
            + [
                pl.BlockSpec((BIN, model), lambda p, *_: (0, 0)),
                pl.BlockSpec((BIN, 1), lambda p, *_: (0, 0)),
                pl.BlockSpec((1, BIN), lambda p, *_: (0, 0)),
            ],
        ),
        compiler_params=params,
        cost_estimate=cost,
        name="own_front",
    )

    def other(h1, start, w_other, bias_other):
        return pl.pallas_call(
            other_front_kernel,
            out_shape=out_shapes,
            grid=(pairs,),
            in_specs=[fixed((BIN, model)), fixed((BIN, 1))] + per_pair,
            out_specs=outs,
            compiler_params=params,
            cost_estimate=cost,
            name="other_front",
        )(h1, start, w_other, bias_other)

    return own(mine, x, seg, lens, gain, shift, w_own, bias_own), other


def halving_plan(order, rows):
    first, back = [], []
    size = rows
    for n, bit in enumerate(order):
        if n < len(order) - 1 and size % 16 == 0:
            size //= 2
            first.append((bit, size, 0))
            back.append((bit, size, 2))
        else:
            first.append((bit, size, 1))
    return first + back[::-1]


def color_orders(bits, odd):
    plain = list(range(bits))
    orders = [plain, plain, plain]
    if bits > 1:
        orders[1] = [1, 0] + plain[2:]
    if bits > 2:
        orders[2] = [2, 1, 0] + plain[3:] if odd else [2, 0, 1] + plain[3:]
    return orders


def color_plans(bits, odd):
    return [halving_plan(order, CHUNK) for order in color_orders(bits, odd)]


def attend_back_pair(half, place, qkv, dattn, lse_ref, row_ref, dk, dv, vec, pairs):
    dk[...] = jnp.zeros_like(dk)
    dv[...] = jnp.zeros_like(dv)
    pair = half * pairs + place
    dq_sum = jnp.zeros((1, PAIR), F32)
    for block in range(BIN // BLOCK):
        rows = slice(block * BLOCK, (block + 1) * BLOCK)
        seen = (block + 1) * BLOCK
        queries = qkv[pair, 0, rows]
        upstream = dattn[pair, rows]
        key_rows = qkv[pair, 1, 0:seen]
        value_rows = qkv[pair, 2, 0:seen]
        j = lax.broadcasted_iota(jnp.int32, (seen, BLOCK), 0)
        i = lax.broadcasted_iota(jnp.int32, (seen, BLOCK), 1) + block * BLOCK
        visible = (j >= row_ref[0:1, rows]) & (j <= i)
        dq = jnp.zeros((BLOCK, PAIR), F32)
        for head in range(2):
            masked_q = queries * head_mask(head, score_scale)
            masked_up = upstream * head_mask(head, 1.0)
            scores = dot_nt(key_rows, masked_q)
            probs = jnp.exp(scores - lse_ref[pair, head : head + 1, rows])
            probs = jnp.where(visible, probs, 0.0)
            dprobs = dot_nt(value_rows, masked_up)
            inner = jnp.sum(probs * dprobs, axis=0, keepdims=True)
            dscores = (probs * (dprobs - inner)).astype(BF16)
            dv[0:seen] = dv[0:seen] + dot_nn(probs.astype(BF16), masked_up)
            dk[0:seen] = dk[0:seen] + dot_nn(dscores, masked_q)
            dq = dq + dot_tn(dscores, key_rows * head_mask(head, 1.0))
        dq = (dq * score_scale).astype(BF16)
        qkv[pair, 0, rows] = dq
        dq_sum = dq_sum + jnp.sum(dq.astype(F32), axis=0, keepdims=True)
    dv_low = dv[...].astype(BF16)
    qkv[pair, 1] = dk[...].astype(BF16)
    qkv[pair, 2] = dv_low
    dv_sum = jnp.sum(dv_low.astype(F32), axis=0, keepdims=True)
    width = pairs * PAIR
    vec[half, 8:9, pl.ds(pl.multiple_of(place * PAIR, PAIR), PAIR)] = dq_sum
    vec[half, 8:9, pl.ds(pl.multiple_of(width + place * PAIR, PAIR), PAIR)] = dv_sum


def back_kernel(
    bits, groups,
    qkv_own_ref, qkv_other_ref, attn_own_ref, attn_other_ref, h1_ref, w3_own_ref, w3_other_ref,
    x_ref, cot_ref, wo_own_ref, wo_other_ref, wf_own_ref, wf_other_ref, wp_own_ref, wp_other_ref,
    lse_own_ref, lse_other_ref, row_ref, gain_ref, vec_in_ref, bfc_ref,
    op_ref, of_ref, oa_ref, oq_ref, ig_ref, sum_ref, vo_ref,
    acc, mpbuf, rbufs, qkv, dattn, attn, cot, x, tall, flip, total, dwide, first,
    wf, wp, wo, w3, act, slope, lse, dk, dv, vec, vrecv,
    ssem, rsem, mps, mpr, wsem, lsem, bsem, hsem, igsem, vsem,
):
    dp = lax.axis_index("dp")
    mp = lax.axis_index("mp")
    chunks = 3 * groups
    own_bits = [(dp // (1 << b)) % 2 for b in range(bits)]
    partner = [dp + (1 - 2 * own_bits[b]) * (1 << b) for b in range(bits)]
    plans = [color_plans(bits, odd) for odd in range(2)]
    stages = len(plans[0][0])
    flights = [2] + [1] * (stages - 2) + [2]
    offsets = [sum(flights[:s]) for s in range(stages + 1)]
    pairs = qkv_own_ref.shape[0]
    model = x_ref.shape[1]
    width = pairs * PAIR
    pieces = model // CHUNK

    my_rows = pl.ds(pl.multiple_of(mp * BIN, BIN), BIN)
    loads = []

    def load(src, dst):
        loads.append(pltpu.make_async_copy(src, dst, lsem.at[len(loads)]))

    load(attn_own_ref, attn.at[0:pairs])
    load(attn_other_ref, attn.at[pairs : 2 * pairs])
    load(wo_own_ref, wo.at[0])
    load(wo_other_ref, wo.at[1])
    load(x_ref.at[my_rows], x)
    load(cot_ref.at[my_rows], cot)
    early = len(loads)
    load(qkv_own_ref, qkv.at[0:pairs])
    load(qkv_other_ref, qkv.at[pairs : 2 * pairs])
    load(lse_own_ref, lse.at[0:pairs])
    load(lse_other_ref, lse.at[pairs : 2 * pairs])

    def block_loads(u, begin):
        slot = u % 2
        at = pl.ds(pl.multiple_of((u // 2) * CHUNK, CHUNK), CHUNK)
        for half, fc_ref, proj_ref in ((0, wf_own_ref, wp_own_ref), (1, wf_other_ref, wp_other_ref)):
            @pl.when(slot == half)
            def _():
                for item in (
                    pltpu.make_async_copy(fc_ref.at[:, at], wf.at[half], bsem.at[half, 0]),
                    pltpu.make_async_copy(proj_ref.at[at], wp.at[half], bsem.at[half, 1]),
                ):
                    item.start() if begin else item.wait()

    def w3_loads(q, begin):
        slot = q % 2
        at = pl.ds(pl.multiple_of((q // 2) * PAIR, PAIR), PAIR)
        for half, ref in ((0, w3_own_ref), (1, w3_other_ref)):
            @pl.when(slot == half)
            def _():
                for c in range(3):
                    item = pltpu.make_async_copy(ref.at[c, :, at], w3.at[half, c], hsem.at[half, c])
                    item.start() if begin else item.wait()

    def h1_load():
        return pltpu.make_async_copy(h1_ref, tall, lsem.at[9])

    for item in loads:
        item.start()
    block_loads(jnp.int32(0), True)

    barrier = pltpu.get_barrier_semaphore()
    for b in range(bits):
        pl.semaphore_signal(barrier, inc=1, device_id=(partner[b], mp), device_id_type=MESH)
    pl.semaphore_signal(barrier, inc=1, device_id=(dp, 1 - mp), device_id_type=MESH)
    pl.semaphore_wait(barrier, bits + 1)

    def walk(plan):
        base, found = 0, []
        for bit, size, kind in plan:
            found.append(base)
            if kind == 0:
                base = base + own_bits[bit] * size
            if kind == 2:
                base = base - own_bits[bit] * size
        return found

    starts = [[walk(plan) for plan in plans[odd]] for odd in range(2)]

    def place(c, color, s):
        sides = []
        for odd in range(2):
            bit, size, kind = plans[odd][color][s]
            sides.append((starts[odd][color][s], own_bits[bit], partner[bit]))
        if plans[0][color] == plans[1][color]:
            return sides[0]
        return [jnp.where(c % 2 == 0, even, odd) for even, odd in zip(*sides)]

    def lanes(color):
        share = model // 3
        return slice(color * share, (color + 1) * share)

    def copy(c, color, s):
        _, size, kind = plans[0][color][s]
        slot = c % SLOTS
        base, side, device = place(c, color, s)
        if kind == 0:
            base = base + (1 - side) * size
        src = acc.at[c, pl.ds(pl.multiple_of(base, 8), size), lanes(color)]
        dst = src if kind == 2 else rbufs[color][s].at[slot]
        return pltpu.make_async_remote_copy(
            src, dst, ssem.at[slot, color, s], rsem.at[slot, color, s],
            device_id=(device, mp), device_id_type=MESH,
        )

    def finish(c, color, s):
        _, size, kind = plans[0][color][s]
        copy(c, color, s).wait()
        if kind == 2:
            return
        base, side, _ = place(c, color, s)
        if kind == 0:
            base = base + side * size
        rows = pl.ds(pl.multiple_of(base, 8), size)
        acc[c, rows, lanes(color)] = acc[c, rows, lanes(color)] + rbufs[color][s][c % SLOTS]

    def mp_copy(c):
        slot, land = c % SENDS, c % LANDS
        return pltpu.make_async_remote_copy(
            acc.at[chunks + slot], mpbuf.at[land], mps.at[land], mpr.at[land],
            device_id=(dp, 1 - mp), device_id_type=MESH,
        )

    def mp_finish(c):
        mp_copy(c).wait()
        acc[c] = acc[c] + mpbuf[c % LANDS]

    def chunk_rows(n):
        return pl.ds(pl.multiple_of(n * CHUNK, CHUNK), CHUNK)

    def whole_copy(dst, c):
        return pltpu.make_async_copy(acc.at[c], dst, wsem.at[c % SLOTS, 0])

    def piece_copies(c):
        at = chunk_rows(c // 2)
        return [
            pltpu.make_async_copy(
                acc.at[c, :, n * CHUNK : (n + 1) * CHUNK],
                of_ref.at[n * CHUNK : (n + 1) * CHUNK, at],
                wsem.at[c % SLOTS, n],
            )
            for n in range(pieces)
        ]

    def write(c, begin):
        @pl.when((c < 2 * groups) & (c % 2 == 0))
        def _():
            item = whole_copy(op_ref.at[chunk_rows(c // 2)], c)
            item.start() if begin else item.wait()

        @pl.when((c < 2 * groups) & (c % 2 == 1))
        def _():
            for item in piece_copies(c):
                item.start() if begin else item.wait()

        for part in range(2):
            piece = 2 * (c - 2 * groups) + part
            rows = slice(part * PAIR, (part + 1) * PAIR)

            @pl.when((c >= 2 * groups) & (piece < pairs))
            def _():
                at = pl.ds(pl.multiple_of(piece * PAIR, PAIR), PAIR)
                item = pltpu.make_async_copy(acc.at[c, rows], oa_ref.at[at], wsem.at[c % SLOTS, 6 * part])
                item.start() if begin else item.wait()

            @pl.when((c >= 2 * groups) & (piece >= pairs))
            def _():
                across = pl.ds(pl.multiple_of((piece // pairs - 1) * PAIR, PAIR), PAIR)
                for n in range(6):
                    down = pl.ds(pl.multiple_of((n // 3) * width + (piece % pairs) * PAIR, PAIR), PAIR)
                    item = pltpu.make_async_copy(
                        acc.at[c, rows, n * PAIR : (n + 1) * PAIR],
                        oq_ref.at[n % 3, down, across],
                        wsem.at[c % SLOTS, 6 * part + n],
                    )
                    item.start() if begin else item.wait()

    middle_tick = 2 * groups
    attend_tick = middle_tick + 1
    input_tick = attend_tick + 2 * pairs
    late = chunks - 4
    late_tick = late + 4
    arrivals = [(middle_tick + 2, [0]), (middle_tick + 4, [1, 2]), (middle_tick + 6, [3]), (middle_tick + 8, [4, 5])]
    ticks = chunks + 4 + offsets[stages] + 1

    def at_stage(t, shift):
        since = t - shift
        early = (since >= 3) & (since < late + 3)
        last = (since >= late_tick) & (since < chunks + 4)
        c = jnp.where(since < late_tick, since - 3, since - late_tick + late)
        return jnp.clip(c, 0, chunks - 1), early | last

    def ring_tick(t):
        @pl.when((t >= 3) & (t % 2 == 1) & (t < middle_tick + 3))
        def _():
            mp_finish(t - 3)
            mp_finish(t - 2)

        for at, made in arrivals:
            @pl.when(t == at)
            def _():
                for n in made:
                    mp_finish(2 * groups + n)

        for s in range(stages):
            c, valid = at_stage(t, offsets[s + 1])

            @pl.when(valid)
            def _():
                for color in range(3):
                    finish(c, color, s)

        for s in list(range(stages)) + [-1]:
            c, valid = at_stage(t, offsets[s + 1])

            @pl.when(valid)
            def _():
                if s + 1 == stages:
                    write(c, True)
                else:
                    for color in range(3):
                        copy(c, color, s + 1).start()

    def begin_layer():
        for item in loads[:early]:
            item.wait()
        out_bias = vec_in_ref[0:1]
        gain = vec_in_ref[1:2]
        shift = vec_in_ref[2:3]
        vec[...] = jnp.zeros_like(vec)

        def step(block, carry):
            rows = pl.ds(pl.multiple_of(block * BLOCK, BLOCK), BLOCK)
            branch = out_bias
            for half in range(2):
                mixed = [attn[half * pairs + p, rows] for p in range(pairs)]
                branch = branch + dot_nn(jnp.concatenate(mixed, axis=1), wo[half].astype(BF16))
            r1 = x[rows].astype(F32) + branch
            first[rows] = r1
            total[rows] = r1
            dwide[rows] = jnp.zeros((BLOCK, model), F32)
            normal, _ = norm_parts(r1)
            h2 = (normal * gain + shift).astype(BF16)
            tall[rows] = h2
            flip[:, rows] = h2.T
            return carry

        lax.fori_loop(0, BIN // BLOCK, step, 0)

    def hidden_half(u):
        b, half = u // 2, u % 2
        block_loads(u, False)

        @pl.when(u + 1 < 2 * groups)
        def _():
            block_loads(u + 1, True)

        span = 2 * BLOCK
        wf_low = wf[half].astype(BF16)
        wp_low = wp[half].astype(BF16)
        bias = bfc_ref[pl.ds(half * groups + b, 1), :]
        df_sum = jnp.zeros((1, CHUNK), F32)
        for block in range(BIN // span):
            rows = slice(block * span, (block + 1) * span)
            pre = dot_nn(tall[rows], wf_low) + bias
            hidden, rise = gelu_pair(pre)
            hidden = hidden.astype(BF16)
            act[rows] = hidden
            total[rows] = total[rows] + dot_nn(hidden, wp_low)
            df = (dot_nt(cot[rows], wp_low) * rise).astype(BF16)
            slope[rows] = df
            df_sum = df_sum + jnp.sum(df.astype(F32), axis=0, keepdims=True)
            dwide[rows] = dwide[rows] + dot_nt(df, wf_low)

        vec[half, pl.ds(6 + b // pieces, 1), pl.ds(pl.multiple_of((b % pieces) * CHUNK, CHUNK), CHUNK)] = df_sum
        at = jnp.where(half == 0, 2 * b, chunks + (2 * b) % SENDS)
        acc[at] = dot_tn(act[...], cot[...])
        fc = dot_nn(flip[...], slope[...])
        for n in range(pieces):
            acc[at + 1, :, n * CHUNK : (n + 1) * CHUNK] = fc[n * CHUNK : (n + 1) * CHUNK]

        @pl.when(half == 1)
        def _():
            mp_copy(2 * b).start()
            mp_copy(2 * b + 1).start()

    def put_piece(half, piece, part, value):
        n = piece // 2
        at = jnp.where(half == 0, 2 * groups + n, chunks + (2 * groups + n) % SENDS)
        rows = pl.ds(pl.multiple_of((piece % 2) * PAIR, PAIR), PAIR)
        acc[at, rows, part * width : part * width + value.shape[1]] = value

    def sum_copies():
        local = pltpu.make_async_copy(total, sum_ref.at[my_rows], igsem.at[3])
        remote = pltpu.make_async_remote_copy(
            total, sum_ref.at[my_rows], igsem.at[4], igsem.at[5],
            device_id=(dp, 1 - mp), device_id_type=MESH,
        )
        return local, remote

    def middle_back():
        for item in sum_copies():
            item.start()
        gain = vec_in_ref[1:2]
        w3_loads(jnp.int32(0), True)

        def step(block, sums):
            rows = pl.ds(pl.multiple_of(block * BLOCK, BLOCK), BLOCK)
            normal, inverse = norm_parts(first[rows])
            up = dwide[rows]
            upstream = cot[rows].astype(F32)
            dr1 = upstream + norm_back(up, normal, inverse, gain)
            first[rows] = dr1
            dwide[rows] = jnp.zeros((BLOCK, model), F32)
            da = dr1.astype(BF16)
            tall[rows] = da
            for half in range(2):
                back = dot_nt(da, wo[half].astype(BF16)).astype(BF16)
                for p in range(pairs):
                    dattn[half * pairs + p, rows] = back[:, p * PAIR : (p + 1) * PAIR]
            return tuple(
                total_row + jnp.sum(item, axis=0, keepdims=True)
                for total_row, item in zip(sums, (da.astype(F32), up * normal, up, upstream))
            )

        sums = lax.fori_loop(0, BIN // BLOCK, step, (jnp.zeros((1, model), F32),) * 4)
        for half in range(2):
            for n in range(4):
                vec[half, 2 + n : 3 + n] = sums[n]
            mixed = jnp.concatenate([attn[half * pairs + p] for p in range(pairs)], axis=1)
            grad = dot_tn(mixed, tall[...])
            for piece in range(pairs):
                put_piece(half, piece, 0, grad[piece * PAIR : (piece + 1) * PAIR])
        mp_copy(2 * groups).start()
        h1_load().start()
        for item in loads[early:]:
            item.wait()

    def attend_half(q):
        p, half = q // 2, q % 2

        @pl.when(q + 1 < 2 * pairs)
        def _():
            w3_loads(q + 1, True)

        @pl.when(q == 0)
        def _():
            h1_load().wait()
            flip[...] = tall[...].T

        attend_back_pair(half, p, qkv, dattn, lse, row_ref, dk, dv, vec, pairs)
        w3_loads(q, False)
        pair = half * pairs + p
        low = jnp.concatenate([qkv[pair, c] for c in range(3)], axis=1)
        grad = dot_nn(flip[...], low)
        for n in range(2 * pairs):
            put_piece(half, pairs * (p + 1) + n % pairs, n // pairs, grad[n * PAIR : (n + 1) * PAIR])
        weights = jnp.concatenate([w3[half, c].astype(BF16) for c in range(3)], axis=1)
        dwide[...] = dwide[...] + dot_nt(low, weights)
        for at, made in ((1, [1, 2]), (3, [3]), (5, [4, 5])):
            @pl.when(q == at)
            def _():
                for n in made:
                    mp_copy(2 * groups + n).start()

    def input_grad():
        gain = gain_ref[...].astype(F32)

        def step(block, sums):
            rows = pl.ds(pl.multiple_of(block * BLOCK, BLOCK), BLOCK)
            normal, inverse = norm_parts(x[rows].astype(F32))
            up = dwide[rows]
            first[rows] = first[rows] + norm_back(up, normal, inverse, gain)
            return (
                sums[0] + jnp.sum(up * normal, axis=0, keepdims=True),
                sums[1] + jnp.sum(up, axis=0, keepdims=True),
            )

        gain_sum, shift_sum = lax.fori_loop(0, BIN // BLOCK, step, (jnp.zeros((1, model), F32),) * 2)
        for half in range(2):
            vec[half, 0:1] = gain_sum
            vec[half, 1:2] = shift_sum

    def ig_copies():
        local = pltpu.make_async_copy(first, ig_ref.at[my_rows], igsem.at[0])
        remote = pltpu.make_async_remote_copy(
            first, ig_ref.at[my_rows], igsem.at[1], igsem.at[2],
            device_id=(dp, 1 - mp), device_id_type=MESH,
        )
        return local, remote

    def vec_copy(n):
        if n == 0:
            src, device = vec.at[1], (dp, 1 - mp)
        else:
            src, device = vec.at[0], (partner[n - 1], mp)
        return pltpu.make_async_remote_copy(
            src, vrecv.at[n], vsem.at[0, n], vsem.at[1, n], device_id=device, device_id_type=MESH
        )

    begin_layer()

    def tick(t, carry):
        ring_tick(t)

        @pl.when(t < middle_tick)
        def _():
            hidden_half(t)

        @pl.when(t == middle_tick)
        def _():
            middle_back()

        @pl.when((t >= attend_tick) & (t < input_tick))
        def _():
            attend_half(t - attend_tick)

        @pl.when(t == input_tick)
        def _():
            input_grad()
            for item in ig_copies():
                item.start()
            vec_copy(0).start()

        for n in range(bits + 1):
            @pl.when(t == input_tick + 1 + n)
            def _():
                vec_copy(n).wait()
                vec[0] = vec[0] + vrecv[n]
                if n < bits:
                    vec_copy(n + 1).start()

        c, valid = at_stage(t, offsets[stages] + 1)

        @pl.when(valid)
        def _():
            write(c, False)

        return carry

    lax.fori_loop(0, ticks, tick, 0)
    for item in ig_copies() + sum_copies():
        item.wait()
    vo_ref[...] = vec[0]


def back(bits, arrays, row, gain, vec_in, bfc, sizes):
    pairs, hidden, model = sizes
    width = pairs * PAIR
    groups = hidden // CHUNK
    chunks = 3 * groups
    plans = color_plans(bits, 0)
    stages = len(plans[0])
    recv = [
        [pltpu.VMEM((SLOTS, size, model // 3), F32) for _, size, kind in plan if kind < 2]
        for plan in plans
    ]
    here = pl.BlockSpec(memory_space=pl.ANY)
    vmem = pl.BlockSpec(memory_space=pltpu.VMEM)
    dma = pltpu.SemaphoreType.DMA
    return pl.pallas_call(
        functools.partial(back_kernel, bits, groups),
        out_shape=[
            jax.ShapeDtypeStruct((hidden, model), F32),
            jax.ShapeDtypeStruct((model, hidden), F32),
            jax.ShapeDtypeStruct((width, model), F32),
            jax.ShapeDtypeStruct((3, model, width), F32),
            jax.ShapeDtypeStruct((2 * BIN, model), F32),
            jax.ShapeDtypeStruct((2 * BIN, model), F32),
            jax.ShapeDtypeStruct((16, model), F32),
        ],
        in_specs=[here] * len(arrays) + [vmem] * 4,
        out_specs=[here] * 6 + [vmem],
        scratch_shapes=[
            pltpu.VMEM((chunks + SENDS, CHUNK, model), F32),
            pltpu.VMEM((LANDS, CHUNK, model), F32),
            recv,
            pltpu.VMEM((2 * pairs, 3, BIN, PAIR), BF16),
            pltpu.VMEM((2 * pairs, BIN, PAIR), BF16),
            pltpu.VMEM((2 * pairs, BIN, PAIR), BF16),
            pltpu.VMEM((BIN, model), BF16),
            pltpu.VMEM((BIN, model), BF16),
            pltpu.VMEM((BIN, model), BF16),
            pltpu.VMEM((model, BIN), BF16),
            pltpu.VMEM((BIN, model), F32),
            pltpu.VMEM((BIN, model), F32),
            pltpu.VMEM((BIN, model), F32),
            pltpu.VMEM((2, model, CHUNK), F32),
            pltpu.VMEM((2, CHUNK, model), F32),
            pltpu.VMEM((2, width, model), F32),
            pltpu.VMEM((2, 3, model, PAIR), F32),
            pltpu.VMEM((BIN, CHUNK), BF16),
            pltpu.VMEM((BIN, CHUNK), BF16),
            pltpu.VMEM((2 * pairs, 8, BIN), F32),
            pltpu.VMEM((BIN, PAIR), F32),
            pltpu.VMEM((BIN, PAIR), F32),
            pltpu.VMEM((2, 16, model), F32),
            pltpu.VMEM((bits + 1, 16, model), F32),
            dma((SLOTS, 3, stages)),
            dma((SLOTS, 3, stages)),
            dma((LANDS,)),
            dma((LANDS,)),
            dma((SLOTS, 12)),
            dma((10,)),
            dma((2, 2)),
            dma((2, 3)),
            dma((6,)),
            dma((2, bits + 1)),
        ],
        compiler_params=pltpu.CompilerParams(
            collective_id=0, has_side_effects=True, vmem_limit_bytes=67_043_328
        ),
        name="back",
    )(*arrays, row, gain, vec_in, bfc)


def on_device(
    tokens, segments, lengths, ln1_gain, ln1_bias, w_qkv, b_qv, w_out, out_bias,
    ln2_gain, ln2_bias, w_fc, b_fc, w_proj, proj_bias, cotangent,
):
    model = tokens.shape[1]
    width = w_qkv.shape[2]
    hidden = w_fc.shape[1]
    pairs = width // PAIR
    groups = lax.axis_size("dp")
    bits = groups.bit_length() - 1
    if lax.axis_size("mp") != 2 or groups != 1 << bits or tokens.shape[0] != 2 * BIN:
        raise ValueError("unsupported mesh")
    side = lax.axis_index("mp")
    mine = side.astype(jnp.int32).reshape(1)
    swap = [(0, 1), (1, 0)]

    def cross(value):
        return lax.ppermute(value, "mp", swap)

    w3 = jnp.transpose(w_qkv, (1, 0, 2)).astype(F32)
    small = jnp.concatenate([b_qv.reshape(-1), b_fc]).astype(F32)
    small_other = cross(small)
    w3_other = cross(w3)
    wo_own, wf_own, wp_own = (item.astype(F32) for item in (w_out, w_fc, w_proj))
    wo_other = cross(wo_own)
    wf_other = cross(wf_own)
    wp_other = cross(wp_own)

    def qkv_bias(flat):
        return jnp.stack([flat[:width], jnp.zeros((width,), F32), flat[width : 2 * width]])

    own, other_front = front(
        mine, tokens, segments.reshape(2, BIN), lengths,
        ln1_gain.reshape(1, -1), ln1_bias.reshape(1, -1), w3, qkv_bias(small), width,
    )
    qkv_own, attn_own, lse_own, h1, start, row = own
    small_other, w3_other, h1 = lax.optimization_barrier((small_other, w3_other, h1))
    qkv_other, attn_other, lse_other = other_front(h1, start, w3_other, qkv_bias(small_other))
    vec_in = jnp.stack([out_bias, ln2_gain, ln2_bias, proj_bias]).astype(F32)
    bfc = jnp.concatenate([small[2 * width :], small_other[2 * width :]]).reshape(-1, CHUNK)
    arrays = (
        qkv_own, qkv_other, attn_own, attn_other, h1, w3, w3_other, tokens, cotangent,
        wo_own, wo_other, wf_own, wf_other, wp_own, wp_other, lse_own, lse_other,
    )
    grad_proj, grad_fc, grad_out, grad_qkv, input_grad, block_sum, rows = back(
        bits, arrays, row, ln1_gain.reshape(1, -1), vec_in, bfc, (pairs, hidden, model)
    )
    block_out = (block_sum + vec_in[3]).astype(BF16)
    grad_qkv = jnp.transpose(grad_qkv, (1, 0, 2))
    return (
        block_out,
        input_grad,
        rows[0],
        rows[1],
        grad_qkv,
        rows[8].reshape(2, width),
        grad_out,
        rows[2],
        rows[3],
        rows[4],
        grad_fc,
        rows[6:8].reshape(-1),
        grad_proj,
        rows[5],
    )


def solution(mesh):
    rows = P("dp", None)
    placed = (
        rows, P("dp"), rows, P(), P(), P(None, None, "mp"), P(None, "mp"), P("mp", None), P(),
        P(), P(), P(None, "mp"), P("mp"), P("mp", None), P(), rows,
    )
    results = (
        rows, rows, P(), P(), P(None, None, "mp"), P(None, "mp"), P("mp", None), P(), P(), P(),
        P(None, "mp"), P("mp"), P("mp", None), P(),
    )
    return jax.shard_map(
        on_device, mesh=mesh, in_specs=placed, out_specs=results, check_vma=False
    )
```

```python
import functools

import jax
import jax.numpy as jnp
from jax import lax
from jax.experimental import pallas as pl
from jax.experimental.pallas import tpu as pltpu
from jax.sharding import PartitionSpec as P

HEAD_DIM = 64
BIN = 1024
PAIR = 2 * HEAD_DIM
BLOCK = 256
CHUNK = 256
SLOTS = 4
SENDS = 4
LANDS = 5
QV_ROW = 6
FC_ROW = 7

epsilon = 1e-05
gelu_scale = 0.7978845608028654
gelu_cubic = 0.044715
score_scale = 0.125
masked_score = -1e30

MESH = pl.DeviceIdType.MESH
F32 = jnp.float32
BF16 = jnp.bfloat16
VMEM_LIMIT = 64_000_000


def dot_nn(left, right):
    return lax.dot_general(left, right, (((1,), (0,)), ((), ())), preferred_element_type=F32)


def dot_nt(left, right):
    return lax.dot_general(left, right, (((1,), (1,)), ((), ())), preferred_element_type=F32)


def dot_tn(left, right):
    return lax.dot_general(left, right, (((0,), (0,)), ((), ())), preferred_element_type=F32)


def norm_parts(values):
    center = values - jnp.mean(values, axis=-1, keepdims=True)
    inverse = lax.rsqrt(jnp.mean(center * center, axis=-1, keepdims=True) + epsilon)
    return center * inverse, inverse


def norm_back(upstream, normal, inverse, gain):
    scaled = upstream * gain
    centered = scaled - jnp.mean(scaled, axis=-1, keepdims=True)
    return inverse * (centered - normal * jnp.mean(scaled * normal, axis=-1, keepdims=True))


def gelu_pair(values):
    square = values * values
    tangent = jnp.tanh(gelu_scale * (values + gelu_cubic * square * values))
    half = 0.5 * (1.0 + tangent)
    slope = half + 0.5 * values * (1.0 - tangent * tangent) * (
        gelu_scale + 3.0 * gelu_cubic * gelu_scale * square
    )
    return values * half, slope


def column_to_row(column):
    rows = column.shape[0]
    return jnp.broadcast_to(column, (rows, 128)).T[0:1]


def head_mask(head, scale):
    lane = lax.broadcasted_iota(jnp.int32, (1, PAIR), 1)
    return jnp.where(lane // HEAD_DIM == head, scale, 0.0).astype(BF16)


def attend_pair(qkv_ref, start_ref, attn_ref, lse_ref):
    lane = lax.broadcasted_iota(jnp.int32, (1, PAIR), 1)
    for block in range(BIN // BLOCK):
        rows = slice(block * BLOCK, (block + 1) * BLOCK)
        seen = (block + 1) * BLOCK
        queries = qkv_ref[0, 0, rows]
        key_rows = qkv_ref[0, 1, 0:seen]
        value_rows = qkv_ref[0, 2, 0:seen]
        j = lax.broadcasted_iota(jnp.int32, (BLOCK, seen), 1)
        i = lax.broadcasted_iota(jnp.int32, (BLOCK, seen), 0) + block * BLOCK
        visible = (j >= start_ref[rows]) & (j <= i)
        mixed = []
        for head in range(2):
            scores = dot_nt(queries * head_mask(head, score_scale), key_rows)
            scores = jnp.where(visible, scores, masked_score)
            highest = jnp.max(scores, axis=-1, keepdims=True)
            weights = jnp.exp(scores - highest)
            totals = jnp.sum(weights, axis=-1, keepdims=True)
            mixed.append(dot_nn(weights.astype(BF16), value_rows) / totals)
            lse_ref[0, head : head + 1, rows] = column_to_row(highest + jnp.log(totals))
        attn_ref[0, rows] = jnp.where(lane < HEAD_DIM, mixed[0], mixed[1]).astype(BF16)


def project_and_attend(h1, w_ref, pack_ref, start_ref, qkv_ref, attn_ref, lse_ref):
    width = pl.num_programs(0) * PAIR
    place = pl.program_id(0) * PAIR
    for c in range(3):
        out = dot_nn(h1, w_ref[c].astype(BF16))
        if c != 1:
            at = place if c == 0 else width + place
            out = out + pack_ref[QV_ROW : QV_ROW + 1, pl.ds(pl.multiple_of(at, PAIR), PAIR)]
        qkv_ref[0, c] = out.astype(BF16)
    attend_pair(qkv_ref, start_ref, attn_ref, lse_ref)


def own_front_kernel(
    mp_ref, x_ref, seg_ref, len_ref, pack_ref, w_ref,
    qkv_ref, attn_ref, lse_ref, h1_ref, start_ref, row_ref,
):
    @pl.when(pl.program_id(0) == 0)
    def _():
        gain = pack_ref[0:1]
        shift = pack_ref[1:2]
        for block in range(BIN // BLOCK):
            rows = slice(block * BLOCK, (block + 1) * BLOCK)
            normal, _ = norm_parts(x_ref[rows].astype(F32))
            h1_ref[rows] = (normal * gain + shift).astype(BF16)
        mine = mp_ref[0]
        count = len_ref.shape[1]
        seg = seg_ref[pl.ds(mine, 1), :].astype(F32)
        seg = jnp.broadcast_to(seg, (128, BIN)).T
        seg = seg[:, :count]
        label = lax.broadcasted_iota(jnp.int32, (BIN, count), 1).astype(F32)
        sizes = len_ref[pl.ds(mine, 1), :].astype(F32)
        start = jnp.sum(jnp.where(label < seg, sizes, 0.0), axis=1, keepdims=True)
        rows_of = jnp.sum(jnp.where(label == seg, 1.0, 0.0), axis=0, keepdims=True)
        first = jnp.sum(jnp.where(label < seg, rows_of, 0.0), axis=1, keepdims=True)
        start = jnp.maximum(start, first)
        start_ref[...] = start.astype(jnp.int32)
        row_ref[...] = column_to_row(start).astype(jnp.int32)

    project_and_attend(h1_ref[...], w_ref, pack_ref, start_ref, qkv_ref, attn_ref, lse_ref)


def other_front_kernel(h1_ref, start_ref, pack_ref, w_ref, qkv_ref, attn_ref, lse_ref):
    project_and_attend(h1_ref[...], w_ref, pack_ref, start_ref, qkv_ref, attn_ref, lse_ref)


def fixed(shape):
    return pl.BlockSpec(shape, lambda *_: (0,) * len(shape), pipeline_mode=pl.Buffered(1))


def front(mine, x, seg, lens, pack, w_own, width):
    model = x.shape[1]
    pairs = width // PAIR
    per_pair = [pl.BlockSpec((3, model, PAIR), lambda p, *_: (0, 0, p))]
    outs = [
        pl.BlockSpec((1, 3, BIN, PAIR), lambda p, *_: (p, 0, 0, 0)),
        pl.BlockSpec((1, BIN, PAIR), lambda p, *_: (p, 0, 0)),
        pl.BlockSpec((1, 8, BIN), lambda p, *_: (p, 0, 0)),
    ]
    out_shapes = [
        jax.ShapeDtypeStruct((pairs, 3, BIN, PAIR), BF16),
        jax.ShapeDtypeStruct((pairs, BIN, PAIR), BF16),
        jax.ShapeDtypeStruct((pairs, 8, BIN), F32),
    ]
    cost = pl.CostEstimate(flops=6_000_000_000, bytes_accessed=10_000_000, transcendentals=0)
    params = pltpu.CompilerParams(vmem_limit_bytes=VMEM_LIMIT)
    own = pl.pallas_call(
        own_front_kernel,
        out_shape=out_shapes
        + [
            jax.ShapeDtypeStruct((BIN, model), BF16),
            jax.ShapeDtypeStruct((BIN, 1), jnp.int32),
            jax.ShapeDtypeStruct((1, BIN), jnp.int32),
        ],
        grid_spec=pltpu.PrefetchScalarGridSpec(
            num_scalar_prefetch=1,
            grid=(pairs,),
            in_specs=[
                pl.BlockSpec((BIN, model), lambda p, m: (m[0], 0)),
                fixed(seg.shape), fixed(lens.shape), fixed(pack.shape),
            ]
            + per_pair,
            out_specs=outs
            + [
                pl.BlockSpec((BIN, model), lambda p, *_: (0, 0)),
                pl.BlockSpec((BIN, 1), lambda p, *_: (0, 0)),
                pl.BlockSpec((1, BIN), lambda p, *_: (0, 0)),
            ],
        ),
        compiler_params=params,
        cost_estimate=cost,
        name="own_front",
    )

    def other(h1, start, pack_other, w_other):
        return pl.pallas_call(
            other_front_kernel,
            out_shape=out_shapes,
            grid=(pairs,),
            in_specs=[fixed((BIN, model)), fixed((BIN, 1)), fixed(pack.shape)] + per_pair,
            out_specs=outs,
            compiler_params=params,
            cost_estimate=cost,
            name="other_front",
        )(h1, start, pack_other, w_other)

    return own(mine, x, seg, lens, pack, w_own), other


def halving_plan(order, rows):
    first, back = [], []
    size = rows
    for n, bit in enumerate(order):
        if n < len(order) - 1 and size % 16 == 0:
            size //= 2
            first.append((bit, size, 0))
            back.append((bit, size, 2))
        else:
            first.append((bit, size, 1))
    return first + back[::-1]


def color_orders(bits, odd):
    plain = list(range(bits))
    orders = [plain, plain, plain]
    if bits > 1:
        orders[1] = [1, 0] + plain[2:]
    if bits > 2:
        orders[2] = [2, 1, 0] + plain[3:] if odd else [2, 0, 1] + plain[3:]
    return orders


def color_plans(bits, odd):
    return [halving_plan(order, CHUNK) for order in color_orders(bits, odd)]


def attend_back_pair(half, place, qkv, dattn, lse_ref, row_ref, dk, dv, vec, pairs):
    dk[...] = jnp.zeros_like(dk)
    dv[...] = jnp.zeros_like(dv)
    pair = half * pairs + place
    dq_sum = jnp.zeros((1, PAIR), F32)
    for block in range(BIN // BLOCK):
        rows = slice(block * BLOCK, (block + 1) * BLOCK)
        seen = (block + 1) * BLOCK
        queries = qkv[pair, 0, rows]
        upstream = dattn[pair, rows]
        key_rows = qkv[pair, 1, 0:seen]
        value_rows = qkv[pair, 2, 0:seen]
        j = lax.broadcasted_iota(jnp.int32, (seen, BLOCK), 0)
        i = lax.broadcasted_iota(jnp.int32, (seen, BLOCK), 1) + block * BLOCK
        visible = (j >= row_ref[0:1, rows]) & (j <= i)
        dq = jnp.zeros((BLOCK, PAIR), F32)
        for head in range(2):
            masked_q = queries * head_mask(head, score_scale)
            masked_up = upstream * head_mask(head, 1.0)
            scores = dot_nt(key_rows, masked_q)
            probs = jnp.exp(scores - lse_ref[pair, head : head + 1, rows])
            probs = jnp.where(visible, probs, 0.0)
            dprobs = dot_nt(value_rows, masked_up)
            inner = jnp.sum(probs * dprobs, axis=0, keepdims=True)
            dscores = (probs * (dprobs - inner)).astype(BF16)
            dv[0:seen] = dv[0:seen] + dot_nn(probs.astype(BF16), masked_up)
            dk[0:seen] = dk[0:seen] + dot_nn(dscores, masked_q)
            dq = dq + dot_tn(dscores, key_rows * head_mask(head, 1.0))
        dq = (dq * score_scale).astype(BF16)
        qkv[pair, 0, rows] = dq
        dq_sum = dq_sum + jnp.sum(dq.astype(F32), axis=0, keepdims=True)
    dv_low = dv[...].astype(BF16)
    qkv[pair, 1] = dk[...].astype(BF16)
    qkv[pair, 2] = dv_low
    dv_sum = jnp.sum(dv_low.astype(F32), axis=0, keepdims=True)
    width = pairs * PAIR
    vec[half, 8:9, pl.ds(pl.multiple_of(place * PAIR, PAIR), PAIR)] = dq_sum
    vec[half, 8:9, pl.ds(pl.multiple_of(width + place * PAIR, PAIR), PAIR)] = dv_sum


def back_kernel(
    bits, groups,
    qkv_own_ref, qkv_other_ref, attn_own_ref, attn_other_ref, h1_ref, w3_own_ref, w3_other_ref,
    x_ref, cot_ref, wo_own_ref, wo_other_ref, wf_ref, wp_ref,
    lse_own_ref, lse_other_ref, row_ref, pack_ref, pack_other_ref,
    op_ref, of_ref, oa_ref, oq_ref, ig_ref, bo_ref, sum_ref, vo_ref,
    acc, mpbuf, rbufs, qkv, dattn, attn, cot, x, tall, flip, total, dwide, first,
    wf, wp, wf_low, wp_low, wf_out, wp_out, wo, w3, act, slope, lse, dk, dv, vec, vrecv,
    ssem, rsem, mps, mpr, wsem, lsem, bsem, wsend, wrecv, hsem, igsem, vsem,
):
    dp = lax.axis_index("dp")
    mp = lax.axis_index("mp")
    chunks = 3 * groups
    own_bits = [(dp // (1 << b)) % 2 for b in range(bits)]
    partner = [dp + (1 - 2 * own_bits[b]) * (1 << b) for b in range(bits)]
    plans = [color_plans(bits, odd) for odd in range(2)]
    stages = len(plans[0][0])
    flights = [2] + [1] * (stages - 2) + [2]
    offsets = [sum(flights[:s]) for s in range(stages + 1)]
    pairs = qkv_own_ref.shape[0]
    model = x_ref.shape[1]
    width = pairs * PAIR
    pieces = model // CHUNK

    my_rows = pl.ds(pl.multiple_of(mp * BIN, BIN), BIN)
    far_rows = pl.ds(pl.multiple_of((1 - mp) * BIN, BIN), BIN)
    loads = []

    def load(src, dst):
        loads.append(pltpu.make_async_copy(src, dst, lsem.at[len(loads)]))

    load(attn_own_ref, attn.at[0:pairs])
    load(attn_other_ref, attn.at[pairs : 2 * pairs])
    load(wo_own_ref, wo.at[0])
    load(wo_other_ref, wo.at[1])
    load(x_ref.at[my_rows], x)
    early = len(loads)
    load(cot_ref.at[my_rows], cot)
    load(qkv_own_ref, qkv.at[0:pairs])
    load(qkv_other_ref, qkv.at[pairs : 2 * pairs])
    load(lse_own_ref, lse.at[0:pairs])
    load(lse_other_ref, lse.at[pairs : 2 * pairs])

    def block_loads(b):
        slot = b % 2
        at = pl.ds(pl.multiple_of(b * CHUNK, CHUNK), CHUNK)
        return [
            pltpu.make_async_copy(wf_ref.at[:, at], wf_low.at[slot], bsem.at[slot, 0]),
            pltpu.make_async_copy(wp_ref.at[at], wp_low.at[slot], bsem.at[slot, 1]),
        ]

    def block_sends(b):
        slot = b % 2
        return [
            pltpu.make_async_remote_copy(
                src, dst.at[slot], wsend.at[n], wrecv.at[slot, n],
                device_id=(dp, 1 - mp), device_id_type=MESH,
            )
            for n, (src, dst) in enumerate(((wf_out, wf), (wp_out, wp)))
        ]

    def send_block(b):
        for item in block_loads(b):
            item.wait()
        wf_out[...] = wf_low[b % 2].astype(F32)
        wp_out[...] = wp_low[b % 2].astype(F32)
        for item in block_sends(b):
            item.start()

    def w3_loads(q, begin):
        slot = q % 2
        at = pl.ds(pl.multiple_of((q // 2) * PAIR, PAIR), PAIR)
        for half, ref in ((0, w3_own_ref), (1, w3_other_ref)):
            @pl.when(slot == half)
            def _():
                for c in range(3):
                    item = pltpu.make_async_copy(ref.at[c, :, at], w3.at[half, c], hsem.at[half, c])
                    item.start() if begin else item.wait()

    def h1_load():
        return pltpu.make_async_copy(h1_ref, tall, lsem.at[9])

    for item in loads:
        item.start()
    for b in range(2):
        for item in block_loads(b):
            item.start()

    barrier = pltpu.get_barrier_semaphore()
    for b in range(bits):
        pl.semaphore_signal(barrier, inc=1, device_id=(partner[b], mp), device_id_type=MESH)
    pl.semaphore_signal(barrier, inc=1, device_id=(dp, 1 - mp), device_id_type=MESH)
    pl.semaphore_wait(barrier, bits + 1)

    def walk(plan):
        base, found = 0, []
        for bit, size, kind in plan:
            found.append(base)
            if kind == 0:
                base = base + own_bits[bit] * size
            if kind == 2:
                base = base - own_bits[bit] * size
        return found

    starts = [[walk(plan) for plan in plans[odd]] for odd in range(2)]

    def place(c, color, s):
        sides = []
        for odd in range(2):
            bit, size, kind = plans[odd][color][s]
            sides.append((starts[odd][color][s], own_bits[bit], partner[bit]))
        if plans[0][color] == plans[1][color]:
            return sides[0]
        return [jnp.where(c % 2 == 0, even, odd) for even, odd in zip(*sides)]

    def lanes(color):
        share = model // 3
        return slice(color * share, (color + 1) * share)

    def copy(c, color, s):
        _, size, kind = plans[0][color][s]
        slot = c % SLOTS
        base, side, device = place(c, color, s)
        if kind == 0:
            base = base + (1 - side) * size
        src = acc.at[c, pl.ds(pl.multiple_of(base, 8), size), lanes(color)]
        dst = src if kind == 2 else rbufs[color][s].at[slot]
        return pltpu.make_async_remote_copy(
            src, dst, ssem.at[slot, color, s], rsem.at[slot, color, s],
            device_id=(device, mp), device_id_type=MESH,
        )

    def finish(c, color, s):
        _, size, kind = plans[0][color][s]
        copy(c, color, s).wait()
        if kind == 2:
            return
        base, side, _ = place(c, color, s)
        if kind == 0:
            base = base + side * size
        rows = pl.ds(pl.multiple_of(base, 8), size)
        acc[c, rows, lanes(color)] = acc[c, rows, lanes(color)] + rbufs[color][s][c % SLOTS]

    def mp_copy(c):
        slot, land = c % SENDS, c % LANDS
        return pltpu.make_async_remote_copy(
            acc.at[chunks + slot], mpbuf.at[land], mps.at[land], mpr.at[land],
            device_id=(dp, 1 - mp), device_id_type=MESH,
        )

    def mp_finish(c):
        mp_copy(c).wait()
        acc[c] = acc[c] + mpbuf[c % LANDS]

    def chunk_rows(n):
        return pl.ds(pl.multiple_of(n * CHUNK, CHUNK), CHUNK)

    def whole_copy(dst, c):
        return pltpu.make_async_copy(acc.at[c], dst, wsem.at[c % SLOTS, 0])

    def piece_copies(c):
        at = chunk_rows(c // 2)
        return [
            pltpu.make_async_copy(
                acc.at[c, :, n * CHUNK : (n + 1) * CHUNK],
                of_ref.at[n * CHUNK : (n + 1) * CHUNK, at],
                wsem.at[c % SLOTS, n],
            )
            for n in range(pieces)
        ]

    def write(c, begin):
        @pl.when((c < 2 * groups) & (c % 2 == 0))
        def _():
            item = whole_copy(op_ref.at[chunk_rows(c // 2)], c)
            item.start() if begin else item.wait()

        @pl.when((c < 2 * groups) & (c % 2 == 1))
        def _():
            for item in piece_copies(c):
                item.start() if begin else item.wait()

        for part in range(2):
            piece = 2 * (c - 2 * groups) + part
            rows = slice(part * PAIR, (part + 1) * PAIR)

            @pl.when((c >= 2 * groups) & (piece < pairs))
            def _():
                at = pl.ds(pl.multiple_of(piece * PAIR, PAIR), PAIR)
                item = pltpu.make_async_copy(acc.at[c, rows], oa_ref.at[at], wsem.at[c % SLOTS, 6 * part])
                item.start() if begin else item.wait()

            @pl.when((c >= 2 * groups) & (piece >= pairs))
            def _():
                across = pl.ds(pl.multiple_of((piece // pairs - 1) * PAIR, PAIR), PAIR)
                for n in range(6):
                    down = pl.ds(pl.multiple_of((n // 3) * width + (piece % pairs) * PAIR, PAIR), PAIR)
                    item = pltpu.make_async_copy(
                        acc.at[c, rows, n * PAIR : (n + 1) * PAIR],
                        oq_ref.at[n % 3, down, across],
                        wsem.at[c % SLOTS, 6 * part + n],
                    )
                    item.start() if begin else item.wait()

    middle_tick = 2 * groups
    attend_tick = middle_tick + 1
    input_tick = attend_tick + 2 * pairs
    late = chunks - 4
    late_tick = late + 4
    arrivals = [(middle_tick + 2, [0]), (middle_tick + 4, [1, 2]), (middle_tick + 6, [3]), (middle_tick + 8, [4, 5])]
    ticks = chunks + 4 + offsets[stages] + 1

    def at_stage(t, shift):
        since = t - shift
        early = (since >= 3) & (since < late + 3)
        last = (since >= late_tick) & (since < chunks + 4)
        c = jnp.where(since < late_tick, since - 3, since - late_tick + late)
        return jnp.clip(c, 0, chunks - 1), early | last

    def ring_tick(t):
        @pl.when((t >= 3) & (t % 2 == 1) & (t < middle_tick + 3))
        def _():
            mp_finish(t - 3)
            mp_finish(t - 2)

        for at, made in arrivals:
            @pl.when(t == at)
            def _():
                for n in made:
                    mp_finish(2 * groups + n)

        for s in range(stages):
            c, valid = at_stage(t, offsets[s + 1])

            @pl.when(valid)
            def _():
                for color in range(3):
                    finish(c, color, s)

        for s in list(range(stages)) + [-1]:
            c, valid = at_stage(t, offsets[s + 1])

            @pl.when(valid)
            def _():
                if s + 1 == stages:
                    write(c, True)
                else:
                    for color in range(3):
                        copy(c, color, s + 1).start()

    def begin_layer():
        send_block(0)
        for item in loads[:early]:
            item.wait()
        out_bias = pack_ref[2:3]
        gain = pack_ref[3:4]
        shift = pack_ref[4:5]
        proj_bias = pack_ref[5:6]
        vec[...] = jnp.zeros_like(vec)

        def step(block, carry):
            rows = pl.ds(pl.multiple_of(block * BLOCK, BLOCK), BLOCK)
            branch = out_bias
            for half in range(2):
                mixed = [attn[half * pairs + p, rows] for p in range(pairs)]
                branch = branch + dot_nn(jnp.concatenate(mixed, axis=1), wo[half].astype(BF16))
            r1 = x[rows].astype(F32) + branch
            first[rows] = r1
            total[rows] = r1 + proj_bias
            dwide[rows] = jnp.zeros((BLOCK, model), F32)
            normal, _ = norm_parts(r1)
            h2 = (normal * gain + shift).astype(BF16)
            tall[rows] = h2
            flip[:, rows] = h2.T
            return carry

        lax.fori_loop(0, BIN // BLOCK, step, 0)
        loads[early].wait()

    def hidden_half(u):
        b, half = u // 2, u % 2

        @pl.when(half == 1)
        def _():
            for item in block_sends(b):
                item.wait()

            @pl.when(b + 1 < groups)
            def _():
                send_block(b + 1)

            @pl.when(b + 2 < groups)
            def _():
                for item in block_loads(b + 2):
                    item.start()

            wf_low[2] = wf[b % 2].astype(BF16)
            wp_low[2] = wp[b % 2].astype(BF16)

        span = 2 * BLOCK
        place = jnp.where(half == 0, b % 2, 2)
        fc = wf_low[place]
        proj = wp_low[place]
        at = pl.ds(FC_ROW + b // pieces, 1), pl.ds(pl.multiple_of((b % pieces) * CHUNK, CHUNK), CHUNK)
        bias = jnp.where(half == 0, pack_ref[at], pack_other_ref[at])
        df_sum = jnp.zeros((1, CHUNK), F32)
        for block in range(BIN // span):
            rows = slice(block * span, (block + 1) * span)
            pre = dot_nn(tall[rows], fc) + bias
            hidden, rise = gelu_pair(pre)
            hidden = hidden.astype(BF16)
            act[rows] = hidden
            total[rows] = total[rows] + dot_nn(hidden, proj)
            df = (dot_nt(cot[rows], proj) * rise).astype(BF16)
            slope[rows] = df
            df_sum = df_sum + jnp.sum(df.astype(F32), axis=0, keepdims=True)
            dwide[rows] = dwide[rows] + dot_nt(df, fc)

        vec[half, pl.ds(6 + b // pieces, 1), pl.ds(pl.multiple_of((b % pieces) * CHUNK, CHUNK), CHUNK)] = df_sum
        at = jnp.where(half == 0, 2 * b, chunks + (2 * b) % SENDS)
        acc[at] = dot_tn(act[...], cot[...])
        grad = dot_nn(flip[...], slope[...])
        for n in range(pieces):
            acc[at + 1, :, n * CHUNK : (n + 1) * CHUNK] = grad[n * CHUNK : (n + 1) * CHUNK]

        @pl.when(half == 1)
        def _():
            mp_copy(2 * b).start()
            mp_copy(2 * b + 1).start()

    def put_piece(half, piece, part, value):
        n = piece // 2
        at = jnp.where(half == 0, 2 * groups + n, chunks + (2 * groups + n) % SENDS)
        rows = pl.ds(pl.multiple_of((piece % 2) * PAIR, PAIR), PAIR)
        acc[at, rows, part * width : part * width + value.shape[1]] = value

    def sum_copy():
        return pltpu.make_async_remote_copy(
            total, sum_ref, igsem.at[3], igsem.at[4],
            device_id=(dp, 1 - mp), device_id_type=MESH,
        )

    def sum_loads(part):
        return [
            pltpu.make_async_copy(
                sum_ref.at[(2 * part + n) * CHUNK : (2 * part + n + 1) * CHUNK], wp.at[n], igsem.at[5 + n]
            )
            for n in range(2)
        ]

    def round_far(part):
        for n, item in enumerate(sum_loads(part)):
            item.wait()
            cot[(2 * part + n) * CHUNK : (2 * part + n + 1) * CHUNK] = wp[n].astype(BF16)

    def out_copy(n):
        src, rows = ((tall, my_rows), (cot, far_rows))[n]
        return pltpu.make_async_copy(src, bo_ref.at[rows], igsem.at[7 + n])

    def middle_back():
        sum_copy().start()
        gain = pack_ref[3:4]
        w3_loads(jnp.int32(0), True)

        def step(block, sums):
            rows = pl.ds(pl.multiple_of(block * BLOCK, BLOCK), BLOCK)
            normal, inverse = norm_parts(first[rows])
            up = dwide[rows]
            upstream = cot[rows].astype(F32)
            dr1 = upstream + norm_back(up, normal, inverse, gain)
            first[rows] = dr1
            dwide[rows] = jnp.zeros((BLOCK, model), F32)
            da = dr1.astype(BF16)
            tall[rows] = da
            for half in range(2):
                back = dot_nt(da, wo[half].astype(BF16)).astype(BF16)
                for p in range(pairs):
                    dattn[half * pairs + p, rows] = back[:, p * PAIR : (p + 1) * PAIR]
            return tuple(
                total_row + jnp.sum(item, axis=0, keepdims=True)
                for total_row, item in zip(sums, (da.astype(F32), up * normal, up, upstream))
            )

        sums = lax.fori_loop(0, BIN // BLOCK, step, (jnp.zeros((1, model), F32),) * 4)
        for half in range(2):
            for n in range(4):
                vec[half, 2 + n : 3 + n] = sums[n]
            mixed = jnp.concatenate([attn[half * pairs + p] for p in range(pairs)], axis=1)
            grad = dot_tn(mixed, tall[...])
            for piece in range(pairs):
                put_piece(half, piece, 0, grad[piece * PAIR : (piece + 1) * PAIR])
        mp_copy(2 * groups).start()
        h1_load().start()
        for item in loads[early + 1 :]:
            item.wait()

    def attend_half(q):
        p, half = q // 2, q % 2

        @pl.when(q + 1 < 2 * pairs)
        def _():
            w3_loads(q + 1, True)

        @pl.when(q == 0)
        def _():
            h1_load().wait()
            flip[...] = tall[...].T

        attend_back_pair(half, p, qkv, dattn, lse, row_ref, dk, dv, vec, pairs)
        w3_loads(q, False)
        pair = half * pairs + p
        low = jnp.concatenate([qkv[pair, c] for c in range(3)], axis=1)
        grad = dot_nn(flip[...], low)
        for n in range(2 * pairs):
            put_piece(half, pairs * (p + 1) + n % pairs, n // pairs, grad[n * PAIR : (n + 1) * PAIR])
        weights = jnp.concatenate([w3[half, c].astype(BF16) for c in range(3)], axis=1)
        dwide[...] = dwide[...] + dot_nt(low, weights)
        for at, made in ((1, [1, 2]), (3, [3]), (5, [4, 5])):
            @pl.when(q == at)
            def _():
                for n in made:
                    mp_copy(2 * groups + n).start()

    def input_grad():
        gain = pack_ref[0:1]

        def step(block, sums):
            rows = pl.ds(pl.multiple_of(block * BLOCK, BLOCK), BLOCK)
            normal, inverse = norm_parts(x[rows].astype(F32))
            up = dwide[rows]
            first[rows] = first[rows] + norm_back(up, normal, inverse, gain)
            return (
                sums[0] + jnp.sum(up * normal, axis=0, keepdims=True),
                sums[1] + jnp.sum(up, axis=0, keepdims=True),
            )

        gain_sum, shift_sum = lax.fori_loop(0, BIN // BLOCK, step, (jnp.zeros((1, model), F32),) * 2)
        for half in range(2):
            vec[half, 0:1] = gain_sum
            vec[half, 1:2] = shift_sum

    def ig_copies():
        local = pltpu.make_async_copy(first, ig_ref.at[my_rows], igsem.at[0])
        remote = pltpu.make_async_remote_copy(
            first, ig_ref.at[my_rows], igsem.at[1], igsem.at[2],
            device_id=(dp, 1 - mp), device_id_type=MESH,
        )
        return local, remote

    def vec_copy(n):
        if n == 0:
            src, device = vec.at[1], (dp, 1 - mp)
        else:
            src, device = vec.at[0], (partner[n - 1], mp)
        return pltpu.make_async_remote_copy(
            src, vrecv.at[n], vsem.at[0, n], vsem.at[1, n], device_id=device, device_id_type=MESH
        )

    begin_layer()

    def tick(t, carry):
        ring_tick(t)

        @pl.when(t < middle_tick)
        def _():
            hidden_half(t)

        @pl.when(t == middle_tick)
        def _():
            middle_back()

        @pl.when((t >= attend_tick) & (t < input_tick))
        def _():
            attend_half(t - attend_tick)

        @pl.when(t == input_tick)
        def _():
            input_grad()
            for item in ig_copies():
                item.start()
            vec_copy(0).start()
            tall[...] = total[...].astype(BF16)
            out_copy(0).start()

        @pl.when(t == input_tick + 1)
        def _():
            sum_copy().wait()
            for item in sum_loads(0):
                item.start()

        @pl.when(t == input_tick + 2)
        def _():
            round_far(0)
            for item in sum_loads(1):
                item.start()

        @pl.when(t == input_tick + 3)
        def _():
            round_far(1)
            out_copy(1).start()

        for n in range(bits + 1):
            @pl.when(t == input_tick + 1 + n)
            def _():
                vec_copy(n).wait()
                vec[0] = vec[0] + vrecv[n]
                if n < bits:
                    vec_copy(n + 1).start()

        c, valid = at_stage(t, offsets[stages] + 1)

        @pl.when(valid)
        def _():
            write(c, False)

        return carry

    lax.fori_loop(0, ticks, tick, 0)
    for item in list(ig_copies()) + [out_copy(0), out_copy(1)]:
        item.wait()
    vo_ref[...] = vec[0]


def back(bits, arrays, row, packs, sizes):
    pairs, hidden, model = sizes
    width = pairs * PAIR
    groups = hidden // CHUNK
    chunks = 3 * groups
    plans = color_plans(bits, 0)
    stages = len(plans[0])
    recv = [
        [pltpu.VMEM((SLOTS, size, model // 3), F32) for _, size, kind in plan if kind < 2]
        for plan in plans
    ]
    here = pl.BlockSpec(memory_space=pl.ANY)
    vmem = pl.BlockSpec(memory_space=pltpu.VMEM)
    dma = pltpu.SemaphoreType.DMA
    return pl.pallas_call(
        functools.partial(back_kernel, bits, groups),
        out_shape=[
            jax.ShapeDtypeStruct((hidden, model), F32),
            jax.ShapeDtypeStruct((model, hidden), F32),
            jax.ShapeDtypeStruct((width, model), F32),
            jax.ShapeDtypeStruct((3, model, width), F32),
            jax.ShapeDtypeStruct((2 * BIN, model), F32),
            jax.ShapeDtypeStruct((2 * BIN, model), BF16),
            jax.ShapeDtypeStruct((BIN, model), F32),
            jax.ShapeDtypeStruct((16, model), F32),
        ],
        in_specs=[here] * len(arrays) + [vmem] * 3,
        out_specs=[here] * 7 + [vmem],
        scratch_shapes=[
            pltpu.VMEM((chunks + SENDS, CHUNK, model), F32),
            pltpu.VMEM((LANDS, CHUNK, model), F32),
            recv,
            pltpu.VMEM((2 * pairs, 3, BIN, PAIR), BF16),
            pltpu.VMEM((2 * pairs, BIN, PAIR), BF16),
            pltpu.VMEM((2 * pairs, BIN, PAIR), BF16),
            pltpu.VMEM((BIN, model), BF16),
            pltpu.VMEM((BIN, model), BF16),
            pltpu.VMEM((BIN, model), BF16),
            pltpu.VMEM((model, BIN), BF16),
            pltpu.VMEM((BIN, model), F32),
            pltpu.VMEM((BIN, model), F32),
            pltpu.VMEM((BIN, model), F32),
            pltpu.VMEM((2, model, CHUNK), F32),
            pltpu.VMEM((2, CHUNK, model), F32),
            pltpu.VMEM((3, model, CHUNK), BF16),
            pltpu.VMEM((3, CHUNK, model), BF16),
            pltpu.VMEM((model, CHUNK), F32),
            pltpu.VMEM((CHUNK, model), F32),
            pltpu.VMEM((2, width, model), F32),
            pltpu.VMEM((2, 3, model, PAIR), F32),
            pltpu.VMEM((BIN, CHUNK), BF16),
            pltpu.VMEM((BIN, CHUNK), BF16),
            pltpu.VMEM((2 * pairs, 8, BIN), F32),
            pltpu.VMEM((BIN, PAIR), F32),
            pltpu.VMEM((BIN, PAIR), F32),
            pltpu.VMEM((2, 16, model), F32),
            pltpu.VMEM((bits + 1, 16, model), F32),
            dma((SLOTS, 3, stages)),
            dma((SLOTS, 3, stages)),
            dma((LANDS,)),
            dma((LANDS,)),
            dma((SLOTS, 12)),
            dma((10,)),
            dma((2, 2)),
            dma((2,)),
            dma((2, 2)),
            dma((2, 3)),
            dma((9,)),
            dma((2, bits + 1)),
        ],
        compiler_params=pltpu.CompilerParams(
            collective_id=0, has_side_effects=True, vmem_limit_bytes=67_043_328
        ),
        name="back",
    )(*arrays, row, *packs)


def on_device(
    tokens, segments, lengths, ln1_gain, ln1_bias, w_qkv, b_qv, w_out, out_bias,
    ln2_gain, ln2_bias, w_fc, b_fc, w_proj, proj_bias, cotangent,
):
    model = tokens.shape[1]
    width = w_qkv.shape[2]
    hidden = w_fc.shape[1]
    pairs = width // PAIR
    groups = lax.axis_size("dp")
    bits = groups.bit_length() - 1
    if lax.axis_size("mp") != 2 or groups != 1 << bits or tokens.shape[0] != 2 * BIN:
        raise ValueError("unsupported mesh")
    side = lax.axis_index("mp")
    mine = side.astype(jnp.int32).reshape(1)
    swap = [(0, 1), (1, 0)]

    def cross(value):
        return lax.ppermute(value, "mp", swap)

    w3 = jnp.transpose(w_qkv, (1, 0, 2)).astype(F32)
    vectors = (ln1_gain, ln1_bias, out_bias, ln2_gain, ln2_bias, proj_bias, b_qv.reshape(-1), b_fc)
    pack = jnp.concatenate([item.astype(F32) for item in vectors]).reshape(-1, model)
    pack_other = cross(pack)
    w3_other = cross(w3)
    wo_own = w_out.astype(F32)
    wo_other = cross(wo_own)

    own, other_front = front(
        mine, tokens, segments.reshape(2, BIN), lengths, pack, w3, width,
    )
    qkv_own, attn_own, lse_own, h1, start, row = own
    pack_other, w3_other, h1 = lax.optimization_barrier((pack_other, w3_other, h1))
    qkv_other, attn_other, lse_other = other_front(h1, start, pack_other, w3_other)
    arrays = (
        qkv_own, qkv_other, attn_own, attn_other, h1, w3, w3_other, tokens, cotangent,
        wo_own, wo_other, w_fc, w_proj, lse_own, lse_other,
    )
    grad_proj, grad_fc, grad_out, grad_qkv, input_grad, block_out, _, rows = back(
        bits, arrays, row, (pack, pack_other), (pairs, hidden, model)
    )
    grad_qkv = jnp.transpose(grad_qkv, (1, 0, 2))
    return (
        block_out,
        input_grad,
        rows[0],
        rows[1],
        grad_qkv,
        rows[8].reshape(2, width),
        grad_out,
        rows[2],
        rows[3],
        rows[4],
        grad_fc,
        rows[6:8].reshape(-1),
        grad_proj,
        rows[5],
    )


def solution(mesh):
    rows = P("dp", None)
    placed = (
        rows, P("dp"), rows, P(), P(), P(None, None, "mp"), P(None, "mp"), P("mp", None), P(),
        P(), P(), P(None, "mp"), P("mp"), P("mp", None), P(), rows,
    )
    results = (
        rows, rows, P(), P(), P(None, None, "mp"), P(None, "mp"), P("mp", None), P(), P(), P(),
        P(None, "mp"), P("mp"), P("mp", None), P(),
    )
    return jax.shard_map(
        on_device, mesh=mesh, in_specs=placed, out_specs=results, check_vma=False
    )
```

```python
import functools

import jax
import jax.numpy as jnp
from jax import lax
from jax.experimental import pallas as pl
from jax.experimental.pallas import tpu as pltpu
from jax.sharding import PartitionSpec as P

HEAD_DIM = 64
BIN = 1024
PAIR = 2 * HEAD_DIM
BLOCK = 256
CHUNK = 256
SLOTS = 4
SENDS = 4
LANDS = 5
QV_ROW = 6
FC_ROW = 7

epsilon = 1e-05
gelu_scale = 0.7978845608028654
gelu_cubic = 0.044715
score_scale = 0.125
masked_score = -1e30

MESH = pl.DeviceIdType.MESH
F32 = jnp.float32
BF16 = jnp.bfloat16
VMEM_LIMIT = 64_000_000


def dot_nn(left, right):
    return lax.dot_general(left, right, (((1,), (0,)), ((), ())), preferred_element_type=F32)


def dot_nt(left, right):
    return lax.dot_general(left, right, (((1,), (1,)), ((), ())), preferred_element_type=F32)


def dot_tn(left, right):
    return lax.dot_general(left, right, (((0,), (0,)), ((), ())), preferred_element_type=F32)


def norm_parts(values):
    center = values - jnp.mean(values, axis=-1, keepdims=True)
    inverse = lax.rsqrt(jnp.mean(center * center, axis=-1, keepdims=True) + epsilon)
    return center * inverse, inverse


def norm_back(upstream, normal, inverse, gain):
    scaled = upstream * gain
    centered = scaled - jnp.mean(scaled, axis=-1, keepdims=True)
    return inverse * (centered - normal * jnp.mean(scaled * normal, axis=-1, keepdims=True))


def gelu_pair(values):
    square = values * values
    tangent = jnp.tanh(gelu_scale * (values + gelu_cubic * square * values))
    half = 0.5 * (1.0 + tangent)
    slope = half + 0.5 * values * (1.0 - tangent * tangent) * (
        gelu_scale + 3.0 * gelu_cubic * gelu_scale * square
    )
    return values * half, slope


def column_to_row(column):
    rows = column.shape[0]
    return jnp.broadcast_to(column, (rows, 128)).T[0:1]


def head_mask(head, scale):
    lane = lax.broadcasted_iota(jnp.int32, (1, PAIR), 1)
    return jnp.where(lane // HEAD_DIM == head, scale, 0.0).astype(BF16)


def attend_pair(qkv_ref, start_ref, attn_ref, lse_ref):
    lane = lax.broadcasted_iota(jnp.int32, (1, PAIR), 1)
    for block in range(BIN // BLOCK):
        rows = slice(block * BLOCK, (block + 1) * BLOCK)
        seen = (block + 1) * BLOCK
        queries = qkv_ref[0, 0, rows]
        key_rows = qkv_ref[0, 1, 0:seen]
        value_rows = qkv_ref[0, 2, 0:seen]
        j = lax.broadcasted_iota(jnp.int32, (BLOCK, seen), 1)
        i = lax.broadcasted_iota(jnp.int32, (BLOCK, seen), 0) + block * BLOCK
        visible = (j >= start_ref[rows]) & (j <= i)
        both = jnp.concatenate([queries * head_mask(head, score_scale) for head in range(2)], axis=0)
        scores = dot_nt(both, key_rows).reshape(2, BLOCK, seen)
        scores = jnp.where(visible[None], scores, masked_score)
        highest = jnp.max(scores, axis=-1, keepdims=True)
        weights = jnp.exp(scores - highest)
        totals = jnp.sum(weights, axis=-1, keepdims=True)
        mixed = dot_nn(weights.astype(BF16).reshape(2 * BLOCK, seen), value_rows).reshape(2, BLOCK, PAIR) / totals
        logs = highest + jnp.log(totals)
        for head in range(2):
            lse_ref[0, head : head + 1, rows] = column_to_row(logs[head])
        attn_ref[0, rows] = jnp.where(lane < HEAD_DIM, mixed[0], mixed[1]).astype(BF16)


def project_and_attend(h1, w_ref, pack_ref, start_ref, qkv_ref, attn_ref, lse_ref):
    width = pl.num_programs(0) * PAIR
    place = pl.program_id(0) * PAIR
    weights = jnp.concatenate([w_ref[c].astype(BF16) for c in range(3)], axis=1)
    projected = dot_nn(h1, weights)
    for c in range(3):
        out = projected[:, c * PAIR : (c + 1) * PAIR]
        if c != 1:
            at = place if c == 0 else width + place
            out = out + pack_ref[QV_ROW : QV_ROW + 1, pl.ds(pl.multiple_of(at, PAIR), PAIR)]
        qkv_ref[0, c] = out.astype(BF16)
    attend_pair(qkv_ref, start_ref, attn_ref, lse_ref)


def own_front_kernel(
    mp_ref, x_ref, seg_ref, len_ref, pack_ref, w_ref,
    qkv_ref, attn_ref, lse_ref, h1_ref, start_ref, row_ref,
):
    @pl.when(pl.program_id(0) == 0)
    def _():
        gain = pack_ref[0:1]
        shift = pack_ref[1:2]
        for block in range(BIN // BLOCK):
            rows = slice(block * BLOCK, (block + 1) * BLOCK)
            normal, _ = norm_parts(x_ref[rows].astype(F32))
            h1_ref[rows] = (normal * gain + shift).astype(BF16)
        mine = mp_ref[0]
        count = len_ref.shape[1]
        seg = seg_ref[pl.ds(mine, 1), :].astype(F32)
        seg = jnp.broadcast_to(seg, (128, BIN)).T
        seg = seg[:, :count]
        label = lax.broadcasted_iota(jnp.int32, (BIN, count), 1).astype(F32)
        sizes = len_ref[pl.ds(mine, 1), :].astype(F32)
        start = jnp.sum(jnp.where(label < seg, sizes, 0.0), axis=1, keepdims=True)
        rows_of = jnp.sum(jnp.where(label == seg, 1.0, 0.0), axis=0, keepdims=True)
        first = jnp.sum(jnp.where(label < seg, rows_of, 0.0), axis=1, keepdims=True)
        start = jnp.maximum(start, first)
        start_ref[...] = start.astype(jnp.int32)
        row_ref[...] = column_to_row(start).astype(jnp.int32)

    project_and_attend(h1_ref[...], w_ref, pack_ref, start_ref, qkv_ref, attn_ref, lse_ref)


def other_front_kernel(h1_ref, start_ref, pack_ref, w_ref, qkv_ref, attn_ref, lse_ref):
    project_and_attend(h1_ref[...], w_ref, pack_ref, start_ref, qkv_ref, attn_ref, lse_ref)


def fixed(shape):
    return pl.BlockSpec(shape, lambda *_: (0,) * len(shape), pipeline_mode=pl.Buffered(1))


def front(mine, x, seg, lens, pack, w_own, width):
    model = x.shape[1]
    pairs = width // PAIR
    per_pair = [pl.BlockSpec((3, model, PAIR), lambda p, *_: (0, 0, p))]
    outs = [
        pl.BlockSpec((1, 3, BIN, PAIR), lambda p, *_: (p, 0, 0, 0)),
        pl.BlockSpec((1, BIN, PAIR), lambda p, *_: (p, 0, 0)),
        pl.BlockSpec((1, 8, BIN), lambda p, *_: (p, 0, 0)),
    ]
    out_shapes = [
        jax.ShapeDtypeStruct((pairs, 3, BIN, PAIR), BF16),
        jax.ShapeDtypeStruct((pairs, BIN, PAIR), BF16),
        jax.ShapeDtypeStruct((pairs, 8, BIN), F32),
    ]
    cost = pl.CostEstimate(flops=6_000_000_000, bytes_accessed=10_000_000, transcendentals=0)
    params = pltpu.CompilerParams(vmem_limit_bytes=VMEM_LIMIT)
    own = pl.pallas_call(
        own_front_kernel,
        out_shape=out_shapes
        + [
            jax.ShapeDtypeStruct((BIN, model), BF16),
            jax.ShapeDtypeStruct((BIN, 1), jnp.int32),
            jax.ShapeDtypeStruct((1, BIN), jnp.int32),
        ],
        grid_spec=pltpu.PrefetchScalarGridSpec(
            num_scalar_prefetch=1,
            grid=(pairs,),
            in_specs=[
                pl.BlockSpec((BIN, model), lambda p, m: (m[0], 0)),
                fixed(seg.shape), fixed(lens.shape), fixed(pack.shape),
            ]
            + per_pair,
            out_specs=outs
            + [
                pl.BlockSpec((BIN, model), lambda p, *_: (0, 0)),
                pl.BlockSpec((BIN, 1), lambda p, *_: (0, 0)),
                pl.BlockSpec((1, BIN), lambda p, *_: (0, 0)),
            ],
        ),
        compiler_params=params,
        cost_estimate=cost,
        name="own_front",
    )

    def other(h1, start, pack_other, w_other):
        return pl.pallas_call(
            other_front_kernel,
            out_shape=out_shapes,
            grid=(pairs,),
            in_specs=[fixed((BIN, model)), fixed((BIN, 1)), fixed(pack.shape)] + per_pair,
            out_specs=outs,
            compiler_params=params,
            cost_estimate=cost,
            name="other_front",
        )(h1, start, pack_other, w_other)

    return own(mine, x, seg, lens, pack, w_own), other


def halving_plan(order, rows):
    first, back = [], []
    size = rows
    for n, bit in enumerate(order):
        if n < len(order) - 1 and size % 16 == 0:
            size //= 2
            first.append((bit, size, 0))
            back.append((bit, size, 2))
        else:
            first.append((bit, size, 1))
    return first + back[::-1]


def color_orders(bits, odd):
    plain = list(range(bits))
    orders = [plain, plain, plain]
    if bits > 1:
        orders[1] = [1, 0] + plain[2:]
    if bits > 2:
        orders[2] = [2, 1, 0] + plain[3:] if odd else [2, 0, 1] + plain[3:]
    return orders


def color_plans(bits, odd):
    return [halving_plan(order, CHUNK) for order in color_orders(bits, odd)]


def attend_back_pair(half, place, qkv, dattn, lse_ref, row_ref, dk, dv, vec, pairs):
    dk[...] = jnp.zeros_like(dk)
    dv[...] = jnp.zeros_like(dv)
    pair = half * pairs + place
    dq_sum = jnp.zeros((1, PAIR), F32)
    for block in range(BIN // BLOCK):
        rows = slice(block * BLOCK, (block + 1) * BLOCK)
        seen = (block + 1) * BLOCK
        queries = qkv[pair, 0, rows]
        upstream = dattn[pair, rows]
        key_rows = qkv[pair, 1, 0:seen]
        value_rows = qkv[pair, 2, 0:seen]
        j = lax.broadcasted_iota(jnp.int32, (seen, BLOCK), 0)
        i = lax.broadcasted_iota(jnp.int32, (seen, BLOCK), 1) + block * BLOCK
        visible = (j >= row_ref[0:1, rows]) & (j <= i)
        dq = jnp.zeros((BLOCK, PAIR), F32)
        for head in range(2):
            masked_q = queries * head_mask(head, score_scale)
            masked_up = upstream * head_mask(head, 1.0)
            scores = dot_nt(key_rows, masked_q)
            probs = jnp.exp(scores - lse_ref[pair, head : head + 1, rows])
            probs = jnp.where(visible, probs, 0.0)
            dprobs = dot_nt(value_rows, masked_up)
            inner = jnp.sum(probs * dprobs, axis=0, keepdims=True)
            dscores = (probs * (dprobs - inner)).astype(BF16)
            dv[0:seen] = dv[0:seen] + dot_nn(probs.astype(BF16), masked_up)
            dk[0:seen] = dk[0:seen] + dot_nn(dscores, masked_q)
            dq = dq + dot_tn(dscores, key_rows * head_mask(head, 1.0))
        dq = (dq * score_scale).astype(BF16)
        qkv[pair, 0, rows] = dq
        dq_sum = dq_sum + jnp.sum(dq.astype(F32), axis=0, keepdims=True)
    dv_low = dv[...].astype(BF16)
    qkv[pair, 1] = dk[...].astype(BF16)
    qkv[pair, 2] = dv_low
    dv_sum = jnp.sum(dv_low.astype(F32), axis=0, keepdims=True)
    width = pairs * PAIR
    vec[half, 8:9, pl.ds(pl.multiple_of(place * PAIR, PAIR), PAIR)] = dq_sum
    vec[half, 8:9, pl.ds(pl.multiple_of(width + place * PAIR, PAIR), PAIR)] = dv_sum


def back_kernel(
    bits, groups,
    qkv_own_ref, qkv_other_ref, attn_own_ref, attn_other_ref, h1_ref, w3_own_ref, w3_other_ref,
    x_ref, cot_ref, wo_own_ref, wo_other_ref, wf_ref, wp_ref,
    lse_own_ref, lse_other_ref, row_ref, pack_ref, pack_other_ref,
    op_ref, of_ref, oa_ref, oq_ref, ig_ref, bo_ref, sum_ref, vo_ref,
    acc, mpbuf, rbufs, qkv, dattn, attn, cot, x, tall, flip, total, dwide, first,
    wf, wp, wf_low, wp_low, wf_out, wp_out, wo, w3, act, slope, lse, dk, dv, vec, vrecv,
    ssem, rsem, mps, mpr, wsem, lsem, bsem, wsend, wrecv, hsem, igsem, vsem,
):
    dp = lax.axis_index("dp")
    mp = lax.axis_index("mp")
    chunks = 3 * groups
    own_bits = [(dp // (1 << b)) % 2 for b in range(bits)]
    partner = [dp + (1 - 2 * own_bits[b]) * (1 << b) for b in range(bits)]
    plans = [color_plans(bits, odd) for odd in range(2)]
    stages = len(plans[0][0])
    flights = [2] + [1] * (stages - 2) + [2]
    offsets = [sum(flights[:s]) for s in range(stages + 1)]
    pairs = qkv_own_ref.shape[0]
    model = x_ref.shape[1]
    width = pairs * PAIR
    pieces = model // CHUNK

    my_rows = pl.ds(pl.multiple_of(mp * BIN, BIN), BIN)
    far_rows = pl.ds(pl.multiple_of((1 - mp) * BIN, BIN), BIN)
    loads = []

    def load(src, dst):
        loads.append(pltpu.make_async_copy(src, dst, lsem.at[len(loads)]))

    load(attn_own_ref, attn.at[0:pairs])
    load(attn_other_ref, attn.at[pairs : 2 * pairs])
    load(wo_own_ref, wo.at[0])
    load(wo_other_ref, wo.at[1])
    load(x_ref.at[my_rows], x)
    early = len(loads)
    load(cot_ref.at[my_rows], cot)
    load(qkv_own_ref, qkv.at[0:pairs])
    load(qkv_other_ref, qkv.at[pairs : 2 * pairs])
    load(lse_own_ref, lse.at[0:pairs])
    load(lse_other_ref, lse.at[pairs : 2 * pairs])

    def block_loads(b):
        slot = b % 3
        at = pl.ds(pl.multiple_of(b * CHUNK, CHUNK), CHUNK)
        return [
            pltpu.make_async_copy(wf_ref.at[:, at], wf_low.at[slot], bsem.at[slot, 0]),
            pltpu.make_async_copy(wp_ref.at[at], wp_low.at[slot], bsem.at[slot, 1]),
        ]

    def block_sends(b):
        slot = b % 2
        return [
            pltpu.make_async_remote_copy(
                src, dst.at[slot], wsend.at[n], wrecv.at[slot, n],
                device_id=(dp, 1 - mp), device_id_type=MESH,
            )
            for n, (src, dst) in enumerate(((wf_out, wf), (wp_out, wp)))
        ]

    def send_block(b):
        for item in block_loads(b):
            item.wait()
        wf_out[...] = wf_low[b % 3].astype(F32)
        wp_out[...] = wp_low[b % 3].astype(F32)
        for item in block_sends(b):
            item.start()

    def w3_loads(q, begin):
        slot = 1 - q % 2
        at = pl.ds(pl.multiple_of((q // 2) * PAIR, PAIR), PAIR)
        for half, ref in ((0, w3_own_ref), (1, w3_other_ref)):
            @pl.when(slot == half)
            def _():
                for c in range(3):
                    item = pltpu.make_async_copy(ref.at[c, :, at], w3.at[half, c], hsem.at[half, c])
                    item.start() if begin else item.wait()

    def h1_load():
        return pltpu.make_async_copy(h1_ref, tall, lsem.at[9])

    for item in loads:
        item.start()
    for b in range(2):
        for item in block_loads(b):
            item.start()

    barrier = pltpu.get_barrier_semaphore()
    for b in range(bits):
        pl.semaphore_signal(barrier, inc=1, device_id=(partner[b], mp), device_id_type=MESH)
    pl.semaphore_signal(barrier, inc=1, device_id=(dp, 1 - mp), device_id_type=MESH)
    pl.semaphore_wait(barrier, bits + 1)

    def walk(plan):
        base, found = 0, []
        for bit, size, kind in plan:
            found.append(base)
            if kind == 0:
                base = base + own_bits[bit] * size
            if kind == 2:
                base = base - own_bits[bit] * size
        return found

    starts = [[walk(plan) for plan in plans[odd]] for odd in range(2)]

    def place(c, color, s):
        sides = []
        for odd in range(2):
            bit, size, kind = plans[odd][color][s]
            sides.append((starts[odd][color][s], own_bits[bit], partner[bit]))
        if plans[0][color] == plans[1][color]:
            return sides[0]
        return [jnp.where(c % 2 == 0, even, odd) for even, odd in zip(*sides)]

    def lanes(color):
        share = model // 3
        return slice(color * share, (color + 1) * share)

    def copy(c, color, s):
        _, size, kind = plans[0][color][s]
        slot = c % SLOTS
        base, side, device = place(c, color, s)
        if kind == 0:
            base = base + (1 - side) * size
        src = acc.at[c, pl.ds(pl.multiple_of(base, 8), size), lanes(color)]
        dst = src if kind == 2 else rbufs[color][s].at[slot]
        return pltpu.make_async_remote_copy(
            src, dst, ssem.at[slot, color, s], rsem.at[slot, color, s],
            device_id=(device, mp), device_id_type=MESH,
        )

    def finish(c, color, s):
        _, size, kind = plans[0][color][s]
        copy(c, color, s).wait()
        if kind == 2:
            return
        base, side, _ = place(c, color, s)
        if kind == 0:
            base = base + side * size
        rows = pl.ds(pl.multiple_of(base, 8), size)
        acc[c, rows, lanes(color)] = acc[c, rows, lanes(color)] + rbufs[color][s][c % SLOTS]

    def mp_copy(c):
        slot, land = c % SENDS, c % LANDS
        return pltpu.make_async_remote_copy(
            acc.at[chunks + slot], mpbuf.at[land], mps.at[land], mpr.at[land],
            device_id=(dp, 1 - mp), device_id_type=MESH,
        )

    def mp_finish(c):
        mp_copy(c).wait()
        acc[c] = acc[c] + mpbuf[c % LANDS]

    def chunk_rows(n):
        return pl.ds(pl.multiple_of(n * CHUNK, CHUNK), CHUNK)

    def whole_copy(dst, c):
        return pltpu.make_async_copy(acc.at[c], dst, wsem.at[c % SLOTS, 0])

    def piece_copies(c):
        at = chunk_rows(c // 2)
        return [
            pltpu.make_async_copy(
                acc.at[c, :, n * CHUNK : (n + 1) * CHUNK],
                of_ref.at[n * CHUNK : (n + 1) * CHUNK, at],
                wsem.at[c % SLOTS, n],
            )
            for n in range(pieces)
        ]

    def write(c, begin):
        @pl.when((c < 2 * groups) & (c % 2 == 0))
        def _():
            item = whole_copy(op_ref.at[chunk_rows(c // 2)], c)
            item.start() if begin else item.wait()

        @pl.when((c < 2 * groups) & (c % 2 == 1))
        def _():
            for item in piece_copies(c):
                item.start() if begin else item.wait()

        for part in range(2):
            piece = 2 * (c - 2 * groups) + part
            rows = slice(part * PAIR, (part + 1) * PAIR)

            @pl.when((c >= 2 * groups) & (piece < pairs))
            def _():
                at = pl.ds(pl.multiple_of(piece * PAIR, PAIR), PAIR)
                item = pltpu.make_async_copy(acc.at[c, rows], oa_ref.at[at], wsem.at[c % SLOTS, 6 * part])
                item.start() if begin else item.wait()

            @pl.when((c >= 2 * groups) & (piece >= pairs))
            def _():
                across = pl.ds(pl.multiple_of((piece // pairs - 1) * PAIR, PAIR), PAIR)
                for n in range(6):
                    down = pl.ds(pl.multiple_of((n // 3) * width + (piece % pairs) * PAIR, PAIR), PAIR)
                    item = pltpu.make_async_copy(
                        acc.at[c, rows, n * PAIR : (n + 1) * PAIR],
                        oq_ref.at[n % 3, down, across],
                        wsem.at[c % SLOTS, 6 * part + n],
                    )
                    item.start() if begin else item.wait()

    middle_tick = 2 * groups
    attend_tick = middle_tick + 1
    input_tick = attend_tick + 2 * pairs
    late = chunks - 4
    late_tick = late + 3
    arrivals = [(middle_tick + 2, [0]), (middle_tick + 3, [1, 2]), (middle_tick + 5, [3]), (middle_tick + 7, [4, 5])]
    ticks = chunks + 3 + offsets[stages] + 1

    def at_stage(t, shift):
        since = t - shift
        early = (since >= 2) & (since < late + 2)
        last = (since >= late_tick) & (since < chunks + 3)
        c = jnp.where(since < late_tick, since - 2, since - late_tick + late)
        return jnp.clip(c, 0, chunks - 1), early | last

    def ring_tick(t):
        @pl.when((t >= 2) & (t % 2 == 0) & (t < middle_tick + 2))
        def _():
            mp_finish(t - 2)
            mp_finish(t - 1)

        for at, made in arrivals:
            @pl.when(t == at)
            def _():
                for n in made:
                    mp_finish(2 * groups + n)

        for s in range(stages):
            c, valid = at_stage(t, offsets[s + 1])

            @pl.when(valid)
            def _():
                for color in range(3):
                    finish(c, color, s)

        for s in list(range(stages)) + [-1]:
            c, valid = at_stage(t, offsets[s + 1])

            @pl.when(valid)
            def _():
                if s + 1 == stages:
                    write(c, True)
                else:
                    for color in range(3):
                        copy(c, color, s + 1).start()

    def begin_layer():
        send_block(0)
        for item in loads[:early]:
            item.wait()
        out_bias = pack_ref[2:3]
        gain = pack_ref[3:4]
        shift = pack_ref[4:5]
        proj_bias = pack_ref[5:6]
        vec[...] = jnp.zeros_like(vec)

        def step(block, carry):
            rows = pl.ds(pl.multiple_of(block * BLOCK, BLOCK), BLOCK)
            branch = out_bias
            for half in range(2):
                mixed = [attn[half * pairs + p, rows] for p in range(pairs)]
                branch = branch + dot_nn(jnp.concatenate(mixed, axis=1), wo[half].astype(BF16))
            r1 = x[rows].astype(F32) + branch
            first[rows] = r1
            total[rows] = r1 + proj_bias
            dwide[rows] = jnp.zeros((BLOCK, model), F32)
            normal, _ = norm_parts(r1)
            h2 = (normal * gain + shift).astype(BF16)
            tall[rows] = h2
            flip[:, rows] = h2.T
            return carry

        lax.fori_loop(0, BIN // BLOCK, step, 0)
        loads[early].wait()

    def hidden_half(u):
        b, half = u // 2, 1 - u % 2

        @pl.when(half == 1)
        def _():
            for item in block_sends(b):
                item.wait()

            @pl.when(b + 1 < groups)
            def _():
                send_block(b + 1)

            @pl.when(b + 2 < groups)
            def _():
                for item in block_loads(b + 2):
                    item.start()

            wf_low[3] = wf[b % 2].astype(BF16)
            wp_low[3] = wp[b % 2].astype(BF16)

        span = 2 * BLOCK
        place = jnp.where(half == 0, b % 3, 3)
        fc = wf_low[place]
        proj = wp_low[place]
        at = pl.ds(FC_ROW + b // pieces, 1), pl.ds(pl.multiple_of((b % pieces) * CHUNK, CHUNK), CHUNK)
        bias = jnp.where(half == 0, pack_ref[at], pack_other_ref[at])
        df_sum = jnp.zeros((1, CHUNK), F32)
        for block in range(BIN // span):
            rows = slice(block * span, (block + 1) * span)
            pre = dot_nn(tall[rows], fc) + bias
            hidden, rise = gelu_pair(pre)
            hidden = hidden.astype(BF16)
            act[rows] = hidden
            total[rows] = total[rows] + dot_nn(hidden, proj)
            df = (dot_nt(cot[rows], proj) * rise).astype(BF16)
            slope[rows] = df
            df_sum = df_sum + jnp.sum(df.astype(F32), axis=0, keepdims=True)
            dwide[rows] = dwide[rows] + dot_nt(df, fc)

        vec[half, pl.ds(6 + b // pieces, 1), pl.ds(pl.multiple_of((b % pieces) * CHUNK, CHUNK), CHUNK)] = df_sum
        at = jnp.where(half == 0, 2 * b, chunks + (2 * b) % SENDS)
        acc[at] = dot_tn(act[...], cot[...])
        grad = dot_nn(flip[...], slope[...])
        for n in range(pieces):
            acc[at + 1, :, n * CHUNK : (n + 1) * CHUNK] = grad[n * CHUNK : (n + 1) * CHUNK]

        @pl.when(half == 1)
        def _():
            mp_copy(2 * b).start()
            mp_copy(2 * b + 1).start()

    def put_piece(half, piece, part, value):
        n = piece // 2
        at = jnp.where(half == 0, 2 * groups + n, chunks + (2 * groups + n) % SENDS)
        rows = pl.ds(pl.multiple_of((piece % 2) * PAIR, PAIR), PAIR)
        acc[at, rows, part * width : part * width + value.shape[1]] = value

    def sum_copy():
        return pltpu.make_async_remote_copy(
            total, sum_ref, igsem.at[3], igsem.at[4],
            device_id=(dp, 1 - mp), device_id_type=MESH,
        )

    def sum_loads(part):
        return [
            pltpu.make_async_copy(
                sum_ref.at[(2 * part + n) * CHUNK : (2 * part + n + 1) * CHUNK], wp.at[n], igsem.at[5 + n]
            )
            for n in range(2)
        ]

    def round_far(part):
        for n, item in enumerate(sum_loads(part)):
            item.wait()
            cot[(2 * part + n) * CHUNK : (2 * part + n + 1) * CHUNK] = wp[n].astype(BF16)

    def out_copy(n):
        src, rows = ((tall, my_rows), (cot, far_rows))[n]
        return pltpu.make_async_copy(src, bo_ref.at[rows], igsem.at[7 + n])

    def middle_back():
        sum_copy().start()
        gain = pack_ref[3:4]
        w3_loads(jnp.int32(0), True)

        def step(block, sums):
            rows = pl.ds(pl.multiple_of(block * BLOCK, BLOCK), BLOCK)
            normal, inverse = norm_parts(first[rows])
            up = dwide[rows]
            upstream = cot[rows].astype(F32)
            dr1 = upstream + norm_back(up, normal, inverse, gain)
            first[rows] = dr1
            dwide[rows] = jnp.zeros((BLOCK, model), F32)
            da = dr1.astype(BF16)
            tall[rows] = da
            for half in range(2):
                back = dot_nt(da, wo[half].astype(BF16)).astype(BF16)
                for p in range(pairs):
                    dattn[half * pairs + p, rows] = back[:, p * PAIR : (p + 1) * PAIR]
            return tuple(
                total_row + jnp.sum(item, axis=0, keepdims=True)
                for total_row, item in zip(sums, (da.astype(F32), up * normal, up, upstream))
            )

        sums = lax.fori_loop(0, BIN // BLOCK, step, (jnp.zeros((1, model), F32),) * 4)
        for half in range(2):
            for n in range(4):
                vec[half, 2 + n : 3 + n] = sums[n]
            mixed = jnp.concatenate([attn[half * pairs + p] for p in range(pairs)], axis=1)
            grad = dot_tn(mixed, tall[...])
            for piece in range(pairs):
                put_piece(half, piece, 0, grad[piece * PAIR : (piece + 1) * PAIR])
        mp_copy(2 * groups).start()
        h1_load().start()
        for item in loads[early + 1 :]:
            item.wait()

    def attend_half(q):
        p, half = q // 2, 1 - q % 2

        @pl.when(q + 1 < 2 * pairs)
        def _():
            w3_loads(q + 1, True)

        @pl.when(q == 0)
        def _():
            h1_load().wait()
            flip[...] = tall[...].T

        attend_back_pair(half, p, qkv, dattn, lse, row_ref, dk, dv, vec, pairs)
        w3_loads(q, False)
        pair = half * pairs + p
        low = jnp.concatenate([qkv[pair, c] for c in range(3)], axis=1)
        grad = dot_nn(flip[...], low)
        for n in range(2 * pairs):
            put_piece(half, pairs * (p + 1) + n % pairs, n // pairs, grad[n * PAIR : (n + 1) * PAIR])
        weights = jnp.concatenate([w3[half, c].astype(BF16) for c in range(3)], axis=1)
        dwide[...] = dwide[...] + dot_nt(low, weights)
        for at, made in ((0, [1, 2]), (2, [3]), (4, [4, 5])):
            @pl.when(q == at)
            def _():
                for n in made:
                    mp_copy(2 * groups + n).start()

    def input_grad():
        gain = pack_ref[0:1]

        def step(block, sums):
            rows = pl.ds(pl.multiple_of(block * BLOCK, BLOCK), BLOCK)
            normal, inverse = norm_parts(x[rows].astype(F32))
            up = dwide[rows]
            first[rows] = first[rows] + norm_back(up, normal, inverse, gain)
            return (
                sums[0] + jnp.sum(up * normal, axis=0, keepdims=True),
                sums[1] + jnp.sum(up, axis=0, keepdims=True),
            )

        gain_sum, shift_sum = lax.fori_loop(0, BIN // BLOCK, step, (jnp.zeros((1, model), F32),) * 2)
        for half in range(2):
            vec[half, 0:1] = gain_sum
            vec[half, 1:2] = shift_sum

    def ig_copies():
        local = pltpu.make_async_copy(first, ig_ref.at[my_rows], igsem.at[0])
        remote = pltpu.make_async_remote_copy(
            first, ig_ref.at[my_rows], igsem.at[1], igsem.at[2],
            device_id=(dp, 1 - mp), device_id_type=MESH,
        )
        return local, remote

    def vec_copy(n):
        if n == 0:
            src, device = vec.at[1], (dp, 1 - mp)
        else:
            src, device = vec.at[0], (partner[n - 1], mp)
        return pltpu.make_async_remote_copy(
            src, vrecv.at[n], vsem.at[0, n], vsem.at[1, n], device_id=device, device_id_type=MESH
        )

    begin_layer()

    def tick(t, carry):
        ring_tick(t)

        @pl.when(t < middle_tick)
        def _():
            hidden_half(t)

        @pl.when(t == middle_tick)
        def _():
            middle_back()

        @pl.when((t >= attend_tick) & (t < input_tick))
        def _():
            attend_half(t - attend_tick)

        @pl.when(t == input_tick)
        def _():
            input_grad()
            for item in ig_copies():
                item.start()
            vec_copy(0).start()
            tall[...] = total[...].astype(BF16)
            out_copy(0).start()

        @pl.when(t == input_tick + 1)
        def _():
            sum_copy().wait()
            for item in sum_loads(0):
                item.start()

        @pl.when(t == input_tick + 2)
        def _():
            round_far(0)
            for item in sum_loads(1):
                item.start()

        @pl.when(t == input_tick + 3)
        def _():
            round_far(1)
            out_copy(1).start()

        for n in range(bits + 1):
            @pl.when(t == input_tick + 1 + n)
            def _():
                vec_copy(n).wait()
                vec[0] = vec[0] + vrecv[n]
                if n < bits:
                    vec_copy(n + 1).start()

        c, valid = at_stage(t, offsets[stages] + 1)

        @pl.when(valid)
        def _():
            write(c, False)

        return carry

    lax.fori_loop(0, ticks, tick, 0)
    for item in list(ig_copies()) + [out_copy(0), out_copy(1)]:
        item.wait()
    vo_ref[...] = vec[0]


def back(bits, arrays, row, packs, sizes):
    pairs, hidden, model = sizes
    width = pairs * PAIR
    groups = hidden // CHUNK
    chunks = 3 * groups
    plans = color_plans(bits, 0)
    stages = len(plans[0])
    recv = [
        [pltpu.VMEM((SLOTS, size, model // 3), F32) for _, size, kind in plan if kind < 2]
        for plan in plans
    ]
    here = pl.BlockSpec(memory_space=pl.ANY)
    vmem = pl.BlockSpec(memory_space=pltpu.VMEM)
    dma = pltpu.SemaphoreType.DMA
    return pl.pallas_call(
        functools.partial(back_kernel, bits, groups),
        out_shape=[
            jax.ShapeDtypeStruct((hidden, model), F32),
            jax.ShapeDtypeStruct((model, hidden), F32),
            jax.ShapeDtypeStruct((width, model), F32),
            jax.ShapeDtypeStruct((3, model, width), F32),
            jax.ShapeDtypeStruct((2 * BIN, model), F32),
            jax.ShapeDtypeStruct((2 * BIN, model), BF16),
            jax.ShapeDtypeStruct((BIN, model), F32),
            jax.ShapeDtypeStruct((16, model), F32),
        ],
        in_specs=[here] * len(arrays) + [vmem] * 3,
        out_specs=[here] * 7 + [vmem],
        scratch_shapes=[
            pltpu.VMEM((chunks + SENDS, CHUNK, model), F32),
            pltpu.VMEM((LANDS, CHUNK, model), F32),
            recv,
            pltpu.VMEM((2 * pairs, 3, BIN, PAIR), BF16),
            pltpu.VMEM((2 * pairs, BIN, PAIR), BF16),
            pltpu.VMEM((2 * pairs, BIN, PAIR), BF16),
            pltpu.VMEM((BIN, model), BF16),
            pltpu.VMEM((BIN, model), BF16),
            pltpu.VMEM((BIN, model), BF16),
            pltpu.VMEM((model, BIN), BF16),
            pltpu.VMEM((BIN, model), F32),
            pltpu.VMEM((BIN, model), F32),
            pltpu.VMEM((BIN, model), F32),
            pltpu.VMEM((2, model, CHUNK), F32),
            pltpu.VMEM((2, CHUNK, model), F32),
            pltpu.VMEM((4, model, CHUNK), BF16),
            pltpu.VMEM((4, CHUNK, model), BF16),
            pltpu.VMEM((model, CHUNK), F32),
            pltpu.VMEM((CHUNK, model), F32),
            pltpu.VMEM((2, width, model), F32),
            pltpu.VMEM((2, 3, model, PAIR), F32),
            pltpu.VMEM((BIN, CHUNK), BF16),
            pltpu.VMEM((BIN, CHUNK), BF16),
            pltpu.VMEM((2 * pairs, 8, BIN), F32),
            pltpu.VMEM((BIN, PAIR), F32),
            pltpu.VMEM((BIN, PAIR), F32),
            pltpu.VMEM((2, 16, model), F32),
            pltpu.VMEM((bits + 1, 16, model), F32),
            dma((SLOTS, 3, stages)),
            dma((SLOTS, 3, stages)),
            dma((LANDS,)),
            dma((LANDS,)),
            dma((SLOTS, 12)),
            dma((10,)),
            dma((3, 2)),
            dma((2,)),
            dma((2, 2)),
            dma((2, 3)),
            dma((9,)),
            dma((2, bits + 1)),
        ],
        compiler_params=pltpu.CompilerParams(
            collective_id=0, has_side_effects=True, vmem_limit_bytes=67_043_328
        ),
        name="back",
    )(*arrays, row, *packs)


def on_device(
    tokens, segments, lengths, ln1_gain, ln1_bias, w_qkv, b_qv, w_out, out_bias,
    ln2_gain, ln2_bias, w_fc, b_fc, w_proj, proj_bias, cotangent,
):
    model = tokens.shape[1]
    width = w_qkv.shape[2]
    hidden = w_fc.shape[1]
    pairs = width // PAIR
    groups = lax.axis_size("dp")
    bits = groups.bit_length() - 1
    if lax.axis_size("mp") != 2 or groups != 1 << bits or tokens.shape[0] != 2 * BIN:
        raise ValueError("unsupported mesh")
    side = lax.axis_index("mp")
    mine = side.astype(jnp.int32).reshape(1)
    swap = [(0, 1), (1, 0)]

    def cross(value):
        return lax.ppermute(value, "mp", swap)

    w3 = jnp.transpose(w_qkv, (1, 0, 2)).astype(F32)
    vectors = (ln1_gain, ln1_bias, out_bias, ln2_gain, ln2_bias, proj_bias, b_qv.reshape(-1), b_fc)
    pack = jnp.concatenate([item.astype(F32) for item in vectors]).reshape(-1, model)
    pack_other = cross(pack)
    w3_other = cross(w3)
    wo_own = w_out.astype(F32)
    wo_other = cross(wo_own)

    own, other_front = front(
        mine, tokens, segments.reshape(2, BIN), lengths, pack, w3, width,
    )
    qkv_own, attn_own, lse_own, h1, start, row = own
    pack_other, w3_other, h1 = lax.optimization_barrier((pack_other, w3_other, h1))
    qkv_other, attn_other, lse_other = other_front(h1, start, pack_other, w3_other)
    arrays = (
        qkv_own, qkv_other, attn_own, attn_other, h1, w3, w3_other, tokens, cotangent,
        wo_own, wo_other, w_fc, w_proj, lse_own, lse_other,
    )
    grad_proj, grad_fc, grad_out, grad_qkv, input_grad, block_out, _, rows = back(
        bits, arrays, row, (pack, pack_other), (pairs, hidden, model)
    )
    grad_qkv = jnp.transpose(grad_qkv, (1, 0, 2))
    return (
        block_out,
        input_grad,
        rows[0],
        rows[1],
        grad_qkv,
        rows[8].reshape(2, width),
        grad_out,
        rows[2],
        rows[3],
        rows[4],
        grad_fc,
        rows[6:8].reshape(-1),
        grad_proj,
        rows[5],
    )


def solution(mesh):
    rows = P("dp", None)
    placed = (
        rows, P("dp"), rows, P(), P(), P(None, None, "mp"), P(None, "mp"), P("mp", None), P(),
        P(), P(), P(None, "mp"), P("mp"), P("mp", None), P(), rows,
    )
    results = (
        rows, rows, P(), P(), P(None, None, "mp"), P(None, "mp"), P("mp", None), P(), P(), P(),
        P(None, "mp"), P("mp"), P("mp", None), P(),
    )
    return jax.shard_map(
        on_device, mesh=mesh, in_specs=placed, out_specs=results, check_vma=False
    )
```

```python
import functools

import jax
import jax.numpy as jnp
from jax import lax
from jax.experimental import pallas as pl
from jax.experimental.pallas import tpu as pltpu
from jax.sharding import PartitionSpec as P

HEAD_DIM = 64
BIN = 1024
PAIR = 2 * HEAD_DIM
BLOCK = 256
CHUNK = 256
SLOTS = 4
SENDS = 4
LANDS = 5
QV_ROW = 6
FC_ROW = 7

epsilon = 1e-05
gelu_scale = 0.7978845608028654
gelu_cubic = 0.044715
score_scale = 0.125
masked_score = -1e30

MESH = pl.DeviceIdType.MESH
F32 = jnp.float32
BF16 = jnp.bfloat16
VMEM_LIMIT = 64_000_000


def dot_nn(left, right):
    return lax.dot_general(left, right, (((1,), (0,)), ((), ())), preferred_element_type=F32)


def dot_nt(left, right):
    return lax.dot_general(left, right, (((1,), (1,)), ((), ())), preferred_element_type=F32)


def dot_tn(left, right):
    return lax.dot_general(left, right, (((0,), (0,)), ((), ())), preferred_element_type=F32)


def norm_parts(values):
    center = values - jnp.mean(values, axis=-1, keepdims=True)
    inverse = lax.rsqrt(jnp.mean(center * center, axis=-1, keepdims=True) + epsilon)
    return center * inverse, inverse


def norm_back(upstream, normal, inverse, gain):
    scaled = upstream * gain
    centered = scaled - jnp.mean(scaled, axis=-1, keepdims=True)
    return inverse * (centered - normal * jnp.mean(scaled * normal, axis=-1, keepdims=True))


def gelu_pair(values):
    square = values * values
    tangent = jnp.tanh(gelu_scale * (values + gelu_cubic * square * values))
    half = 0.5 * (1.0 + tangent)
    slope = half + 0.5 * values * (1.0 - tangent * tangent) * (
        gelu_scale + 3.0 * gelu_cubic * gelu_scale * square
    )
    return values * half, slope


def column_to_row(column):
    rows = column.shape[0]
    return jnp.broadcast_to(column, (rows, 128)).T[0:1]


def head_mask(head, scale):
    lane = lax.broadcasted_iota(jnp.int32, (1, PAIR), 1)
    return jnp.where(lane // HEAD_DIM == head, scale, 0.0).astype(BF16)


def attend_pair(qkv_ref, start_ref, attn_ref, lse_ref):
    lane = lax.broadcasted_iota(jnp.int32, (1, PAIR), 1)
    blocks = BIN // BLOCK

    def score(block):
        queries = qkv_ref[0, 0, block * BLOCK : (block + 1) * BLOCK]
        both = jnp.concatenate([queries * head_mask(head, score_scale) for head in range(2)], axis=0)
        return dot_nt(both, qkv_ref[0, 1, 0 : (block + 1) * BLOCK])

    ahead = score(0)
    for block in range(blocks):
        rows = slice(block * BLOCK, (block + 1) * BLOCK)
        seen = (block + 1) * BLOCK
        scores = ahead.reshape(2, BLOCK, seen)
        if block + 1 < blocks:
            ahead = score(block + 1)
        j = lax.broadcasted_iota(jnp.int32, (BLOCK, seen), 1)
        i = lax.broadcasted_iota(jnp.int32, (BLOCK, seen), 0) + block * BLOCK
        visible = (j >= start_ref[rows]) & (j <= i)
        scores = jnp.where(visible[None], scores, masked_score)
        highest = jnp.max(scores, axis=-1, keepdims=True)
        weights = jnp.exp(scores - highest)
        totals = jnp.sum(weights, axis=-1, keepdims=True)
        mixed = dot_nn(weights.astype(BF16).reshape(2 * BLOCK, seen), qkv_ref[0, 2, 0:seen])
        mixed = mixed.reshape(2, BLOCK, PAIR) / totals
        logs = highest + jnp.log(totals)
        for head in range(2):
            lse_ref[0, head : head + 1, rows] = column_to_row(logs[head])
        attn_ref[0, rows] = jnp.where(lane < HEAD_DIM, mixed[0], mixed[1]).astype(BF16)


def project_and_attend(h1, w_ref, pack_ref, start_ref, qkv_ref, attn_ref, lse_ref):
    width = pl.num_programs(0) * PAIR
    place = pl.program_id(0) * PAIR
    weights = jnp.concatenate([w_ref[c].astype(BF16) for c in range(3)], axis=1)
    projected = dot_nn(h1, weights)
    for c in range(3):
        out = projected[:, c * PAIR : (c + 1) * PAIR]
        if c != 1:
            at = place if c == 0 else width + place
            out = out + pack_ref[QV_ROW : QV_ROW + 1, pl.ds(pl.multiple_of(at, PAIR), PAIR)]
        qkv_ref[0, c] = out.astype(BF16)
    attend_pair(qkv_ref, start_ref, attn_ref, lse_ref)


def own_front_kernel(
    mp_ref, x_ref, seg_ref, len_ref, pack_ref, w_ref,
    qkv_ref, attn_ref, lse_ref, h1_ref, start_ref, row_ref,
):
    @pl.when(pl.program_id(0) == 0)
    def _():
        gain = pack_ref[0:1]
        shift = pack_ref[1:2]
        for block in range(BIN // BLOCK):
            rows = slice(block * BLOCK, (block + 1) * BLOCK)
            normal, _ = norm_parts(x_ref[rows].astype(F32))
            h1_ref[rows] = (normal * gain + shift).astype(BF16)
        mine = mp_ref[0]
        count = len_ref.shape[1]
        seg = seg_ref[pl.ds(mine, 1), :].astype(F32)
        seg = jnp.broadcast_to(seg, (128, BIN)).T
        seg = seg[:, :count]
        label = lax.broadcasted_iota(jnp.int32, (BIN, count), 1).astype(F32)
        sizes = len_ref[pl.ds(mine, 1), :].astype(F32)
        start = jnp.sum(jnp.where(label < seg, sizes, 0.0), axis=1, keepdims=True)
        rows_of = jnp.sum(jnp.where(label == seg, 1.0, 0.0), axis=0, keepdims=True)
        first = jnp.sum(jnp.where(label < seg, rows_of, 0.0), axis=1, keepdims=True)
        start = jnp.maximum(start, first)
        start_ref[...] = start.astype(jnp.int32)
        row_ref[...] = column_to_row(start).astype(jnp.int32)

    project_and_attend(h1_ref[...], w_ref, pack_ref, start_ref, qkv_ref, attn_ref, lse_ref)


def other_front_kernel(h1_ref, start_ref, pack_ref, w_ref, qkv_ref, attn_ref, lse_ref):
    project_and_attend(h1_ref[...], w_ref, pack_ref, start_ref, qkv_ref, attn_ref, lse_ref)


def fixed(shape):
    return pl.BlockSpec(shape, lambda *_: (0,) * len(shape), pipeline_mode=pl.Buffered(1))


def front(mine, x, seg, lens, pack, w_own, width):
    model = x.shape[1]
    pairs = width // PAIR
    per_pair = [pl.BlockSpec((3, model, PAIR), lambda p, *_: (0, 0, p))]
    outs = [
        pl.BlockSpec((1, 3, BIN, PAIR), lambda p, *_: (p, 0, 0, 0)),
        pl.BlockSpec((1, BIN, PAIR), lambda p, *_: (p, 0, 0)),
        pl.BlockSpec((1, 8, BIN), lambda p, *_: (p, 0, 0)),
    ]
    out_shapes = [
        jax.ShapeDtypeStruct((pairs, 3, BIN, PAIR), BF16),
        jax.ShapeDtypeStruct((pairs, BIN, PAIR), BF16),
        jax.ShapeDtypeStruct((pairs, 8, BIN), F32),
    ]
    cost = pl.CostEstimate(flops=6_000_000_000, bytes_accessed=10_000_000, transcendentals=0)
    params = pltpu.CompilerParams(vmem_limit_bytes=VMEM_LIMIT)
    own = pl.pallas_call(
        own_front_kernel,
        out_shape=out_shapes
        + [
            jax.ShapeDtypeStruct((BIN, model), BF16),
            jax.ShapeDtypeStruct((BIN, 1), jnp.int32),
            jax.ShapeDtypeStruct((1, BIN), jnp.int32),
        ],
        grid_spec=pltpu.PrefetchScalarGridSpec(
            num_scalar_prefetch=1,
            grid=(pairs,),
            in_specs=[
                pl.BlockSpec((BIN, model), lambda p, m: (m[0], 0)),
                fixed(seg.shape), fixed(lens.shape), fixed(pack.shape),
            ]
            + per_pair,
            out_specs=outs
            + [
                pl.BlockSpec((BIN, model), lambda p, *_: (0, 0)),
                pl.BlockSpec((BIN, 1), lambda p, *_: (0, 0)),
                pl.BlockSpec((1, BIN), lambda p, *_: (0, 0)),
            ],
        ),
        compiler_params=params,
        cost_estimate=cost,
        name="own_front",
    )

    def other(h1, start, pack_other, w_other):
        return pl.pallas_call(
            other_front_kernel,
            out_shape=out_shapes,
            grid=(pairs,),
            in_specs=[fixed((BIN, model)), fixed((BIN, 1)), fixed(pack.shape)] + per_pair,
            out_specs=outs,
            compiler_params=params,
            cost_estimate=cost,
            name="other_front",
        )(h1, start, pack_other, w_other)

    return own(mine, x, seg, lens, pack, w_own), other


def halving_plan(order, rows):
    first, back = [], []
    size = rows
    for n, bit in enumerate(order):
        if n < len(order) - 1 and size % 16 == 0:
            size //= 2
            first.append((bit, size, 0))
            back.append((bit, size, 2))
        else:
            first.append((bit, size, 1))
    return first + back[::-1]


def color_orders(bits, odd):
    plain = list(range(bits))
    orders = [plain, plain, plain]
    if bits > 1:
        orders[1] = [1, 0] + plain[2:]
    if bits > 2:
        orders[2] = [2, 1, 0] + plain[3:] if odd else [2, 0, 1] + plain[3:]
    return orders


def color_plans(bits, odd):
    return [halving_plan(order, CHUNK) for order in color_orders(bits, odd)]


def attend_back_pair(half, place, qkv, dattn, lse_ref, row_ref, dk, dv, vec, pairs):
    dk[...] = jnp.zeros_like(dk)
    dv[...] = jnp.zeros_like(dv)
    pair = half * pairs + place
    dq_sum = jnp.zeros((1, PAIR), F32)
    for block in range(BIN // BLOCK):
        rows = slice(block * BLOCK, (block + 1) * BLOCK)
        seen = (block + 1) * BLOCK
        queries = qkv[pair, 0, rows]
        upstream = dattn[pair, rows]
        key_rows = qkv[pair, 1, 0:seen]
        value_rows = qkv[pair, 2, 0:seen]
        j = lax.broadcasted_iota(jnp.int32, (seen, BLOCK), 0)
        i = lax.broadcasted_iota(jnp.int32, (seen, BLOCK), 1) + block * BLOCK
        visible = (j >= row_ref[0:1, rows]) & (j <= i)
        dq = jnp.zeros((BLOCK, PAIR), F32)
        for head in range(2):
            masked_q = queries * head_mask(head, score_scale)
            masked_up = upstream * head_mask(head, 1.0)
            scores = dot_nt(key_rows, masked_q)
            probs = jnp.exp(scores - lse_ref[pair, head : head + 1, rows])
            probs = jnp.where(visible, probs, 0.0)
            dprobs = dot_nt(value_rows, masked_up)
            inner = jnp.sum(probs * dprobs, axis=0, keepdims=True)
            dscores = (probs * (dprobs - inner)).astype(BF16)
            dv[0:seen] = dv[0:seen] + dot_nn(probs.astype(BF16), masked_up)
            dk[0:seen] = dk[0:seen] + dot_nn(dscores, masked_q)
            dq = dq + dot_tn(dscores, key_rows * head_mask(head, 1.0))
        dq = (dq * score_scale).astype(BF16)
        qkv[pair, 0, rows] = dq
        dq_sum = dq_sum + jnp.sum(dq.astype(F32), axis=0, keepdims=True)
    dv_low = dv[...].astype(BF16)
    qkv[pair, 1] = dk[...].astype(BF16)
    qkv[pair, 2] = dv_low
    dv_sum = jnp.sum(dv_low.astype(F32), axis=0, keepdims=True)
    width = pairs * PAIR
    vec[half, 8:9, pl.ds(pl.multiple_of(place * PAIR, PAIR), PAIR)] = dq_sum
    vec[half, 8:9, pl.ds(pl.multiple_of(width + place * PAIR, PAIR), PAIR)] = dv_sum


def back_kernel(
    bits, groups,
    qkv_own_ref, qkv_other_ref, attn_own_ref, attn_other_ref, h1_ref, w3_own_ref, w3_other_ref,
    x_ref, cot_ref, wo_own_ref, wo_other_ref, wf_ref, wp_ref,
    lse_own_ref, lse_other_ref, row_ref, pack_ref, pack_other_ref,
    op_ref, of_ref, oa_ref, oq_ref, ig_ref, bo_ref, sum_ref, vo_ref,
    acc, mpbuf, rbufs, qkv, dattn, attn, cot, x, tall, flip, total, dwide, first,
    wf, wp, wf_low, wp_low, wf_out, wp_out, wo, w3, act, slope, lse, dk, dv, vec, vrecv,
    ssem, rsem, mps, mpr, wsem, lsem, bsem, wsend, wrecv, hsem, igsem, vsem,
):
    dp = lax.axis_index("dp")
    mp = lax.axis_index("mp")
    chunks = 3 * groups
    own_bits = [(dp // (1 << b)) % 2 for b in range(bits)]
    partner = [dp + (1 - 2 * own_bits[b]) * (1 << b) for b in range(bits)]
    plans = [color_plans(bits, odd) for odd in range(2)]
    stages = len(plans[0][0])
    flights = [2] + [1] * (stages - 2) + [2]
    offsets = [sum(flights[:s]) for s in range(stages + 1)]
    pairs = qkv_own_ref.shape[0]
    model = x_ref.shape[1]
    width = pairs * PAIR
    pieces = model // CHUNK

    my_rows = pl.ds(pl.multiple_of(mp * BIN, BIN), BIN)
    far_rows = pl.ds(pl.multiple_of((1 - mp) * BIN, BIN), BIN)
    loads = []

    def load(src, dst):
        loads.append(pltpu.make_async_copy(src, dst, lsem.at[len(loads)]))

    load(attn_own_ref, attn.at[0:pairs])
    load(attn_other_ref, attn.at[pairs : 2 * pairs])
    load(wo_own_ref, wo.at[0])
    load(wo_other_ref, wo.at[1])
    load(x_ref.at[my_rows], x)
    early = len(loads)
    load(cot_ref.at[my_rows], cot)
    load(qkv_own_ref, qkv.at[0:pairs])
    load(qkv_other_ref, qkv.at[pairs : 2 * pairs])
    load(lse_own_ref, lse.at[0:pairs])
    load(lse_other_ref, lse.at[pairs : 2 * pairs])

    def block_loads(b):
        slot = b % 3
        at = pl.ds(pl.multiple_of(b * CHUNK, CHUNK), CHUNK)
        return [
            pltpu.make_async_copy(wf_ref.at[:, at], wf_low.at[slot], bsem.at[slot, 0]),
            pltpu.make_async_copy(wp_ref.at[at], wp_low.at[slot], bsem.at[slot, 1]),
        ]

    def block_sends(b):
        slot = b % 2
        return [
            pltpu.make_async_remote_copy(
                src, dst.at[slot], wsend.at[n], wrecv.at[slot, n],
                device_id=(dp, 1 - mp), device_id_type=MESH,
            )
            for n, (src, dst) in enumerate(((wf_out, wf), (wp_out, wp)))
        ]

    def send_block(b):
        for item in block_loads(b):
            item.wait()
        wf_out[...] = wf_low[b % 3].astype(F32)
        wp_out[...] = wp_low[b % 3].astype(F32)
        for item in block_sends(b):
            item.start()

    def w3_loads(q, begin):
        slot = 1 - q % 2
        at = pl.ds(pl.multiple_of((q // 2) * PAIR, PAIR), PAIR)
        for half, ref in ((0, w3_own_ref), (1, w3_other_ref)):
            @pl.when(slot == half)
            def _():
                for c in range(3):
                    item = pltpu.make_async_copy(ref.at[c, :, at], w3.at[half, c], hsem.at[half, c])
                    item.start() if begin else item.wait()

    def h1_load():
        return pltpu.make_async_copy(h1_ref, tall, lsem.at[9])

    for item in loads:
        item.start()
    for b in range(2):
        for item in block_loads(b):
            item.start()

    barrier = pltpu.get_barrier_semaphore()
    for b in range(bits):
        pl.semaphore_signal(barrier, inc=1, device_id=(partner[b], mp), device_id_type=MESH)
    pl.semaphore_signal(barrier, inc=1, device_id=(dp, 1 - mp), device_id_type=MESH)
    pl.semaphore_wait(barrier, bits + 1)

    def walk(plan):
        base, found = 0, []
        for bit, size, kind in plan:
            found.append(base)
            if kind == 0:
                base = base + own_bits[bit] * size
            if kind == 2:
                base = base - own_bits[bit] * size
        return found

    starts = [[walk(plan) for plan in plans[odd]] for odd in range(2)]

    def place(c, color, s):
        sides = []
        for odd in range(2):
            bit, size, kind = plans[odd][color][s]
            sides.append((starts[odd][color][s], own_bits[bit], partner[bit]))
        if plans[0][color] == plans[1][color]:
            return sides[0]
        return [jnp.where(c % 2 == 0, even, odd) for even, odd in zip(*sides)]

    def lanes(color):
        share = model // 3
        return slice(color * share, (color + 1) * share)

    def copy(c, color, s):
        _, size, kind = plans[0][color][s]
        slot = c % SLOTS
        base, side, device = place(c, color, s)
        if kind == 0:
            base = base + (1 - side) * size
        src = acc.at[c, pl.ds(pl.multiple_of(base, 8), size), lanes(color)]
        dst = src if kind == 2 else rbufs[color][s].at[slot]
        return pltpu.make_async_remote_copy(
            src, dst, ssem.at[slot, color, s], rsem.at[slot, color, s],
            device_id=(device, mp), device_id_type=MESH,
        )

    def finish(c, color, s):
        _, size, kind = plans[0][color][s]
        copy(c, color, s).wait()
        if kind == 2:
            return
        base, side, _ = place(c, color, s)
        if kind == 0:
            base = base + side * size
        rows = pl.ds(pl.multiple_of(base, 8), size)
        acc[c, rows, lanes(color)] = acc[c, rows, lanes(color)] + rbufs[color][s][c % SLOTS]

    def mp_copy(c):
        slot, land = c % SENDS, c % LANDS
        return pltpu.make_async_remote_copy(
            acc.at[chunks + slot], mpbuf.at[land], mps.at[land], mpr.at[land],
            device_id=(dp, 1 - mp), device_id_type=MESH,
        )

    def mp_finish(c):
        mp_copy(c).wait()
        acc[c] = acc[c] + mpbuf[c % LANDS]

    def chunk_rows(n):
        return pl.ds(pl.multiple_of(n * CHUNK, CHUNK), CHUNK)

    def whole_copy(dst, c):
        return pltpu.make_async_copy(acc.at[c], dst, wsem.at[c % SLOTS, 0])

    def piece_copies(c):
        at = chunk_rows(c // 2)
        return [
            pltpu.make_async_copy(
                acc.at[c, :, n * CHUNK : (n + 1) * CHUNK],
                of_ref.at[n * CHUNK : (n + 1) * CHUNK, at],
                wsem.at[c % SLOTS, n],
            )
            for n in range(pieces)
        ]

    def write(c, begin):
        @pl.when((c < 2 * groups) & (c % 2 == 0))
        def _():
            item = whole_copy(op_ref.at[chunk_rows(c // 2)], c)
            item.start() if begin else item.wait()

        @pl.when((c < 2 * groups) & (c % 2 == 1))
        def _():
            for item in piece_copies(c):
                item.start() if begin else item.wait()

        for part in range(2):
            piece = 2 * (c - 2 * groups) + part
            rows = slice(part * PAIR, (part + 1) * PAIR)

            @pl.when((c >= 2 * groups) & (piece < pairs))
            def _():
                at = pl.ds(pl.multiple_of(piece * PAIR, PAIR), PAIR)
                item = pltpu.make_async_copy(acc.at[c, rows], oa_ref.at[at], wsem.at[c % SLOTS, 6 * part])
                item.start() if begin else item.wait()

            @pl.when((c >= 2 * groups) & (piece >= pairs))
            def _():
                across = pl.ds(pl.multiple_of((piece // pairs - 1) * PAIR, PAIR), PAIR)
                for n in range(6):
                    down = pl.ds(pl.multiple_of((n // 3) * width + (piece % pairs) * PAIR, PAIR), PAIR)
                    item = pltpu.make_async_copy(
                        acc.at[c, rows, n * PAIR : (n + 1) * PAIR],
                        oq_ref.at[n % 3, down, across],
                        wsem.at[c % SLOTS, 6 * part + n],
                    )
                    item.start() if begin else item.wait()

    middle_tick = 2 * groups
    attend_tick = middle_tick + 1
    input_tick = attend_tick + 2 * pairs
    late = chunks - 4
    late_tick = late + 3
    arrivals = [(middle_tick + 2, [0]), (middle_tick + 3, [1, 2]), (middle_tick + 5, [3]), (middle_tick + 7, [4, 5])]
    ticks = chunks + 3 + offsets[stages] + 1

    def at_stage(t, shift):
        since = t - shift
        early = (since >= 2) & (since < late + 2)
        last = (since >= late_tick) & (since < chunks + 3)
        c = jnp.where(since < late_tick, since - 2, since - late_tick + late)
        return jnp.clip(c, 0, chunks - 1), early | last

    def ring_tick(t):
        @pl.when((t >= 2) & (t % 2 == 0) & (t < middle_tick + 2))
        def _():
            mp_finish(t - 2)
            mp_finish(t - 1)

        for at, made in arrivals:
            @pl.when(t == at)
            def _():
                for n in made:
                    mp_finish(2 * groups + n)

        for s in range(stages):
            c, valid = at_stage(t, offsets[s + 1])

            @pl.when(valid)
            def _():
                for color in range(3):
                    finish(c, color, s)

        for s in list(range(stages)) + [-1]:
            c, valid = at_stage(t, offsets[s + 1])

            @pl.when(valid)
            def _():
                if s + 1 == stages:
                    write(c, True)
                else:
                    for color in range(3):
                        copy(c, color, s + 1).start()

    def begin_layer():
        send_block(0)
        for item in loads[:early]:
            item.wait()
        out_bias = pack_ref[2:3]
        gain = pack_ref[3:4]
        shift = pack_ref[4:5]
        proj_bias = pack_ref[5:6]
        vec[...] = jnp.zeros_like(vec)

        def step(block, carry):
            rows = pl.ds(pl.multiple_of(block * BLOCK, BLOCK), BLOCK)
            branch = out_bias
            for half in range(2):
                mixed = [attn[half * pairs + p, rows] for p in range(pairs)]
                branch = branch + dot_nn(jnp.concatenate(mixed, axis=1), wo[half].astype(BF16))
            r1 = x[rows].astype(F32) + branch
            first[rows] = r1
            total[rows] = r1 + proj_bias
            dwide[rows] = jnp.zeros((BLOCK, model), F32)
            normal, _ = norm_parts(r1)
            h2 = (normal * gain + shift).astype(BF16)
            tall[rows] = h2
            flip[:, rows] = h2.T
            return carry

        lax.fori_loop(0, BIN // BLOCK, step, 0)
        loads[early].wait()

    def hidden_half(u):
        b, half = u // 2, 1 - u % 2

        @pl.when(half == 1)
        def _():
            for item in block_sends(b):
                item.wait()

            @pl.when(b + 1 < groups)
            def _():
                send_block(b + 1)

            @pl.when(b + 2 < groups)
            def _():
                for item in block_loads(b + 2):
                    item.start()

            wf_low[3] = wf[b % 2].astype(BF16)
            wp_low[3] = wp[b % 2].astype(BF16)

        span = 2 * BLOCK
        place = jnp.where(half == 0, b % 3, 3)
        fc = wf_low[place]
        proj = wp_low[place]
        at = pl.ds(FC_ROW + b // pieces, 1), pl.ds(pl.multiple_of((b % pieces) * CHUNK, CHUNK), CHUNK)
        bias = jnp.where(half == 0, pack_ref[at], pack_other_ref[at])
        df_sum = jnp.zeros((1, CHUNK), F32)
        for block in range(BIN // span):
            rows = slice(block * span, (block + 1) * span)
            pre = dot_nn(tall[rows], fc) + bias
            hidden, rise = gelu_pair(pre)
            hidden = hidden.astype(BF16)
            act[rows] = hidden
            total[rows] = total[rows] + dot_nn(hidden, proj)
            df = (dot_nt(cot[rows], proj) * rise).astype(BF16)
            slope[rows] = df
            df_sum = df_sum + jnp.sum(df.astype(F32), axis=0, keepdims=True)
            dwide[rows] = dwide[rows] + dot_nt(df, fc)

        vec[half, pl.ds(6 + b // pieces, 1), pl.ds(pl.multiple_of((b % pieces) * CHUNK, CHUNK), CHUNK)] = df_sum
        at = jnp.where(half == 0, 2 * b, chunks + (2 * b) % SENDS)
        acc[at] = dot_tn(act[...], cot[...])
        grad = dot_nn(flip[...], slope[...])
        for n in range(pieces):
            acc[at + 1, :, n * CHUNK : (n + 1) * CHUNK] = grad[n * CHUNK : (n + 1) * CHUNK]

        @pl.when(half == 1)
        def _():
            mp_copy(2 * b).start()
            mp_copy(2 * b + 1).start()

    def put_piece(half, piece, part, value):
        n = piece // 2
        at = jnp.where(half == 0, 2 * groups + n, chunks + (2 * groups + n) % SENDS)
        rows = pl.ds(pl.multiple_of((piece % 2) * PAIR, PAIR), PAIR)
        acc[at, rows, part * width : part * width + value.shape[1]] = value

    def sum_copy():
        return pltpu.make_async_remote_copy(
            total, sum_ref, igsem.at[3], igsem.at[4],
            device_id=(dp, 1 - mp), device_id_type=MESH,
        )

    def sum_loads(part):
        return [
            pltpu.make_async_copy(
                sum_ref.at[(2 * part + n) * CHUNK : (2 * part + n + 1) * CHUNK], wp.at[n], igsem.at[5 + n]
            )
            for n in range(2)
        ]

    def round_far(part):
        for n, item in enumerate(sum_loads(part)):
            item.wait()
            cot[(2 * part + n) * CHUNK : (2 * part + n + 1) * CHUNK] = wp[n].astype(BF16)

    def out_copy(n):
        src, rows = ((tall, my_rows), (cot, far_rows))[n]
        return pltpu.make_async_copy(src, bo_ref.at[rows], igsem.at[7 + n])

    def middle_back():
        sum_copy().start()
        gain = pack_ref[3:4]
        w3_loads(jnp.int32(0), True)

        def step(block, sums):
            rows = pl.ds(pl.multiple_of(block * BLOCK, BLOCK), BLOCK)
            normal, inverse = norm_parts(first[rows])
            up = dwide[rows]
            upstream = cot[rows].astype(F32)
            dr1 = upstream + norm_back(up, normal, inverse, gain)
            first[rows] = dr1
            dwide[rows] = jnp.zeros((BLOCK, model), F32)
            da = dr1.astype(BF16)
            tall[rows] = da
            for half in range(2):
                back = dot_nt(da, wo[half].astype(BF16)).astype(BF16)
                for p in range(pairs):
                    dattn[half * pairs + p, rows] = back[:, p * PAIR : (p + 1) * PAIR]
            return tuple(
                total_row + jnp.sum(item, axis=0, keepdims=True)
                for total_row, item in zip(sums, (da.astype(F32), up * normal, up, upstream))
            )

        sums = lax.fori_loop(0, BIN // BLOCK, step, (jnp.zeros((1, model), F32),) * 4)
        for half in range(2):
            for n in range(4):
                vec[half, 2 + n : 3 + n] = sums[n]
            mixed = jnp.concatenate([attn[half * pairs + p] for p in range(pairs)], axis=1)
            grad = dot_tn(mixed, tall[...])
            for piece in range(pairs):
                put_piece(half, piece, 0, grad[piece * PAIR : (piece + 1) * PAIR])
        mp_copy(2 * groups).start()
        h1_load().start()
        for item in loads[early + 1 :]:
            item.wait()

    def attend_half(q):
        p, half = q // 2, 1 - q % 2

        @pl.when(q + 1 < 2 * pairs)
        def _():
            w3_loads(q + 1, True)

        @pl.when(q == 0)
        def _():
            h1_load().wait()
            flip[...] = tall[...].T

        attend_back_pair(half, p, qkv, dattn, lse, row_ref, dk, dv, vec, pairs)
        w3_loads(q, False)
        pair = half * pairs + p
        low = jnp.concatenate([qkv[pair, c] for c in range(3)], axis=1)
        grad = dot_nn(flip[...], low)
        for n in range(2 * pairs):
            put_piece(half, pairs * (p + 1) + n % pairs, n // pairs, grad[n * PAIR : (n + 1) * PAIR])
        weights = jnp.concatenate([w3[half, c].astype(BF16) for c in range(3)], axis=1)
        dwide[...] = dwide[...] + dot_nt(low, weights)
        for at, made in ((0, [1, 2]), (2, [3]), (4, [4, 5])):
            @pl.when(q == at)
            def _():
                for n in made:
                    mp_copy(2 * groups + n).start()

    def input_grad():
        gain = pack_ref[0:1]

        def step(block, sums):
            rows = pl.ds(pl.multiple_of(block * BLOCK, BLOCK), BLOCK)
            normal, inverse = norm_parts(x[rows].astype(F32))
            up = dwide[rows]
            first[rows] = first[rows] + norm_back(up, normal, inverse, gain)
            return (
                sums[0] + jnp.sum(up * normal, axis=0, keepdims=True),
                sums[1] + jnp.sum(up, axis=0, keepdims=True),
            )

        gain_sum, shift_sum = lax.fori_loop(0, BIN // BLOCK, step, (jnp.zeros((1, model), F32),) * 2)
        for half in range(2):
            vec[half, 0:1] = gain_sum
            vec[half, 1:2] = shift_sum

    def ig_copies():
        local = pltpu.make_async_copy(first, ig_ref.at[my_rows], igsem.at[0])
        remote = pltpu.make_async_remote_copy(
            first, ig_ref.at[my_rows], igsem.at[1], igsem.at[2],
            device_id=(dp, 1 - mp), device_id_type=MESH,
        )
        return local, remote

    def vec_copy(n):
        if n == 0:
            src, device = vec.at[1], (dp, 1 - mp)
        else:
            src, device = vec.at[0], (partner[n - 1], mp)
        return pltpu.make_async_remote_copy(
            src, vrecv.at[n], vsem.at[0, n], vsem.at[1, n], device_id=device, device_id_type=MESH
        )

    begin_layer()

    def tick(t, carry):
        ring_tick(t)

        @pl.when(t < middle_tick)
        def _():
            hidden_half(t)

        @pl.when(t == middle_tick)
        def _():
            middle_back()

        @pl.when((t >= attend_tick) & (t < input_tick))
        def _():
            attend_half(t - attend_tick)

        @pl.when(t == input_tick)
        def _():
            input_grad()
            for item in ig_copies():
                item.start()
            vec_copy(0).start()
            tall[...] = total[...].astype(BF16)
            out_copy(0).start()

        @pl.when(t == input_tick + 1)
        def _():
            sum_copy().wait()
            for item in sum_loads(0):
                item.start()

        @pl.when(t == input_tick + 2)
        def _():
            round_far(0)
            for item in sum_loads(1):
                item.start()

        @pl.when(t == input_tick + 3)
        def _():
            round_far(1)
            out_copy(1).start()

        for n in range(bits + 1):
            @pl.when(t == input_tick + 1 + n)
            def _():
                vec_copy(n).wait()
                vec[0] = vec[0] + vrecv[n]
                if n < bits:
                    vec_copy(n + 1).start()

        c, valid = at_stage(t, offsets[stages] + 1)

        @pl.when(valid)
        def _():
            write(c, False)

        return carry

    lax.fori_loop(0, ticks, tick, 0)
    for item in list(ig_copies()) + [out_copy(0), out_copy(1)]:
        item.wait()
    vo_ref[...] = vec[0]


def back(bits, arrays, row, packs, sizes):
    pairs, hidden, model = sizes
    width = pairs * PAIR
    groups = hidden // CHUNK
    chunks = 3 * groups
    plans = color_plans(bits, 0)
    stages = len(plans[0])
    recv = [
        [pltpu.VMEM((SLOTS, size, model // 3), F32) for _, size, kind in plan if kind < 2]
        for plan in plans
    ]
    here = pl.BlockSpec(memory_space=pl.ANY)
    vmem = pl.BlockSpec(memory_space=pltpu.VMEM)
    dma = pltpu.SemaphoreType.DMA
    return pl.pallas_call(
        functools.partial(back_kernel, bits, groups),
        out_shape=[
            jax.ShapeDtypeStruct((hidden, model), F32),
            jax.ShapeDtypeStruct((model, hidden), F32),
            jax.ShapeDtypeStruct((width, model), F32),
            jax.ShapeDtypeStruct((3, model, width), F32),
            jax.ShapeDtypeStruct((2 * BIN, model), F32),
            jax.ShapeDtypeStruct((2 * BIN, model), BF16),
            jax.ShapeDtypeStruct((BIN, model), F32),
            jax.ShapeDtypeStruct((16, model), F32),
        ],
        in_specs=[here] * len(arrays) + [vmem] * 3,
        out_specs=[here] * 7 + [vmem],
        scratch_shapes=[
            pltpu.VMEM((chunks + SENDS, CHUNK, model), F32),
            pltpu.VMEM((LANDS, CHUNK, model), F32),
            recv,
            pltpu.VMEM((2 * pairs, 3, BIN, PAIR), BF16),
            pltpu.VMEM((2 * pairs, BIN, PAIR), BF16),
            pltpu.VMEM((2 * pairs, BIN, PAIR), BF16),
            pltpu.VMEM((BIN, model), BF16),
            pltpu.VMEM((BIN, model), BF16),
            pltpu.VMEM((BIN, model), BF16),
            pltpu.VMEM((model, BIN), BF16),
            pltpu.VMEM((BIN, model), F32),
            pltpu.VMEM((BIN, model), F32),
            pltpu.VMEM((BIN, model), F32),
            pltpu.VMEM((2, model, CHUNK), F32),
            pltpu.VMEM((2, CHUNK, model), F32),
            pltpu.VMEM((4, model, CHUNK), BF16),
            pltpu.VMEM((4, CHUNK, model), BF16),
            pltpu.VMEM((model, CHUNK), F32),
            pltpu.VMEM((CHUNK, model), F32),
            pltpu.VMEM((2, width, model), F32),
            pltpu.VMEM((2, 3, model, PAIR), F32),
            pltpu.VMEM((BIN, CHUNK), BF16),
            pltpu.VMEM((BIN, CHUNK), BF16),
            pltpu.VMEM((2 * pairs, 8, BIN), F32),
            pltpu.VMEM((BIN, PAIR), F32),
            pltpu.VMEM((BIN, PAIR), F32),
            pltpu.VMEM((2, 16, model), F32),
            pltpu.VMEM((bits + 1, 16, model), F32),
            dma((SLOTS, 3, stages)),
            dma((SLOTS, 3, stages)),
            dma((LANDS,)),
            dma((LANDS,)),
            dma((SLOTS, 12)),
            dma((10,)),
            dma((3, 2)),
            dma((2,)),
            dma((2, 2)),
            dma((2, 3)),
            dma((9,)),
            dma((2, bits + 1)),
        ],
        compiler_params=pltpu.CompilerParams(
            collective_id=0, has_side_effects=True, vmem_limit_bytes=67_043_328
        ),
        name="back",
    )(*arrays, row, *packs)


def on_device(
    tokens, segments, lengths, ln1_gain, ln1_bias, w_qkv, b_qv, w_out, out_bias,
    ln2_gain, ln2_bias, w_fc, b_fc, w_proj, proj_bias, cotangent,
):
    model = tokens.shape[1]
    width = w_qkv.shape[2]
    hidden = w_fc.shape[1]
    pairs = width // PAIR
    groups = lax.axis_size("dp")
    bits = groups.bit_length() - 1
    if lax.axis_size("mp") != 2 or groups != 1 << bits or tokens.shape[0] != 2 * BIN:
        raise ValueError("unsupported mesh")
    side = lax.axis_index("mp")
    mine = side.astype(jnp.int32).reshape(1)
    swap = [(0, 1), (1, 0)]

    def cross(value):
        return lax.ppermute(value, "mp", swap)

    w3 = jnp.transpose(w_qkv, (1, 0, 2)).astype(F32)
    vectors = (ln1_gain, ln1_bias, out_bias, ln2_gain, ln2_bias, proj_bias, b_qv.reshape(-1), b_fc)
    pack = jnp.concatenate([item.astype(F32) for item in vectors]).reshape(-1, model)
    pack_other = cross(pack)
    w3_other = cross(w3)
    wo_own = w_out.astype(F32)
    wo_other = cross(wo_own)

    own, other_front = front(
        mine, tokens, segments.reshape(2, BIN), lengths, pack, w3, width,
    )
    qkv_own, attn_own, lse_own, h1, start, row = own
    pack_other, w3_other, wo_other, h1 = lax.optimization_barrier((pack_other, w3_other, wo_other, h1))
    qkv_other, attn_other, lse_other = other_front(h1, start, pack_other, w3_other)
    arrays = (
        qkv_own, qkv_other, attn_own, attn_other, h1, w3, w3_other, tokens, cotangent,
        wo_own, wo_other, w_fc, w_proj, lse_own, lse_other,
    )
    grad_proj, grad_fc, grad_out, grad_qkv, input_grad, block_out, _, rows = back(
        bits, arrays, row, (pack, pack_other), (pairs, hidden, model)
    )
    grad_qkv = jnp.transpose(grad_qkv, (1, 0, 2))
    return (
        block_out,
        input_grad,
        rows[0],
        rows[1],
        grad_qkv,
        rows[8].reshape(2, width),
        grad_out,
        rows[2],
        rows[3],
        rows[4],
        grad_fc,
        rows[6:8].reshape(-1),
        grad_proj,
        rows[5],
    )


def solution(mesh):
    rows = P("dp", None)
    placed = (
        rows, P("dp"), rows, P(), P(), P(None, None, "mp"), P(None, "mp"), P("mp", None), P(),
        P(), P(), P(None, "mp"), P("mp"), P("mp", None), P(), rows,
    )
    results = (
        rows, rows, P(), P(), P(None, None, "mp"), P(None, "mp"), P("mp", None), P(), P(), P(),
        P(None, "mp"), P("mp"), P("mp", None), P(),
    )
    return jax.shard_map(
        on_device, mesh=mesh, in_specs=placed, out_specs=results, check_vma=False
    )
```
